32 devices in a mesh: dp: 8 (over y, x, core), tensor: 4 (over z).
Axes of the slice: x: 2, y: 2, z: 4, core: 2. Of those that a mesh axis runs over, the one named last changes fastest.
Arguments:
- tokens: bfloat16 [16384, 768], P(('dp', 'tensor')), may hold values from -6 to 6
- cotangent: bfloat16 [16384, 768], P(('dp', 'tensor')), may hold values from -6 to 6
- segment_ids: int32 [8, 2048], P('dp'), may hold values from 0 to 15, never falling along the last dimension, each value on 1 to 1024 neighbouring positions
- drop_flags: int32 [8], P('dp'), may hold values 0 or 1
- query_weight: bfloat16 [768, 768], P(None, 'tensor'), may hold values from -0.21875 to 0.21875
- query_bias: bfloat16 [768], P('tensor'), may hold values from -3 to 3
- key_weight: bfloat16 [768, 768], P(None, 'tensor'), may hold values from -0.21875 to 0.21875
- value_weight: bfloat16 [768, 768], P(None, 'tensor'), may hold values from -0.21875 to 0.21875
- value_bias: bfloat16 [768], P('tensor'), may hold values from -3 to 3
- out_weight: bfloat16 [768, 768], P('tensor'), may hold values from -3.5 to 3.5
- out_bias: bfloat16 [768], replicated, may hold values from -3 to 3
- attn_gain: bfloat16 [768], replicated, may hold values from 0.5 to 1.5
- attn_shift: bfloat16 [768], replicated, may hold values from -2 to 2
- up_weight: bfloat16 [768, 3072], P(None, 'tensor'), may hold values from -0.21875 to 0.21875
- up_bias: bfloat16 [3072], P('tensor'), may hold values from -3 to 3
- down_weight: bfloat16 [3072, 768], P('tensor'), may hold values from -0.109375 to 0.109375
- down_bias: bfloat16 [768], replicated, may hold values from -3 to 3
- ffn_gain: bfloat16 [768], replicated, may hold values from 0.5 to 1.5
- ffn_shift: bfloat16 [768], replicated, may hold values from -2 to 2
Outputs:
- layer_out: bfloat16 [16384, 768], P(('dp', 'tensor'))
- tokens_grad: bfloat16 [16384, 768], P(('dp', 'tensor'))
- query_weight_grad: float32 [768, 768], P(None, 'tensor')
- query_bias_grad: float32 [768], P('tensor')
- key_weight_grad: float32 [768, 768], P(None, 'tensor')
- value_weight_grad: float32 [768, 768], P(None, 'tensor')
- value_bias_grad: float32 [768], P('tensor')
- out_weight_grad: float32 [768, 768], P('tensor')
- out_bias_grad: float32 [768], replicated
- attn_gain_grad: float32 [768], replicated
- attn_shift_grad: float32 [768], replicated
- up_weight_grad: float32 [768, 3072], P(None, 'tensor')
- up_bias_grad: float32 [3072], P('tensor')
- down_weight_grad: float32 [3072, 768], P('tensor')
- down_bias_grad: float32 [768], replicated
- ffn_gain_grad: float32 [768], replicated
- ffn_shift_grad: float32 [768], replicated
The draws below stay inside these ranges and needn't reach their ends.
Inputs may be any that keep to these rules, and one draw needn't show every extreme that they name: `segment_ids`: along each sequence the ids never fall; a document holds at most 1024 tokens, and one holds exactly 1024.
All inputs are finite; a program needn't handle non-finite values. No bound on the sum of `drop_flags` on one device may be relied on, other than what follows from the above.
Results may differ from the reference program's by a relative error of at most 0.018.
Values may be sent and summed in bfloat16 or wider, within the bound.
No kernel may reach another device: no remote copies, remote signals or barrier semaphores. Data moves between devices by JAX's collectives and lax.ppermute only.
A program may use at most 128 MiB of HBM per device.

```python
import math
import jax
import jax.numpy as jnp
import numpy as np
from jax import lax

D = 768
HEADS = 12
HEAD_DIM = 64
FF = 3072
LEN = 2048
DOCS = 16
DOC_MOST = 1024
SEQS = 8
TOKENS = 16384


def touch_ends(result, own_key, smallest, top_value):
    extent = result.shape
    spot = [jax.random.randint(jax.random.fold_in(own_key, axis), (), 0, extent[axis]) for axis in range(len(extent))]
    result = result.at[tuple(spot)].set(smallest)
    longest = extent.index(max(extent))
    spot[longest] = (spot[longest] + 1) % extent[longest]
    return result.at[tuple(spot)].set(top_value)


def steps_of(own_key, dims, shards, smallest, top_value):
    factor_of, own = 1.0, jax.random.fold_in(own_key, 6)
    for axis_at, shards_of in shards:
        steps = jnp.exp(jax.random.uniform(jax.random.fold_in(own, axis_at), (shards_of,), jnp.float32, smallest / len(shards), top_value / len(shards)))
        factor_of = factor_of * jnp.repeat(steps, dims[axis_at] // shards_of).reshape([-1 if axis == axis_at else 1 for axis in range(len(dims))])
    return factor_of


def length_profile(count, total, limit, lean):
    weights = [(1 << 20) // math.isqrt(standing ** lean) + 1 for standing in range(2, count + 1)]
    spare, counts = total - limit - (count - 1), [1] * (count - 1)
    while spare > 0:
        candidates = [i for i in range(count - 1) if counts[i] < limit]
        whole, left = sum([weights[i] for i in candidates]), spare
        for i in candidates:
            more = min(limit - counts[i], max(1, left * weights[i] // whole), spare)
            counts[i] = counts[i] + more
            spare = spare - more
    return np.array([limit] + counts)


def ragged(rng, count, total, most, skew):
    if count == 2:
        one = jax.random.randint(rng, (), max(1, total - most), min(most, total - 1) + 1)
        return jnp.stack([one, total - one])
    sizes = jnp.asarray(length_profile(count, total, most, skew), jnp.int32)
    couples = (count - 1) // 2
    source_of, sink = sizes[1:1 + 2 * couples:2], sizes[2:2 + 2 * couples:2]
    margin = jnp.minimum(source_of - 1, most - sink)
    shifted = jax.random.randint(jax.random.fold_in(rng, 1), (couples,), 0, 1 << 20) % (margin + 1)
    sizes = sizes.at[1:1 + 2 * couples:2].set(source_of - shifted).at[2:2 + 2 * couples:2].set(sink + shifted)
    return sizes[jax.random.permutation(jax.random.fold_in(rng, 2), count)]


def normal_values(key, shape, deviation, limit, split=(), held_as=jnp.bfloat16):
    values = deviation * jax.random.normal(key, shape, jnp.float32)
    if split:
        values = values * steps_of(key, shape, split, -0.22, 0.18)
    return jnp.clip(values, -limit, limit).astype(held_as)


def setup_inputs(seed: int = 0) -> dict:
    key_list = jax.random.split(jax.random.key(seed), 20)
    return {
        "tokens": normal_values(key_list[0], (TOKENS, D), 1.0, 6.0, ((0, 32),)),
        "cotangent": normal_values(key_list[1], (TOKENS, D), 1.0, 6.0, ((0, 32),)),
        "segment_ids": jax.vmap(lambda own: jnp.searchsorted(jnp.cumsum(ragged(own, DOCS, LEN, DOC_MOST, 2)), jnp.arange(LEN), side="right"))(jax.random.split(key_list[2], SEQS)).reshape((SEQS, LEN)).astype(jnp.int32),
        "drop_flags": touch_ends((jax.random.randint(key_list[3], (SEQS,), 0, 4) < 1).astype(jnp.int32), jax.random.fold_in(key_list[3], 1), 0, 1),
        "query_weight": normal_values(key_list[4], (D, D), D ** -0.5, 0.21875, ((1, 4),)),
        "query_bias": normal_values(key_list[5], (D,), 0.5, 3.0, ((0, 4),)),
        "key_weight": normal_values(key_list[6], (D, D), D ** -0.5, 0.21875, ((1, 4),)),
        "value_weight": normal_values(key_list[7], (D, D), D ** -0.5, 0.21875, ((1, 4),)),
        "value_bias": normal_values(key_list[8], (D,), 0.5, 3.0, ((0, 4),)),
        "out_weight": normal_values(key_list[9], (D, D), (max(D // 256, 1)) ** -0.5, 3.5, ((0, 4),)),
        "out_bias": normal_values(key_list[10], (D,), 0.5, 3.0),
        "attn_gain": jnp.clip(1.0 + 0.1 * jax.random.normal(key_list[11], (D,), jnp.float32), 0.5, 1.5).astype(jnp.bfloat16),
        "attn_shift": normal_values(key_list[12], (D,), 0.3, 2.0),
        "up_weight": normal_values(key_list[13], (D, FF), D ** -0.5, 0.21875, ((1, 4),)),
        "up_bias": normal_values(key_list[14], (FF,), 0.5, 3.0, ((0, 4),)),
        "down_weight": normal_values(key_list[15], (FF, D), FF ** -0.5, 0.109375, ((0, 4),)),
        "down_bias": normal_values(key_list[16], (D,), 0.5, 3.0),
        "ffn_gain": jnp.clip(1.0 + 0.1 * jax.random.normal(key_list[17], (D,), jnp.float32), 0.5, 1.5).astype(jnp.bfloat16),
        "ffn_shift": normal_values(key_list[18], (D,), 0.3, 2.0),
    }


EPS = 1e-05
NEG = -1e+30
HIGH = lax.Precision.HIGHEST

@jax.custom_vjp
def low(v):
    return lax.optimization_barrier(v.astype(jnp.bfloat16)).astype(jnp.float32)

@jax.custom_vjp
def low_back(v):
    return v

def low_keep(v):
    return (low(v), None)

def low_pass(kept, grad):
    return (grad,)

def back_keep(v):
    return (v, None)

def back_low(kept, grad):
    return (low(grad),)
low.defvjp(low_keep, low_pass)
low_back.defvjp(back_keep, back_low)

def matmul(left, right):
    return jnp.dot(left, right, precision=HIGH)

def rounded_both(value):
    return low_back(low(value))

def layer_norm(value, gain, shift):
    center = value - lax.optimization_barrier(jnp.mean(value, -1, keepdims=True))
    spread = lax.optimization_barrier(jnp.mean(center * center, -1, keepdims=True))
    return center * lax.rsqrt(spread + EPS) * gain + shift

def forward(params, tokens, segment, keep_flag):
    query_weight, query_bias, key_weight, value_weight, value_bias, out_weight, out_bias, attn_gain, attn_shift, up_weight, up_bias, down_weight, down_bias, ffn_gain, ffn_shift = params
    query = rounded_both((matmul(tokens, query_weight) + query_bias) * 0.125).reshape(LEN, HEADS, HEAD_DIM)
    keys = rounded_both(matmul(tokens, key_weight)).reshape(LEN, HEADS, HEAD_DIM)
    values = rounded_both(matmul(tokens, value_weight) + value_bias).reshape(LEN, HEADS, HEAD_DIM)
    block_rows = min(512, LEN)

    def attend(index):
        row_start = index * block_rows
        query_block = lax.dynamic_slice_in_dim(query, row_start, block_rows, 0)
        segment_block = lax.dynamic_slice_in_dim(segment, row_start, block_rows, 0)
        scores = low_back(jnp.einsum('qhd,khd->hqk', query_block, keys, precision=HIGH))
        scores = jnp.where((segment_block[:, None] == segment[None, :])[None], scores, NEG)
        row_max = lax.optimization_barrier(jnp.max(scores, -1, keepdims=True))
        exponent = jnp.exp(scores - row_max)
        probs = low(exponent / lax.optimization_barrier(jnp.sum(exponent, -1, keepdims=True)))
        return jnp.einsum('hqk,khd->qhd', probs, values, precision=HIGH)
    context = lax.map(jax.checkpoint(attend), jnp.arange(LEN // block_rows, dtype=jnp.int32))
    context = rounded_both(context.reshape(LEN, D))
    resid = tokens + low_back(matmul(context, out_weight)) + out_bias
    normed = layer_norm(resid, attn_gain, attn_shift)
    hidden_pre = low_back(matmul(low(normed), up_weight) + up_bias)
    hidden = low(jax.nn.gelu(hidden_pre, approximate=False))
    summed = normed + low_back(matmul(hidden, down_weight)) + down_bias
    final = layer_norm(summed, ffn_gain, ffn_shift)
    return keep_flag * final + (1.0 - keep_flag) * tokens

def reference(tokens, cotangent, segment_ids, drop_flags, query_weight, query_bias, key_weight, value_weight, value_bias, out_weight, out_bias, attn_gain, attn_shift, up_weight, up_bias, down_weight, down_bias, ffn_gain, ffn_shift):
    params = tuple((weight.astype(jnp.float32) for weight in (query_weight, query_bias, key_weight, value_weight, value_bias, out_weight, out_bias, attn_gain, attn_shift, up_weight, up_bias, down_weight, down_bias, ffn_gain, ffn_shift)))
    token_seqs = tokens.astype(jnp.float32).reshape(SEQS, LEN, D)
    cot_seqs = cotangent.astype(jnp.float32).reshape(SEQS, LEN, D)
    keep_flags = (1 - drop_flags).astype(jnp.float32)

    def per_sequence(grad_total, sequence_item):
        seq_tokens, seq_cot, seq_segment, seq_keep = sequence_item

        def closed(weights, inputs):
            return forward(weights, inputs, seq_segment, seq_keep)
        layer_value, backward = jax.vjp(closed, params, seq_tokens)
        weight_grads, input_grad = backward(seq_cot)
        grad_total = jax.tree.map(jnp.add, grad_total, weight_grads)
        return (grad_total, (layer_value, input_grad))
    start_grads = jax.tree.map(jnp.zeros_like, params)
    gradients, (layer_values, input_grads) = lax.scan(per_sequence, start_grads, (token_seqs, cot_seqs, segment_ids, keep_flags))
    return (layer_values.reshape(TOKENS, D).astype(jnp.bfloat16), input_grads.reshape(TOKENS, D).astype(jnp.bfloat16), gradients[0], gradients[1], gradients[2], gradients[3], gradients[4], gradients[5], gradients[6], gradients[7], gradients[8], gradients[9], gradients[10], gradients[11], gradients[12], gradients[13], gradients[14])
```

```python
import jax
import jax.numpy as jnp
from jax import lax
from jax.sharding import PartitionSpec as P

HEAD_DIM = 64
EPS = 1e-05
NEG = -1e30
F32 = jnp.float32
BF16 = jnp.bfloat16
AXES = ("dp", "tensor")


def matmul(left, right):
    return jnp.dot(left, right, preferred_element_type=F32)


def matmul_left(left, right):
    return lax.dot_general(left, right, (((0,), (0,)), ((), ())), preferred_element_type=F32)


def matmul_right(left, right):
    return lax.dot_general(left, right, (((1,), (1,)), ((), ())), preferred_element_type=F32)


def layer_norm(value, gain, shift):
    center = value - jnp.mean(value, -1, keepdims=True)
    spread = jnp.mean(center * center, -1, keepdims=True)
    return center * lax.rsqrt(spread + EPS) * gain + shift


def exact_gelu(value):
    return jax.nn.gelu(value, approximate=False)


def attend_forward(query, keys, values, segment):
    rows = 512
    length, width = query.shape
    heads = width // HEAD_DIM
    keys = keys.reshape(length, heads, HEAD_DIM)
    values = values.reshape(length, heads, HEAD_DIM)
    outs, totals = [], []
    for start in range(0, length, rows):
        block = query[start : start + rows].reshape(rows, heads, HEAD_DIM)
        scores = jnp.einsum("qhd,khd->hqk", block, keys, preferred_element_type=F32)
        same = (segment[start : start + rows, None] == segment[None, :])[None]
        scores = jnp.where(same, scores, NEG)
        top = jnp.max(scores, -1, keepdims=True)
        exponent = jnp.exp(scores - top)
        total = jnp.sum(exponent, -1, keepdims=True)
        probs = (exponent / total).astype(BF16)
        outs.append(
            jnp.einsum("hqk,khd->qhd", probs, values, preferred_element_type=F32).reshape(
                rows, width
            )
        )
        totals.append((top + jnp.log(total))[..., 0])
    return jnp.concatenate(outs, 0), jnp.concatenate(totals, 1)


def attend_backward(query, keys, values, segment, context, totals, dcontext):
    rows = 512
    length, width = query.shape
    heads = width // HEAD_DIM
    keys3 = keys.reshape(length, heads, HEAD_DIM)
    values3 = values.reshape(length, heads, HEAD_DIM)
    dquery, dkey, dvalue = [], 0.0, 0.0
    for start in range(0, length, rows):
        block = query[start : start + rows].reshape(rows, heads, HEAD_DIM)
        dblock = dcontext[start : start + rows].reshape(rows, heads, HEAD_DIM)
        scores = jnp.einsum("qhd,khd->hqk", block, keys3, preferred_element_type=F32)
        same = (segment[start : start + rows, None] == segment[None, :])[None]
        probs = jnp.exp(jnp.where(same, scores, NEG) - totals[:, start : start + rows, None])
        dprobs = jnp.einsum("qhd,khd->hqk", dblock, values3, preferred_element_type=F32)
        weighted = jnp.sum(probs * dprobs, -1, keepdims=True)
        dscores = (probs * (dprobs - weighted)).astype(BF16)
        dquery.append(
            jnp.einsum("hqk,khd->qhd", dscores, keys3, preferred_element_type=F32)
            .astype(BF16)
            .reshape(rows, width)
        )
        dkey = dkey + jnp.einsum("hqk,qhd->khd", dscores, block, preferred_element_type=F32)
        dvalue = dvalue + jnp.einsum(
            "hqk,qhd->khd", probs.astype(BF16), dblock, preferred_element_type=F32
        )
    return (
        jnp.concatenate(dquery, 0),
        dkey.astype(BF16).reshape(length, width),
        dvalue.astype(BF16).reshape(length, width),
    )


def solution(mesh):
    ndp, nt = mesh.shape["dp"], mesh.shape["tensor"]

    def moved_at(i, t):
        return (i & 1) != (t >> 1)

    def exchange(value, target, only=None):
        pairs = []
        for i in range(ndp):
            for t in range(nt):
                if only is None or only(i, t):
                    j, u = target(i, t)
                    pairs.append((i * nt + t, j * nt + u))
        return lax.ppermute(value, AXES, pairs)

    def swap(value):
        return exchange(value, lambda i, t: (i ^ 1, t ^ 2), moved_at)

    def over_core(value):
        return exchange(value, lambda i, t: (i ^ 1, t))

    def over_z(value):
        return exchange(value, lambda i, t: (i, t ^ 1))

    def over_x(value):
        return exchange(value, lambda i, t: (i ^ 2, t))

    def over_y(value):
        return exchange(value, lambda i, t: (i ^ 4, t))

    def shards(
        tokens,
        cotangent,
        segment_ids,
        drop_flags,
        query_weight,
        query_bias,
        key_weight,
        value_weight,
        value_bias,
        out_weight,
        out_bias,
        attn_gain,
        attn_shift,
        up_weight,
        up_bias,
        down_weight,
        down_bias,
        ffn_gain,
        ffn_shift,
    ):
        i, t = lax.axis_index("dp"), lax.axis_index("tensor")
        core, zbit, xbit, ybit = i & 1, t & 1, (i >> 1) & 1, (i >> 2) & 1
        moved = core != (t >> 1)
        length = segment_ids.shape[1]
        rows, model = tokens.shape
        width = query_weight.shape[1]
        part = up_weight.shape[1] // 4

        def own(value):
            return jnp.where(moved, swap(value), value)

        def turned(value, axis, bit):
            return jnp.where(bit == 1, jnp.flip(value, axis), value)

        def reduce_plane(first, second):
            first_low = first[0].astype(F32) + over_y(first[1]).astype(F32)
            second_low = second[:, 0].astype(F32) + over_x(second[:, 1]).astype(F32)
            first_one = first_low[0] + over_x(first_low[1].astype(BF16)).astype(F32)
            second_one = second_low[0] + over_y(second_low[1].astype(BF16)).astype(F32)
            return first_one, second_one

        def spread_plane(first, second):
            first, second = first.astype(BF16), second.astype(BF16)
            handed = exchange(
                second, lambda i, t: (i ^ 1, t), lambda i, t: not moved_at(i, t)
            )
            piece = jnp.where(moved, handed, first)
            one = exchange(piece, lambda i, t: (i ^ 4, t) if moved_at(i, t) else (i ^ 2, t))
            half = jnp.stack([piece, one])
            two = exchange(half, lambda i, t: (i ^ 2, t) if moved_at(i, t) else (i ^ 4, t))
            whole = jnp.stack([half, two])
            other = over_core(whole)
            first_all = jnp.where(moved, other, whole)
            second_all = jnp.swapaxes(jnp.where(moved, whole, other), 0, 1)
            return first_all, second_all

        def absolute(value):
            return turned(turned(value, 0, ybit), 1, xbit)

        def to_home(value):
            value = value + exchange(
                value.astype(BF16), lambda i, t: (i, t ^ 2), moved_at
            ).astype(F32)
            bit = 8
            while bit < ndp:
                value = value + exchange(
                    value.astype(BF16), lambda i, t, bit=bit: (i ^ bit, t)
                ).astype(F32)
                bit *= 2
            return value

        notes = jnp.concatenate(
            [segment_ids, jnp.broadcast_to(drop_flags[:, None], (1, 128))], axis=1
        )
        notes = jnp.where(moved, over_core(notes), notes)
        keep_flag = (1 - notes[0, length]).astype(F32)
        segment = notes[0, :length].reshape(2, 2, length // 4)
        segment = turned(turned(segment, 0, core), 1, zbit)
        segment = jnp.swapaxes(segment, 0, 1).reshape(length)

        token_own = own(tokens)
        token_core = over_core(token_own)
        token_z = over_z(token_own)
        token_zc = over_core(token_z)
        full_tokens = jnp.concatenate([token_own, token_core, token_z, token_zc], 0)

        packed = jnp.concatenate([query_weight, key_weight, value_weight], 1)
        packed = own(packed)
        biases = own(jnp.concatenate([query_bias, value_bias])[None])[0].astype(F32)
        query_w, key_w, value_w = (
            packed[:, :width],
            packed[:, width : 2 * width],
            packed[:, 2 * width :],
        )
        query_b, value_b = biases[:width], biases[width:]

        place = (ybit * 2 + xbit) * part
        quarter = jnp.concatenate(
            [
                lax.dynamic_slice_in_dim(up_weight, place, part, 1).T,
                lax.dynamic_slice_in_dim(down_weight, place, part, 0),
            ],
            0,
        )
        quarter = own(quarter)
        quarters = jnp.stack([quarter, over_z(quarter)])
        up_q, down_q = quarters[:, :part], quarters[:, part:]
        up_x, down_y = over_x(up_q), over_y(down_q)
        up_yy = over_y(jnp.stack([up_q, up_x]))
        down_xx = over_x(jnp.stack([down_q, down_y]))
        up_all = jnp.concatenate([up_q[None], up_x[None], up_yy], 0).reshape(-1, model)
        down_all = jnp.stack([down_q, down_xx[0], down_y, down_xx[1]]).reshape(-1, model)
        up_b = own(up_bias[None])
        up_b = jnp.concatenate([up_b, over_z(up_b)], 0).astype(F32)
        up_b = absolute(up_b.reshape(2, 2, 2, part).transpose(1, 2, 0, 3)).reshape(-1)
        out_own = own(out_weight)
        out_other = over_z(out_own)
        cot_float = own(cotangent).astype(F32)

        query = ((matmul(full_tokens, query_w) + query_b) * 0.125).astype(BF16)
        keys = matmul(full_tokens, key_w).astype(BF16)
        values = (matmul(full_tokens, value_w) + value_b).astype(BF16)
        context_float, totals = attend_forward(query, keys, values, segment)
        context = context_float.astype(BF16)

        context_own = context[: 2 * rows]
        context_other = over_z(context[2 * rows :])
        partial = matmul(context_own, out_own) + matmul(context_other, out_other)
        attention = partial[:rows] + over_core(partial[rows:].astype(BF16)).astype(F32)
        resid = token_own.astype(F32) + attention + out_bias.astype(F32)
        normed, attn_norm_back = jax.vjp(
            layer_norm, resid, attn_gain.astype(F32), attn_shift.astype(F32)
        )
        normed_low = normed.astype(BF16)
        pair_normed = jnp.concatenate([normed_low, over_core(normed_low)], 0)
        hidden_pre = matmul_right(pair_normed, up_all) + up_b
        gelu_value, gelu_back = jax.vjp(exact_gelu, hidden_pre)
        hidden = gelu_value.astype(BF16)
        partial = matmul(hidden, down_all)
        ffn_out = partial[:rows] + over_core(partial[rows:].astype(BF16)).astype(F32)
        summed = normed + ffn_out + down_bias.astype(F32)
        final, ffn_norm_back = jax.vjp(
            layer_norm, summed, ffn_gain.astype(F32), ffn_shift.astype(F32)
        )
        token_float = token_own.astype(F32)
        layer_out = own((keep_flag * final + (1.0 - keep_flag) * token_float).astype(BF16))

        dsummed, ffn_gain_grad, ffn_shift_grad = ffn_norm_back(keep_flag * cot_float)
        down_bias_grad = jnp.sum(dsummed, 0)
        dffn = dsummed.astype(BF16)
        pair_dffn = jnp.concatenate([dffn, over_core(dffn)], 0)
        shape = (2, 2, 2 * part, model)
        down_grad = matmul_left(hidden, pair_dffn).astype(BF16).reshape(shape)
        dhidden = matmul_right(pair_dffn, down_all)
        dpre = gelu_back(dhidden)[0].astype(BF16)
        up_grad = matmul_left(dpre, pair_normed).astype(BF16).reshape(shape)
        up_bias_grad = jnp.sum(dpre.astype(F32), 0)
        partial = matmul(dpre, up_all)
        dnormed = dsummed + partial[:rows] + over_core(partial[rows:].astype(BF16)).astype(F32)
        dresid, attn_gain_grad, attn_shift_grad = attn_norm_back(dnormed)
        out_bias_grad = jnp.sum(dresid, 0)
        dresid_low = dresid.astype(BF16)
        pair_dresid = jnp.concatenate([dresid_low, over_core(dresid_low)], 0)
        dcontext_own = matmul_right(pair_dresid, out_own).astype(BF16)
        dcontext_other = over_z(matmul_right(pair_dresid, out_other).astype(BF16))
        dcontext = jnp.concatenate([dcontext_own, dcontext_other], 0)
        out_grad = matmul_left(context_own, pair_dresid) + over_z(
            matmul_left(context_other, pair_dresid).astype(BF16)
        ).astype(F32)

        up_one, down_one = reduce_plane(up_grad, down_grad)
        both = jnp.concatenate(
            [up_one.reshape(2, part, model), down_one.reshape(2, part, model)], 1
        )
        both = both[0] + over_z(both[1].astype(BF16)).astype(F32)
        both = to_home(both)
        up_sum, down_sum = spread_plane(both[:part], both[part:])
        up_sum = absolute(up_sum).astype(F32).reshape(-1, model).T
        down_sum = absolute(down_sum).astype(F32).reshape(-1, model)

        dquery, dkey, dvalue = attend_backward(
            query, keys, values, segment, context_float, totals, dcontext
        )
        weight_grads = jnp.concatenate(
            [
                matmul_left(dquery, full_tokens) * 0.125,
                matmul_left(dkey, full_tokens),
                matmul_left(dvalue, full_tokens),
                out_grad,
            ],
            0,
        ).astype(BF16)
        weight_grads = weight_grads.reshape(2, 2, 2, -1, model)
        first_one, second_one = reduce_plane(absolute(weight_grads[0]), absolute(weight_grads[1]))
        both = to_home(jnp.concatenate([first_one, second_one], 0))
        count = both.shape[0] // 2
        first_all, second_all = spread_plane(both[:count], both[count:])
        sums = jnp.concatenate([absolute(first_all), absolute(second_all)], 0)
        sums = sums.reshape(4, width, model).astype(F32)

        input_part = (
            matmul_right(dquery, query_w) * 0.125
            + matmul_right(dkey, key_w)
            + matmul_right(dvalue, value_w)
        )
        low = input_part[2 * rows :].astype(BF16)
        chip_part = input_part[: 2 * rows] + over_z(low).astype(F32)
        own_part = chip_part[:rows] + over_core(chip_part[rows:].astype(BF16)).astype(F32)
        tokens_grad = own((dresid + own_part + (1.0 - keep_flag) * cot_float).astype(BF16))

        shard = 2 * core + zbit
        shard_rows = absolute(up_bias_grad.reshape(2, 2, 2, part)).transpose(2, 0, 1, 3)
        shard_rows = shard_rows.reshape(2, model)
        wide = jnp.zeros((4, model), F32)
        wide = lax.dynamic_update_slice_in_dim(wide, shard_rows[0:1], shard, 0)
        wide = lax.dynamic_update_slice_in_dim(wide, shard_rows[1:2], shard ^ 1, 0)
        narrow = jnp.stack(
            [jnp.sum(dquery.astype(F32), 0) * 0.125, jnp.sum(dvalue.astype(F32), 0)]
        )
        narrow = lax.dynamic_update_slice_in_dim(
            jnp.zeros((2, 4 * width), F32), narrow, shard * width, 1
        )
        small = jnp.concatenate(
            [
                jnp.stack(
                    [
                        out_bias_grad,
                        attn_gain_grad,
                        attn_shift_grad,
                        down_bias_grad,
                        ffn_gain_grad,
                        ffn_shift_grad,
                    ]
                ),
                wide,
                narrow,
            ],
            0,
        )
        bit = 1
        while bit < ndp:
            small = small + exchange(small, lambda i, t, bit=bit: (i ^ bit, t))
            bit *= 2
        small = small + over_z(small)
        small = small + exchange(small, lambda i, t: (i, t ^ 2))
        up_bias_sum = lax.dynamic_slice_in_dim(small[6:10], t, 1, 0)[0]
        narrow = lax.dynamic_slice_in_dim(small[10:12], t * width, width, 1)

        return (
            layer_out,
            tokens_grad,
            sums[0].T,
            narrow[0],
            sums[1].T,
            sums[2].T,
            narrow[1],
            sums[3],
            small[0],
            small[1],
            small[2],
            up_sum,
            up_bias_sum,
            down_sum,
            small[3],
            small[4],
            small[5],
        )

    return jax.shard_map(
        shards,
        mesh=mesh,
        in_specs=(
            P(("dp", "tensor"), None),
            P(("dp", "tensor"), None),
            P("dp", None),
            P("dp"),
            P(None, "tensor"),
            P("tensor"),
            P(None, "tensor"),
            P(None, "tensor"),
            P("tensor"),
            P("tensor", None),
            P(),
            P(),
            P(),
            P(None, "tensor"),
            P("tensor"),
            P("tensor", None),
            P(),
            P(),
            P(),
        ),
        out_specs=(
            P(("dp", "tensor"), None),
            P(("dp", "tensor"), None),
            P(None, "tensor"),
            P("tensor"),
            P(None, "tensor"),
            P(None, "tensor"),
            P("tensor"),
            P("tensor", None),
            P(),
            P(),
            P(),
            P(None, "tensor"),
            P("tensor"),
            P("tensor", None),
            P(),
            P(),
            P(),
        ),
        check_vma=False,
    )
```

```python
import functools

import jax
import jax.numpy as jnp
from jax import lax
from jax.experimental import pallas as pl
from jax.experimental.pallas import tpu as pltpu
from jax.sharding import Mesh
from jax.sharding import PartitionSpec as P

HEAD_DIM = 64
EPS = 1e-05
NEG = -1e30
F32 = jnp.float32
BF16 = jnp.bfloat16
SMEM = pl.BlockSpec(memory_space=pltpu.SMEM)
VMEM = pl.BlockSpec(memory_space=pltpu.VMEM)
SHAPE = jax.ShapeDtypeStruct


def matmul(left, right):
    return jnp.dot(left, right, preferred_element_type=F32)


def matmul_left(left, right):
    return lax.dot_general(left, right, (((0,), (0,)), ((), ())), preferred_element_type=F32)


def matmul_right(left, right):
    return lax.dot_general(left, right, (((1,), (1,)), ((), ())), preferred_element_type=F32)


def stage(*values):
    return lax.optimization_barrier(values)


def layer_norm(value, gain, shift):
    center = value - jnp.mean(value, -1, keepdims=True)
    spread = jnp.mean(center * center, -1, keepdims=True)
    return center * lax.rsqrt(spread + EPS) * gain + shift


def cost(micros):
    return pl.CostEstimate(flops=int(micros * 1e9), bytes_accessed=1 << 20, transcendentals=0)


def head_parts(width):
    return [slice(h, h + HEAD_DIM) for h in range(0, width, HEAD_DIM)]


def attend_forward_kernel(
    bq,
    bk,
    first,
    qlow_ref,
    qhigh_ref,
    klow_ref,
    khigh_ref,
    qkv_ref,
    row_ref,
    column_ref,
    wide_ref,
    context_ref,
    totals_ref,
    top_ref,
    sum_ref,
    acc_ref,
):
    width, count = wide_ref.shape
    length = qkv_ref.shape[1]
    parts = head_parts(width)
    heads = range(len(parts))
    key_parts = head_parts(2 * width)[len(parts) :]
    value_parts = head_parts(3 * width)[2 * len(parts) :]

    def over_query(i, _):
        at_o = pl.ds(pl.multiple_of(i * bq, bq), bq)
        at_q = pl.ds(pl.multiple_of(first + i * bq, bq), bq)
        block = i + first // bq
        top_ref[...] = jnp.full(top_ref.shape, NEG, F32)
        sum_ref[...] = jnp.zeros(sum_ref.shape, F32)
        acc_ref[...] = jnp.zeros(acc_ref.shape, F32)
        row = row_ref[0:1, at_q]

        def over_keys(j, _):
            @pl.when((klow_ref[j] <= qhigh_ref[block]) & (qlow_ref[block] <= khigh_ref[j]))
            def _():
                at_k = pl.ds(pl.multiple_of(j * bk, bk), bk)
                column = column_ref[at_k, :]
                same = jnp.concatenate([column] * (bq // 128), 1) == row
                scores = [
                    matmul_left(qkv_ref[k, at_k], qkv_ref[q, at_q])
                    for k, q in zip(key_parts, parts)
                ]
                scores = [jnp.where(same, value, NEG) for value in scores]
                old = [top_ref[h : h + 1, :] for h in heads]
                top = [jnp.maximum(o, jnp.max(v, 0, keepdims=True)) for o, v in zip(old, scores)]
                exponent = [jnp.exp(v - m) for v, m in zip(scores, top)]
                scale = [jnp.exp(o - m) for o, m in zip(old, top)]
                total = [
                    sum_ref[h : h + 1, :] * scale[h] + jnp.sum(exponent[h], 0, keepdims=True)
                    for h in heads
                ]
                added = [
                    matmul(qkv_ref[v, at_k], e.astype(BF16)) for v, e in zip(value_parts, exponent)
                ]
                added = [acc_ref[p, :] * c + v for p, c, v in zip(parts, scale, added)]
                for h in heads:
                    top_ref[h : h + 1, :] = top[h]
                    sum_ref[h : h + 1, :] = total[h]
                    acc_ref[parts[h], :] = added[h]

            return 0

        lax.fori_loop(0, length // bk, over_keys, 0)
        for h in heads:
            value = acc_ref[parts[h], :] / sum_ref[h : h + 1, :]
            wide_ref[parts[h], at_o] = value
            context_ref[parts[h], at_o] = value.astype(BF16)
            totals_ref[h : h + 1, at_o] = top_ref[h : h + 1, :] + jnp.log(sum_ref[h : h + 1, :])
        return 0

    lax.fori_loop(0, count // bq, over_query, 0)


def attend_backward_kernel(
    bq,
    bk,
    first,
    last,
    qlow_ref,
    qhigh_ref,
    klow_ref,
    khigh_ref,
    qkv_ref,
    dcontext_ref,
    wide_ref,
    totals_ref,
    row_ref,
    column_ref,
    *rest,
):
    if last:
        before_ref, dquery_ref, sums_ref, delta_ref, dq_ref, dk_ref, dv_ref = rest
    else:
        dquery_ref, sums_ref, delta_ref, dq_ref, dk_ref, dv_ref = rest
    width, count = dcontext_ref.shape
    length = qkv_ref.shape[1]
    parts = head_parts(width)
    heads = range(len(parts))
    key_parts = head_parts(2 * width)[len(parts) :]
    value_parts = head_parts(3 * width)[2 * len(parts) :]
    dq_ref[...] = jnp.zeros(dq_ref.shape, F32)
    for h in heads:
        delta_ref[h : h + 1, :] = jnp.sum(
            wide_ref[parts[h], :] * dcontext_ref[parts[h], :].astype(F32), 0, keepdims=True
        )

    def over_keys(j, _):
        at_k = pl.ds(pl.multiple_of(j * bk, bk), bk)
        if last:
            for h in heads:
                dk_ref[parts[h], :] = before_ref[parts[h], at_k]
                dv_ref[parts[h], :] = before_ref[key_parts[h], at_k]
        else:
            dk_ref[...] = jnp.zeros(dk_ref.shape, F32)
            dv_ref[...] = jnp.zeros(dv_ref.shape, F32)

        def over_query(i, _):
            block = i + first // bq

            @pl.when((klow_ref[j] <= qhigh_ref[block]) & (qlow_ref[block] <= khigh_ref[j]))
            def _():
                at_o = pl.ds(pl.multiple_of(i * bq, bq), bq)
                at_q = pl.ds(pl.multiple_of(first + i * bq, bq), bq)
                column = column_ref[at_k, :]
                same = jnp.concatenate([column] * (bq // 128), 1) == row_ref[0:1, at_q]
                scores = [
                    matmul_left(qkv_ref[k, at_k], qkv_ref[q, at_q])
                    for k, q in zip(key_parts, parts)
                ]
                dprobs = [
                    matmul_left(qkv_ref[v, at_k], dcontext_ref[p, at_o])
                    for v, p in zip(value_parts, parts)
                ]
                probs = [
                    jnp.exp(jnp.where(same, scores[h], NEG) - totals_ref[h : h + 1, at_o])
                    for h in heads
                ]
                dscores = [
                    (probs[h] * (dprobs[h] - delta_ref[h : h + 1, at_o])).astype(BF16)
                    for h in heads
                ]
                dv = [
                    matmul_right(dcontext_ref[p, at_o], v.astype(BF16)) for p, v in zip(parts, probs)
                ]
                dk = [matmul_right(qkv_ref[p, at_q], v) for p, v in zip(parts, dscores)]
                dq = [matmul(qkv_ref[k, at_k], v) for k, v in zip(key_parts, dscores)]
                for h in heads:
                    dv_ref[parts[h], :] += dv[h]
                    dk_ref[parts[h], :] += dk[h]
                    dq_ref[parts[h], at_o] += dq[h]

            return 0

        lax.fori_loop(0, count // bq, over_query, 0)
        sums_ref[0:width, at_k] = dk_ref[...].astype(sums_ref.dtype)
        sums_ref[width : 2 * width, at_k] = dv_ref[...].astype(sums_ref.dtype)
        return 0

    lax.fori_loop(0, length // bk, over_keys, 0)
    dquery_ref[...] = dq_ref[...].astype(BF16)


def bounds(segment, block):
    blocks = segment.reshape(-1, block)
    return jnp.min(blocks, 1), jnp.max(blocks, 1)


def attend_forward(qkv, marks, first, count, bq=512, bk=256):
    width = qkv.shape[0] // 3
    segment, row, column = marks
    return pl.pallas_call(
        functools.partial(attend_forward_kernel, bq, bk, first),
        out_shape=(SHAPE((width, count), F32), SHAPE((width, count), BF16), SHAPE((8, count), F32)),
        in_specs=[SMEM] * 4 + [VMEM] * 3,
        out_specs=(VMEM,) * 3,
        scratch_shapes=[pltpu.VMEM((8, bq), F32)] * 2 + [pltpu.VMEM((width, bq), F32)],
        cost_estimate=cost(15),
        name="attend_forward",
    )(*bounds(segment, bq), *bounds(segment, bk), qkv, row, column)


def attend_backward(qkv, dcontext, wide, totals, marks, first, before=None, bq=256, bk=256):
    width, count = dcontext.shape
    length = qkv.shape[1]
    segment, row, column = marks
    last = before is not None
    return pl.pallas_call(
        functools.partial(attend_backward_kernel, bq, bk, first, last),
        out_shape=(SHAPE((width, count), BF16), SHAPE((2 * width, length), BF16 if last else F32)),
        in_specs=[SMEM] * 4 + [VMEM] * (7 if last else 6),
        out_specs=(VMEM,) * 2,
        scratch_shapes=[
            pltpu.VMEM((8, count), F32),
            pltpu.VMEM((width, count), F32),
            pltpu.VMEM((width, bk), F32),
            pltpu.VMEM((width, bk), F32),
        ],
        cost_estimate=cost(20),
        name="attend_backward",
    )(
        *bounds(segment, bq),
        *bounds(segment, bk),
        qkv,
        dcontext,
        wide,
        totals,
        row,
        column,
        *((before,) if last else ()),
    )


def feed_forward_kernel(
    own_ref,
    core_ref,
    here_ref,
    x_ref,
    y_ref,
    up_xy_ref,
    down_xy_ref,
    bias_ref,
    hidden_ref,
    slope_ref,
    mine_ref,
    other_ref,
    up_ref,
    down_ref,
):
    rows, cols = own_ref.shape[0], 256
    part = up_xy_ref.shape[1]
    for k, piece_ref in enumerate((here_ref, x_ref, y_ref)):
        for n in range(2):
            to = slice((2 * k + n) * part, (2 * k + n + 1) * part)
            up_ref[to, :] = piece_ref[n, 0:part, :]
            down_ref[to, :] = piece_ref[n, part : 2 * part, :]
    for n in range(2):
        to = slice((6 + n) * part, (7 + n) * part)
        up_ref[to, :] = up_xy_ref[n]
        down_ref[to, :] = down_xy_ref[n]
    for source, target, start in ((core_ref, other_ref, rows), (own_ref, mine_ref, 0)):
        at = slice(start, start + rows)
        value = source[...]
        for n in range(0, up_ref.shape[0], cols):
            to = slice(n, n + cols)
            pre = matmul_right(value, up_ref[to, :]) + bias_ref[0:1, to]
            normal = 0.5 * (1.0 + lax.erf(pre * 0.7071067811865476))
            hidden_ref[at, to] = (pre * normal).astype(BF16)
            density = jnp.exp(-0.5 * pre * pre) * 0.3989422804014327
            slope_ref[at, to] = (normal + pre * density).astype(BF16)
        target[...] = matmul(hidden_ref[at, :], down_ref[...]).astype(target.dtype)


def feed_forward(own, core, here, x_piece, y_piece, up_xy, down_xy, bias):
    rows, model = own.shape
    units = 8 * up_xy.shape[1]
    return pl.pallas_call(
        feed_forward_kernel,
        out_shape=(
            SHAPE((2 * rows, units), BF16),
            SHAPE((2 * rows, units), BF16),
            SHAPE((rows, model), F32),
            SHAPE((rows, model), BF16),
            SHAPE((units, model), BF16),
            SHAPE((units, model), BF16),
        ),
        in_specs=[VMEM] * 8,
        out_specs=(VMEM,) * 6,
        cost_estimate=cost(12),
        name="feed_forward",
    )(own, core, here, x_piece, y_piece, up_xy, down_xy, jnp.broadcast_to(bias[None], (8, units)))


def project_kernel(own_ref, core_ref, z_ref, zc_ref, weights_ref, bias_ref, qkv_ref):
    rows = own_ref.shape[0]
    width = weights_ref.shape[0] // 3
    for k, ref in enumerate((own_ref, core_ref, z_ref, zc_ref)):
        for n, scale in enumerate((0.125, None, None)):
            at = slice(n * width, (n + 1) * width)
            value = matmul_right(weights_ref[at, :], ref[...]) + bias_ref[at, 0:1]
            value = value * scale if scale else value
            qkv_ref[at, k * rows : (k + 1) * rows] = value.astype(BF16)


def project(tokens, weights, bias):
    return pl.pallas_call(
        project_kernel,
        out_shape=SHAPE((weights.shape[0], 4 * tokens[0].shape[0]), BF16),
        in_specs=[VMEM] * 6,
        out_specs=VMEM,
        cost_estimate=cost(4),
        name="project",
    )(*tokens, weights, jnp.broadcast_to(bias[:, None], (bias.shape[0], 128)))


def weight_grads_kernel(
    own_ref,
    core_ref,
    z_ref,
    zc_ref,
    dquery_own_ref,
    dquery_z_ref,
    sums_ref,
    context_ref,
    dresid_ref,
    dresid_core_ref,
    other_ref,
    packed_ref,
    bias_ref,
):
    rows = own_ref.shape[0]
    width = dquery_own_ref.shape[0]
    total = [0.0, 0.0]
    query = 0.0
    for k, ref in enumerate((own_ref, core_ref, z_ref, zc_ref)):
        value = ref[...]
        at = slice(k * rows, (k + 1) * rows)
        half = dquery_own_ref if k < 2 else dquery_z_ref
        query = query + matmul(half[:, (k % 2) * rows : (k % 2 + 1) * rows], value)
        for n in range(2):
            total[n] = total[n] + matmul(sums_ref[n * width : (n + 1) * width, at], value)
    packed_ref[0:width, :] = (query * 0.125).astype(BF16)
    packed_ref[width : 2 * width, :] = total[0].astype(BF16)
    packed_ref[2 * width : 3 * width, :] = total[1].astype(BF16)
    out = matmul(context_ref[:, 0:rows], dresid_ref[...])
    out = out + matmul(context_ref[:, rows : 2 * rows], dresid_core_ref[...])
    packed_ref[3 * width :, :] = (out + other_ref[...].astype(F32)).astype(BF16)
    count = jnp.ones((8, 2 * rows), BF16)
    query = matmul_right(count, dquery_own_ref[...]) + matmul_right(count, dquery_z_ref[...])
    bias_ref[:, 0:width] = query * 0.125
    values = sums_ref[width : 2 * width, :]
    count = jnp.ones((8, 4 * rows), BF16)
    bias_ref[:, width : 2 * width] = matmul_right(count, values)


def weight_grads(tokens, dquery_own, dquery_z, sums, context, dresid, dresid_core, other):
    width = dquery_own.shape[0]
    return pl.pallas_call(
        weight_grads_kernel,
        out_shape=(
            SHAPE((4 * width, tokens[0].shape[1]), BF16),
            SHAPE((8, 2 * width), F32),
        ),
        in_specs=[VMEM] * 11,
        out_specs=(VMEM,) * 2,
        cost_estimate=cost(6),
        name="weight_grads",
    )(*tokens, dquery_own, dquery_z, sums, context, dresid, dresid_core, other)


def solution(mesh):
    ndp, nt = mesh.shape["dp"], mesh.shape["tensor"]
    fine = Mesh(
        mesh.devices.reshape(ndp // 8, 2, 2, 2, nt), ("outer", "y", "x", "core", "tensor")
    )
    DP, AXES = ("outer", "y", "x", "core"), ("outer", "y", "x", "core", "tensor")

    def moved_at(i, t):
        return (i & 1) != (t >> 1)

    def exchange(value, target, only=None):
        pairs = []
        for i in range(ndp):
            for t in range(nt):
                if only is None or only(i, t):
                    j, u = target(i, t)
                    pairs.append((i * nt + t, j * nt + u))
        return lax.ppermute(value, AXES, pairs)

    def swap(value):
        return exchange(value, lambda i, t: (i ^ 1, t ^ 2), moved_at)

    def over_core(value):
        return exchange(value, lambda i, t: (i ^ 1, t))

    def over_z(value):
        return exchange(value, lambda i, t: (i, t ^ 1))

    def over_x(value):
        return exchange(value, lambda i, t: (i ^ 2, t))

    def over_y(value):
        return exchange(value, lambda i, t: (i ^ 4, t))

    def shards(
        tokens,
        cotangent,
        segment_ids,
        drop_flags,
        query_weight,
        query_bias,
        key_weight,
        value_weight,
        value_bias,
        out_weight,
        out_bias,
        attn_gain,
        attn_shift,
        up_weight,
        up_bias,
        down_weight,
        down_bias,
        ffn_gain,
        ffn_shift,
    ):
        i, t = lax.axis_index(DP), lax.axis_index("tensor")
        core, zbit, xbit, ybit = i & 1, t & 1, (i >> 1) & 1, (i >> 2) & 1
        moved = core != (t >> 1)
        length = segment_ids.shape[1]
        rows, model = tokens.shape
        width = query_weight.shape[1]
        part = up_weight.shape[1] // 4

        def own(value):
            return jnp.where(moved, swap(value), value)

        def turned(value, axis, bit):
            return jnp.where(bit == 1, jnp.flip(value, axis), value)

        def over_plane(value):
            copies = jnp.broadcast_to(value[None], (4,) + value.shape)
            return lax.all_to_all(copies, ("y", "x"), split_axis=0, concat_axis=0, tiled=True)

        def absolute(value):
            return turned(turned(value, 0, ybit), 1, xbit)

        notes = jnp.concatenate(
            [segment_ids, jnp.broadcast_to(drop_flags[:, None], (1, 128))], axis=1
        )
        notes = jnp.where(moved, over_core(notes), notes)
        token_swap = swap(tokens)
        token_z = exchange(tokens, lambda i, t: (i, t ^ 1), lambda i, t: not moved_at(i, t))
        weights = jnp.concatenate([query_weight.T, key_weight.T, value_weight.T], 0)
        biases = jnp.concatenate(
            [query_bias, jnp.zeros_like(query_bias), value_bias, jnp.zeros_like(query_bias)]
        )
        fourth = weights.shape[0] // 4
        place = ybit * 2 + xbit
        piece = lax.dynamic_slice_in_dim(weights, place * fourth, fourth, 0)
        piece = swap(
            jnp.concatenate([piece, jnp.broadcast_to(biases[None], (16, 4 * width))], 0)
        )
        quarter = jnp.concatenate(
            [
                lax.dynamic_slice_in_dim(up_weight, place * part, part, 1).T,
                lax.dynamic_slice_in_dim(down_weight, place * part, part, 0),
                jnp.broadcast_to(up_bias[None], (16, model)),
            ],
            0,
        )
        piece, weights, biases = stage(piece, weights, biases)
        gathered = over_plane(piece)

        token_swap, token_z, quarter, out_weight, segment, keep_flag = stage(
            token_swap,
            token_z,
            quarter,
            out_weight,
            notes[0, :length],
            (1 - notes[0, length]).astype(F32),
        )
        token_own = jnp.where(moved, token_swap, tokens)
        token_core = over_core(token_own)
        token_z = jnp.where(
            moved, exchange(token_own, lambda i, t: (i, t ^ 1), moved_at), token_z
        )
        token_zc = over_core(token_z)
        quarter_swap = swap(quarter)
        biases = jnp.where(moved, gathered[0, fourth], biases)[: 3 * width].astype(F32)
        weights = jnp.where(moved, gathered[:, :fourth].reshape(weights.shape), weights)
        segment = segment.reshape(2, 2, length // 4)
        segment = turned(turned(segment, 0, core), 1, zbit)
        segment = jnp.swapaxes(segment, 0, 1).reshape(length)
        marks = (
            segment,
            jnp.broadcast_to(segment[None], (8, length)),
            jnp.broadcast_to(segment[:, None], (length, 128)),
        )
        group = (token_own, token_core, token_z, token_zc)
        qkv = project(group, weights, biases)

        qkv, quarter_swap, out_weight = stage(qkv, quarter_swap, out_weight)
        quarter = jnp.where(moved, quarter_swap, quarter)
        quarter_z = over_z(quarter)
        out_swap = swap(out_weight)
        half = 2 * rows
        wide_z, context_z, totals_z = attend_forward(qkv, marks, half, half)

        qkv, context_z, quarter, quarter_z, out_swap, cot_in = stage(
            qkv, context_z, quarter, quarter_z, out_swap, cotangent
        )
        context_other = over_z(context_z)
        here = jnp.stack([quarter[: 2 * part], quarter_z[: 2 * part]])
        up_b = jnp.stack([quarter[2 * part], quarter_z[2 * part]]).astype(F32)
        up_b = absolute(up_b.reshape(2, 2, 2, part).transpose(1, 2, 0, 3)).reshape(-1)
        out_own = jnp.where(moved, out_swap, out_weight)
        out_other = over_z(out_own)
        x_piece, y_piece = over_x(here), over_y(here)
        wide_own, context_own, totals_own = attend_forward(qkv, marks, 0, half)

        context_own, context_other, out_other, cot_in = stage(
            context_own, context_other, out_other, cot_in
        )
        cot_swap = swap(cot_in)
        partial = matmul_left(context_own, out_own) + matmul_left(context_other, out_other)
        attention = partial[:rows] + over_core(partial[rows:].astype(BF16)).astype(F32)
        token_float = token_own.astype(F32)
        resid = token_float + attention + out_bias.astype(F32)
        resid, x_piece, y_piece = stage(resid, x_piece, y_piece)
        up_xy, down_xy = over_y(x_piece[:, :part]), over_x(y_piece[:, part:])
        normed, attn_norm_back = jax.vjp(
            layer_norm, resid, attn_gain.astype(F32), attn_shift.astype(F32)
        )
        normed_low = normed.astype(BF16)
        normed_core = over_core(normed_low)

        normed_low, normed_core, up_xy, down_xy, cot_swap = stage(
            normed_low, normed_core, up_xy, down_xy, cot_swap
        )
        hidden, slope, mine, theirs, up_all, down_all = feed_forward(
            normed_low, normed_core, here, x_piece, y_piece, up_xy, down_xy, up_b
        )
        pair_normed = jnp.concatenate([normed_low, normed_core], 0)
        ffn_out = mine + over_core(theirs).astype(F32)
        summed = normed + ffn_out + down_bias.astype(F32)
        final, ffn_norm_back = jax.vjp(
            layer_norm, summed, ffn_gain.astype(F32), ffn_shift.astype(F32)
        )
        cot_float = jnp.where(moved, cot_swap, cotangent).astype(F32)
        dsummed, ffn_gain_grad, ffn_shift_grad = ffn_norm_back(keep_flag * cot_float)
        down_bias_grad = jnp.sum(dsummed, 0)
        dffn = dsummed.astype(BF16)
        pair_dffn = jnp.concatenate([dffn, over_core(dffn)], 0)
        layer_out = (keep_flag * final + (1.0 - keep_flag) * token_float).astype(BF16)

        pair_dffn, layer_out = stage(pair_dffn, layer_out)
        layer_swap = swap(layer_out)
        shape = (2, 2, 2 * part, model)
        down_grad = matmul_left(hidden, pair_dffn).astype(BF16).reshape(shape)
        down_send, down_grad, pair_dffn = stage(down_grad[:, 1], down_grad, pair_dffn)
        down_x = over_x(down_send)
        dhidden = matmul_right(pair_dffn, down_all)
        dpre = (dhidden * slope.astype(F32)).astype(BF16)
        up_grad = matmul_left(dpre, pair_normed).astype(BF16).reshape(shape)
        up_bias_grad = jnp.sum(dpre.astype(F32), 0)
        up_grad, dpre = stage(up_grad, dpre)
        up_y = over_y(up_grad[1])
        partial = matmul(dpre, up_all)
        dnormed = dsummed + partial[:rows] + over_core(partial[rows:].astype(BF16)).astype(F32)
        dresid, attn_gain_grad, attn_shift_grad = attn_norm_back(dnormed)
        out_bias_grad = jnp.sum(dresid, 0)
        dresid_low = dresid.astype(BF16)
        dresid_core = over_core(dresid_low)
        pair_dresid = jnp.concatenate([dresid_low, dresid_core], 0)
        dcontext = matmul_right(jnp.concatenate([out_own, out_other], 0), pair_dresid).astype(BF16)
        dcontext_own, dcontext_z = dcontext[:width], dcontext[width:]
        out_grad_z = matmul(context_other, pair_dresid).astype(BF16)

        dcontext_z, dcontext_own, out_grad_z, down_x, up_y, layer_swap = stage(
            dcontext_z, dcontext_own, out_grad_z, down_x, up_y, layer_swap
        )
        dcontext_other = over_z(dcontext_z)
        out_grad_other = over_z(out_grad_z)
        down_one = down_grad[:, 0].astype(F32) + down_x.astype(F32)
        up_one = up_grad[0].astype(F32) + up_y.astype(F32)
        down_yy = over_y(down_one[1].astype(BF16))
        up_xx = over_x(up_one[1].astype(BF16))
        dquery_own, sums_own = attend_backward(qkv, dcontext_own, wide_own, totals_own, marks, 0)

        dquery_own, sums_own, dcontext_other, out_grad_other, down_yy, up_xx = stage(
            dquery_own, sums_own, dcontext_other, out_grad_other, down_yy, up_xx
        )
        both = jnp.concatenate(
            [
                (up_one[0] + up_xx.astype(F32)).reshape(2, part, model),
                (down_one[0] + down_yy.astype(F32)).reshape(2, part, model),
            ],
            1,
        )
        both_z = over_z(both[1].astype(BF16))
        dquery_z, sums = attend_backward(
            qkv, dcontext_other, wide_z, totals_z, marks, half, sums_own
        )

        dquery_z, sums, both_z = stage(dquery_z, sums, both_z)
        both = both[0] + both_z.astype(F32)
        home = both.astype(BF16)
        eighth = jnp.where(jnp.arange(3 * width) < width, 0.125, 1.0).astype(BF16)[:, None]
        back_weights = weights * eighth
        input_z = (
            matmul_left(dquery_z, back_weights[:width])
            + matmul_left(sums[:, half:], back_weights[width:])
        ).astype(BF16)
        input_z, home = stage(input_z, home)
        input_other = over_z(input_z)
        home = exchange(home, lambda i, t: (i, t ^ 2), moved_at)
        packed, bias_sums = weight_grads(
            group, dquery_own, dquery_z, sums, context_own, dresid_low, dresid_core, out_grad_other
        )
        packed, bias_sums, dquery_own = stage(packed, bias_sums, dquery_own)
        parted = lax.all_to_all(
            packed.reshape(4, width, model), ("y", "x"), split_axis=0, concat_axis=0, tiled=True
        )
        input_own = matmul_left(dquery_own, back_weights[:width]) + matmul_left(
            sums[:, :half], back_weights[width:]
        )
        shard = 2 * core + zbit
        shard_rows = absolute(up_bias_grad.reshape(2, 2, 2, part)).transpose(2, 0, 1, 3)
        shard_rows = shard_rows.reshape(2, 1, model)
        at_shard = (jnp.arange(4) == shard)[:, None], (jnp.arange(4) == (shard ^ 1))[:, None]
        wide = jnp.where(at_shard[0], shard_rows[0], 0.0) + jnp.where(
            at_shard[1], shard_rows[1], 0.0
        )
        narrow = bias_sums[0].reshape(2, 1, width)
        narrow = jnp.where(at_shard[0], narrow, 0.0).reshape(2, model)
        small = jnp.concatenate(
            [
                jnp.stack(
                    [
                        out_bias_grad,
                        attn_gain_grad,
                        attn_shift_grad,
                        down_bias_grad,
                        ffn_gain_grad,
                        ffn_shift_grad,
                    ]
                ),
                wide,
                narrow,
            ],
            0,
        )
        hops = [lambda v: v + over_core(v), lambda v: v + over_x(v), lambda v: v + over_y(v)]
        bit = 8
        while bit < ndp:
            hops.append(lambda v, bit=bit: v + exchange(v, lambda i, t: (i ^ bit, t)))
            bit *= 2
        hops.append(lambda v: v + over_z(v))
        hops.append(lambda v: v + exchange(v, lambda i, t: (i, t ^ 2)))

        def outer(value):
            bit = 8
            while bit < ndp:
                value = value + exchange(
                    value.astype(BF16), lambda i, t, bit=bit: (i ^ bit, t)
                ).astype(F32)
                bit *= 2
            return value

        def hand(first, second):
            handed = exchange(
                second.astype(BF16), lambda i, t: (i ^ 1, t), lambda i, t: not moved_at(i, t)
            )
            return jnp.where(moved, handed, first.astype(BF16))

        input_own, input_other, home, parted, small = stage(
            input_own, input_other, home, parted, small
        )
        chip_part = input_own + input_other.astype(F32)
        core_part = over_core(chip_part[rows:].astype(BF16))
        home = outer(both + home.astype(F32))
        unit_half = hand(home[:part], home[part:])
        quarter_sum = jnp.sum(parted.astype(F32), 0)
        quarter_home = exchange(quarter_sum.astype(BF16), lambda i, t: (i, t ^ 2), moved_at)
        small = hops[0](small)

        core_part, unit_half, quarter_home, small = stage(
            core_part, unit_half, quarter_home, small
        )
        own_part = chip_part[:rows] + core_part.astype(F32)
        tokens_grad = (dresid + own_part + (1.0 - keep_flag) * cot_float).astype(BF16)
        tokens_swap = swap(tokens_grad)
        unit_all = over_plane(unit_half)
        quarter_sum = outer(quarter_sum + quarter_home.astype(F32))
        head_half = hand(quarter_sum[: width // 2], quarter_sum[width // 2 :])
        small = hops[1](small)

        head_half, small = stage(head_half, small)
        head_all = over_plane(head_half)
        small = hops[2](small)
        unit_all, small = stage(unit_all, small)
        unit_other = over_core(unit_all)
        for hop in hops[3:]:
            small = hop(small)
        unit_other, head_all, small = stage(unit_other, head_all, small)
        head_other = over_core(head_all)
        up_sum = jnp.where(moved, unit_other, unit_all).astype(F32).reshape(-1, model).T
        down_sum = jnp.where(moved, unit_all, unit_other).astype(F32).reshape(-1, model)
        up_bias_sum = lax.dynamic_slice_in_dim(small[6:10], t, 1, 0)[0]
        narrow = lax.dynamic_slice_in_dim(small[10:12], t * width, width, 1)
        sums = jnp.concatenate(
            [
                jnp.where(moved, head_other, head_all),
                jnp.where(moved, head_all, head_other),
            ],
            1,
        ).astype(F32)
        tokens_grad = jnp.where(moved, tokens_swap, tokens_grad)
        layer_out = jnp.where(moved, layer_swap, layer_out)

        return (
            layer_out,
            tokens_grad,
            sums[0].T,
            narrow[0],
            sums[1].T,
            sums[2].T,
            narrow[1],
            sums[3],
            small[0],
            small[1],
            small[2],
            up_sum,
            up_bias_sum,
            down_sum,
            small[3],
            small[4],
            small[5],
        )

    return jax.shard_map(
        shards,
        mesh=fine,
        in_specs=(
            P(AXES, None),
            P(AXES, None),
            P(DP, None),
            P(DP),
            P(None, "tensor"),
            P("tensor"),
            P(None, "tensor"),
            P(None, "tensor"),
            P("tensor"),
            P("tensor", None),
            P(),
            P(),
            P(),
            P(None, "tensor"),
            P("tensor"),
            P("tensor", None),
            P(),
            P(),
            P(),
        ),
        out_specs=(
            P(AXES, None),
            P(AXES, None),
            P(None, "tensor"),
            P("tensor"),
            P(None, "tensor"),
            P(None, "tensor"),
            P("tensor"),
            P("tensor", None),
            P(),
            P(),
            P(),
            P(None, "tensor"),
            P("tensor"),
            P("tensor", None),
            P(),
            P(),
            P(),
        ),
        check_vma=False,
    )
```

```python
import functools

import jax
import jax.numpy as jnp
from jax import lax
from jax.experimental import pallas as pl
from jax.experimental.pallas import tpu as pltpu
from jax.sharding import Mesh
from jax.sharding import PartitionSpec as P

HEAD_DIM = 64
QUERIES, KEYS = 512, 256
EPS = 1e-05
NEG = -1e30
F32 = jnp.float32
BF16 = jnp.bfloat16
SMEM = pl.BlockSpec(memory_space=pltpu.SMEM)
VMEM = pl.BlockSpec(memory_space=pltpu.VMEM)
SHAPE = jax.ShapeDtypeStruct


def matmul(left, right):
    return jnp.dot(left, right, preferred_element_type=F32)


def matmul_left(left, right):
    return lax.dot_general(left, right, (((0,), (0,)), ((), ())), preferred_element_type=F32)


def matmul_right(left, right):
    return lax.dot_general(left, right, (((1,), (1,)), ((), ())), preferred_element_type=F32)


def stage(*values):
    return lax.optimization_barrier(values)


def cost(micros):
    return pl.CostEstimate(flops=int(micros * 1e9), bytes_accessed=1 << 12, transcendentals=0)


def room(mebibytes):
    return pltpu.CompilerParams(vmem_limit_bytes=mebibytes << 20)


def head_parts(width):
    return [slice(h, h + HEAD_DIM) for h in range(0, width, HEAD_DIM)]


def attend_forward_kernel(
    bq,
    bk,
    first,
    qlow_ref,
    qhigh_ref,
    klow_ref,
    khigh_ref,
    qkv_ref,
    row_ref,
    column_ref,
    wide_ref,
    context_ref,
    totals_ref,
    top_ref,
    sum_ref,
    acc_ref,
):
    width, count = wide_ref.shape
    length = qkv_ref.shape[1]
    parts = head_parts(width)
    heads = range(len(parts))
    key_parts = head_parts(2 * width)[len(parts) :]
    value_parts = head_parts(3 * width)[2 * len(parts) :]

    def over_query(i, _):
        at_o = pl.ds(pl.multiple_of(i * bq, bq), bq)
        at_q = pl.ds(pl.multiple_of(first + i * bq, bq), bq)
        block = i + first // bq
        top_ref[...] = jnp.full(top_ref.shape, NEG, F32)
        sum_ref[...] = jnp.zeros(sum_ref.shape, F32)
        acc_ref[...] = jnp.zeros(acc_ref.shape, F32)
        row = row_ref[0:1, at_q]

        def over_keys(j, _):
            @pl.when((klow_ref[j] <= qhigh_ref[block]) & (qlow_ref[block] <= khigh_ref[j]))
            def _():
                at_k = pl.ds(pl.multiple_of(j * bk, bk), bk)
                column = column_ref[at_k, :]
                same = jnp.concatenate([column] * (bq // 128), 1) == row
                scores = [
                    matmul_left(qkv_ref[k, at_k], qkv_ref[q, at_q])
                    for k, q in zip(key_parts, parts)
                ]
                scores = [jnp.where(same, value, NEG) for value in scores]
                old = [top_ref[h : h + 1, :] for h in heads]
                top = [jnp.maximum(o, jnp.max(v, 0, keepdims=True)) for o, v in zip(old, scores)]
                exponent = [jnp.exp(v - m) for v, m in zip(scores, top)]
                scale = [jnp.exp(o - m) for o, m in zip(old, top)]
                total = [
                    sum_ref[h : h + 1, :] * scale[h] + jnp.sum(exponent[h], 0, keepdims=True)
                    for h in heads
                ]
                added = [
                    matmul(qkv_ref[v, at_k], e.astype(BF16)) for v, e in zip(value_parts, exponent)
                ]
                added = [acc_ref[p, :] * c + v for p, c, v in zip(parts, scale, added)]
                for h in heads:
                    top_ref[h : h + 1, :] = top[h]
                    sum_ref[h : h + 1, :] = total[h]
                    acc_ref[parts[h], :] = added[h]

            return 0

        lax.fori_loop(0, length // bk, over_keys, 0)
        for h in heads:
            value = acc_ref[parts[h], :] / sum_ref[h : h + 1, :]
            wide_ref[parts[h], at_o] = value
            context_ref[parts[h], at_o] = value.astype(BF16)
            totals_ref[h : h + 1, at_o] = top_ref[h : h + 1, :] + jnp.log(sum_ref[h : h + 1, :])
        return 0

    lax.fori_loop(0, count // bq, over_query, 0)


def attend_backward_kernel(
    bq,
    bk,
    first,
    base,
    follows,
    qlow_ref,
    qhigh_ref,
    klow_ref,
    khigh_ref,
    qkv_ref,
    dcontext_ref,
    wide_ref,
    totals_ref,
    row_ref,
    column_ref,
    *rest,
):
    if follows:
        before_ref, dquery_ref, sums_ref, delta_ref, dq_ref, dk_ref, dv_ref = rest
    else:
        dquery_ref, sums_ref, delta_ref, dq_ref, dk_ref, dv_ref = rest
    width, count = dquery_ref.shape
    length = qkv_ref.shape[1]
    parts = head_parts(width)
    heads = range(len(parts))
    key_parts = head_parts(2 * width)[len(parts) :]
    value_parts = head_parts(3 * width)[2 * len(parts) :]
    dq_ref[...] = jnp.zeros(dq_ref.shape, F32)
    chunk = slice(base, base + count)
    for h in heads:
        delta_ref[h : h + 1, :] = jnp.sum(
            wide_ref[parts[h], chunk] * dcontext_ref[parts[h], chunk].astype(F32), 0, keepdims=True
        )

    def over_keys(j, _):
        at_k = pl.ds(pl.multiple_of(j * bk, bk), bk)
        if follows:
            dk_ref[...] = before_ref[0:width, at_k]
            dv_ref[...] = before_ref[width : 2 * width, at_k]
        else:
            dk_ref[...] = jnp.zeros(dk_ref.shape, F32)
            dv_ref[...] = jnp.zeros(dv_ref.shape, F32)

        def over_query(i, _):
            block = i + first // bq

            @pl.when((klow_ref[j] <= qhigh_ref[block]) & (qlow_ref[block] <= khigh_ref[j]))
            def _():
                at_o = pl.ds(pl.multiple_of(i * bq, bq), bq)
                at_b = pl.ds(pl.multiple_of(base + i * bq, bq), bq)
                at_q = pl.ds(pl.multiple_of(first + i * bq, bq), bq)
                column = column_ref[at_k, :]
                same = jnp.concatenate([column] * (bq // 128), 1) == row_ref[0:1, at_q]
                scores = [
                    matmul_left(qkv_ref[k, at_k], qkv_ref[q, at_q])
                    for k, q in zip(key_parts, parts)
                ]
                dprobs = [
                    matmul_left(qkv_ref[v, at_k], dcontext_ref[p, at_b])
                    for v, p in zip(value_parts, parts)
                ]
                probs = [
                    jnp.exp(jnp.where(same, scores[h], NEG) - totals_ref[h : h + 1, at_b])
                    for h in heads
                ]
                dscores = [
                    (probs[h] * (dprobs[h] - delta_ref[h : h + 1, at_o])).astype(BF16)
                    for h in heads
                ]
                dv = [
                    matmul_right(dcontext_ref[p, at_b], v.astype(BF16)) for p, v in zip(parts, probs)
                ]
                dk = [matmul_right(qkv_ref[p, at_q], v) for p, v in zip(parts, dscores)]
                dq = [matmul(qkv_ref[k, at_k], v) for k, v in zip(key_parts, dscores)]
                for h in heads:
                    dv_ref[parts[h], :] += dv[h]
                    dk_ref[parts[h], :] += dk[h]
                    dq_ref[parts[h], at_o] += dq[h]

            return 0

        lax.fori_loop(0, count // bq, over_query, 0)
        sums_ref[0:width, at_k] = dk_ref[...].astype(sums_ref.dtype)
        sums_ref[width : 2 * width, at_k] = dv_ref[...].astype(sums_ref.dtype)
        return 0

    lax.fori_loop(0, length // bk, over_keys, 0)
    dquery_ref[...] = dq_ref[...].astype(BF16)


def bounds(segment, block):
    blocks = segment.reshape(-1, block)
    return jnp.min(blocks, 1), jnp.max(blocks, 1)


def attend_forward(qkv, marks, first, count):
    width = qkv.shape[0] // 3
    wide_low, wide_high, low, high, row, column = marks
    bq, bk = QUERIES, KEYS
    return pl.pallas_call(
        functools.partial(attend_forward_kernel, bq, bk, first),
        out_shape=(SHAPE((width, count), F32), SHAPE((width, count), BF16), SHAPE((8, count), F32)),
        in_specs=[SMEM] * 4 + [VMEM] * 3,
        out_specs=(VMEM,) * 3,
        scratch_shapes=[pltpu.VMEM((8, bq), F32)] * 2 + [pltpu.VMEM((width, bq), F32)],
        cost_estimate=cost(15),
        compiler_params=room(16),
        name="attend_forward",
    )(wide_low, wide_high, low, high, qkv, row, column)


def attend_backward(qkv, around, marks, first, base, count, before, kind):
    dcontext, wide, totals = around
    width, length = dcontext.shape[0], qkv.shape[1]
    _, _, low, high, row, column = marks
    bq = bk = KEYS
    follows = before is not None
    return pl.pallas_call(
        functools.partial(attend_backward_kernel, bq, bk, first, base, follows),
        out_shape=(SHAPE((width, count), BF16), SHAPE((2 * width, length), kind)),
        in_specs=[SMEM] * 4 + [VMEM] * (7 if follows else 6),
        out_specs=(VMEM,) * 2,
        scratch_shapes=[
            pltpu.VMEM((8, count), F32),
            pltpu.VMEM((width, count), F32),
            pltpu.VMEM((width, bk), F32),
            pltpu.VMEM((width, bk), F32),
        ],
        cost_estimate=cost(count // 64),
        compiler_params=room(22),
        name="attend_backward",
    )(
        low,
        high,
        low,
        high,
        qkv,
        dcontext,
        wide,
        totals,
        row,
        column,
        *((before,) if follows else ()),
    )


def plane_slots(flags_ref, slots):
    slots = [jnp.where(flags_ref[2] == 1, slots[k ^ 1], slots[k]) for k in range(4)]
    return [jnp.where(flags_ref[3] == 1, slots[k ^ 2], slots[k]) for k in range(4)]


def feed_forward_kernel(flags_ref, own_ref, core_ref, *rest):
    pieces, (hidden_ref, slope_ref, mine_ref, other_ref, up_ref, down_ref) = rest[:-6], rest[-6:]
    rows, cols = own_ref.shape[0], 256
    part = up_ref.shape[0] // 8
    for n in range(2):
        for k in range(4):
            to = slice((2 * k + n) * part, (2 * k + n + 1) * part)
            up, down = pieces[4 * n + k][0:part, :], pieces[4 * n + k][part : 2 * part, :]
            if n == 0 and k > 0:
                up = up + pieces[8][k - 1, 0:part, :]
                down = down + pieces[8][k - 1, part : 2 * part, :]
            up_ref[to, :] = up
            down_ref[to, :] = down
    biases = []
    for n in range(2):
        value = pieces[4 * n][2 * part : 2 * part + 16, :].astype(F32)[0:1]
        biases.append(plane_slots(flags_ref, [value[:, k * part : (k + 1) * part] for k in range(4)]))
    biases = jnp.concatenate([biases[n][k] for k in range(4) for n in range(2)], 1)
    for source, target, start in ((core_ref, other_ref, rows), (own_ref, mine_ref, 0)):
        at = slice(start, start + rows)
        value = source[...]
        for n in range(0, up_ref.shape[0], cols):
            to = slice(n, n + cols)
            pre = matmul_right(value, up_ref[to, :]) + biases[:, to]
            normal = 0.5 * (1.0 + lax.erf(pre * 0.7071067811865476))
            hidden_ref[at, to] = (pre * normal).astype(BF16)
            density = jnp.exp(-0.5 * pre * pre) * 0.3989422804014327
            slope_ref[at, to] = (normal + pre * density).astype(BF16)
        target[...] = matmul(hidden_ref[at, :], down_ref[...]).astype(target.dtype)


def feed_forward(flags, own, core, pieces):
    rows, model = own.shape
    units = 2 * model
    return pl.pallas_call(
        feed_forward_kernel,
        out_shape=(
            SHAPE((2 * rows, units), BF16),
            SHAPE((2 * rows, units), BF16),
            SHAPE((rows, model), F32),
            SHAPE((rows, model), BF16),
            SHAPE((units, model), BF16),
            SHAPE((units, model), BF16),
        ),
        in_specs=[SMEM] + [VMEM] * 11,
        out_specs=(VMEM,) * 6,
        cost_estimate=cost(12),
        compiler_params=room(32),
        name="feed_forward",
    )(flags, own, core, *pieces)


def hidden_back_kernel(
    own_ref, core_ref, slope_ref, up_ref, down_ref, dpre_ref, mine_ref, other_ref, bias_ref
):
    rows, cols = own_ref.shape[0], 256
    for source, target, start in ((core_ref, other_ref, rows), (own_ref, mine_ref, 0)):
        at = slice(start, start + rows)
        value = source[...]
        for n in range(0, up_ref.shape[0], cols):
            to = slice(n, n + cols)
            dhidden = matmul_right(value, down_ref[to, :])
            dpre_ref[at, to] = (dhidden * slope_ref[at, to].astype(F32)).astype(BF16)
        target[...] = matmul(dpre_ref[at, :], up_ref[...]).astype(target.dtype)
    bias_ref[...] = matmul(jnp.ones((8, 2 * rows), BF16), dpre_ref[...])


def hidden_back(own, core, slope, up, down):
    rows, model = own.shape
    units = up.shape[0]
    return pl.pallas_call(
        hidden_back_kernel,
        out_shape=(
            SHAPE((2 * rows, units), BF16),
            SHAPE((rows, model), F32),
            SHAPE((rows, model), BF16),
            SHAPE((8, units), F32),
        ),
        in_specs=[VMEM] * 5,
        out_specs=(VMEM,) * 4,
        cost_estimate=cost(6),
        compiler_params=room(26),
        name="hidden_back",
    )(own, core, slope, up, down)


def unit_grads_kernel(left_ref, own_ref, core_ref, *refs):
    rows = own_ref.shape[0]
    part = left_ref.shape[1] // 8
    places = ((0, 0), (1, 0), (0, 1), (1, 1)), ((0, 0), (0, 1), (1, 0), (1, 1))
    for k in range(4):
        at = slice(2 * k * part, 2 * (k + 1) * part)
        total = matmul_left(left_ref[0:rows, at], own_ref[...])
        total = total + matmul_left(left_ref[rows : 2 * rows, at], core_ref[...])
        for n in range(2):
            sent, slot = places[n][k]
            to = slice(slot * part, (slot + 1) * part)
            refs[2 * n + sent][to, :] = total[n * part : (n + 1) * part].astype(BF16)


def unit_grads(left, own, core):
    return pl.pallas_call(
        unit_grads_kernel,
        out_shape=(SHAPE((left.shape[1] // 4, own.shape[1]), BF16),) * 4,
        in_specs=[VMEM] * 3,
        out_specs=(VMEM,) * 4,
        cost_estimate=cost(3),
        compiler_params=room(18),
        name="unit_grads",
    )(left, own, core)


def out_project_kernel(own_ref, other_ref, own_w_ref, other_w_ref, mine_ref, theirs_ref):
    rows = mine_ref.shape[0]
    for target, at in ((theirs_ref, slice(rows, 2 * rows)), (mine_ref, slice(0, rows))):
        value = matmul_left(own_ref[:, at], own_w_ref[...])
        value = value + matmul_left(other_ref[:, at], other_w_ref[...])
        target[...] = value.astype(target.dtype)


def out_project(own, other, own_weight, other_weight):
    rows, model = own.shape[1] // 2, own_weight.shape[1]
    return pl.pallas_call(
        out_project_kernel,
        out_shape=(SHAPE((rows, model), F32), SHAPE((rows, model), BF16)),
        in_specs=[VMEM] * 4,
        out_specs=(VMEM,) * 2,
        cost_estimate=cost(3),
        compiler_params=room(12),
        name="out_project",
    )(own, other, own_weight, other_weight)


def input_back_kernel(start, first_ref, second_ref, sums_ref, weights_ref, mine_ref, theirs_ref):
    rows = first_ref.shape[1]
    width = first_ref.shape[0]
    query_weights = weights_ref[0:width, :] * 0.125
    for k, ref, target in ((1, second_ref, theirs_ref), (0, first_ref, mine_ref)):
        at = slice(start + k * rows, start + (k + 1) * rows)
        value = matmul_left(ref[...], query_weights)
        value = value + matmul_left(sums_ref[:, at], weights_ref[width:, :])
        target[...] = value.astype(target.dtype)


def input_back(start, first, second, sums, weights):
    shape = (first.shape[1], weights.shape[1])
    return pl.pallas_call(
        functools.partial(input_back_kernel, start),
        out_shape=(SHAPE(shape, F32), SHAPE(shape, BF16)),
        in_specs=[VMEM] * 4,
        out_specs=(VMEM,) * 2,
        cost_estimate=cost(0),
        compiler_params=room(14),
        name="input_back",
    )(first, second, sums, weights)


def input_own_kernel(
    flags_ref,
    first_ref,
    second_ref,
    sums_ref,
    weights_ref,
    dresid_ref,
    cotangent_ref,
    mine_ref,
    theirs_ref,
):
    width, rows = first_ref.shape
    query_weights = weights_ref[0:width, :] * 0.125
    for k, ref in ((1, second_ref), (0, first_ref)):
        at = slice(k * rows, (k + 1) * rows)
        value = matmul_left(ref[...], query_weights)
        value = value + matmul_left(sums_ref[:, at], weights_ref[width:, :])
        if k == 1:
            theirs_ref[...] = value.astype(BF16)
        else:
            skipped = (1 - flags_ref[1]).astype(F32)
            mine_ref[...] = value + dresid_ref[...] + skipped * cotangent_ref[...].astype(F32)


def context_back_kernel(
    own_ref, core_ref, own_w_ref, other_w_ref, context_ref, mine_ref, theirs_ref, grad_ref
):
    rows = own_ref.shape[0]
    grad = 0.0
    for k, ref in enumerate((own_ref, core_ref)):
        at = slice(k * rows, (k + 1) * rows)
        theirs_ref[:, at] = matmul_right(other_w_ref[...], ref[...]).astype(BF16)
        mine_ref[:, at] = matmul_right(own_w_ref[...], ref[...]).astype(BF16)
        grad = grad + matmul(context_ref[:, at], ref[...])
    grad_ref[...] = grad.astype(BF16)


def take_kernel(
    flags_ref,
    query_ref,
    key_ref,
    value_ref,
    extra_ref,
    up_ref,
    down_ref,
    piece_ref,
    quarter_ref,
    local_ref,
    turned_ref,
):
    place = flags_ref[0]
    held = 1.0 - flags_ref[1].astype(F32)
    fourth = query_ref.shape[0] // 4
    for n, ref in enumerate((query_ref, key_ref, value_ref)):
        at = pl.ds(pl.multiple_of(place * fourth, fourth), fourth)
        piece_ref[n * fourth : (n + 1) * fourth, :] = ref[at, :]
    piece_ref[3 * fourth :, :] = extra_ref[0:16, :]
    turned_ref[...] = up_ref[...].T
    part = local_ref.shape[1] // 2
    quarter_ref[2 * part :, :] = extra_ref[16:32, :]
    for k in range(4):
        at = pl.ds(pl.multiple_of((place ^ k) * part, part), part)
        if k == 0:
            quarter_ref[0:part, :] = turned_ref[at, :]
            quarter_ref[part : 2 * part, :] = down_ref[at, :]
        else:
            local_ref[k - 1, 0:part, :] = (turned_ref[at, :] * held).astype(BF16)
            local_ref[k - 1, part : 2 * part, :] = (down_ref[at, :] * held).astype(BF16)


def take(place, heads, extra, up, down):
    units, model = down.shape
    rows = heads[0].shape[0] // 4 * 3 + 16
    return pl.pallas_call(
        take_kernel,
        out_shape=(
            SHAPE((rows, model), BF16),
            SHAPE((units // 2 + 16, model), BF16),
            SHAPE((3, units // 2, model), BF16),
        ),
        in_specs=[SMEM] + [VMEM] * 6,
        out_specs=(VMEM,) * 3,
        scratch_shapes=[pltpu.VMEM((units, model), BF16)],
        cost_estimate=cost(20),
        compiler_params=room(14),
        name="take",
    )(place, *heads, extra, up, down)


def small_kernel(kernel, name, results, flags, *operands, mebibytes=16):
    return pl.pallas_call(
        kernel,
        out_shape=tuple(SHAPE(shape, kind) for shape, kind in results),
        in_specs=[SMEM] * len(flags) + [VMEM] * len(operands),
        out_specs=(VMEM,) * len(results),
        cost_estimate=cost(0),
        compiler_params=room(mebibytes),
        name=name,
    )(*flags, *operands)


def fold_plane_kernel(*refs):
    part = refs[0].shape[0] // 2
    for n in range(2):
        kept_ref, send_ref = refs[8 + 2 * n], refs[9 + 2 * n]
        for k in range(2):
            keep_ref, got_ref = refs[4 * n + 2 * k], refs[4 * n + 2 * k + 1]
            at = slice(k * part, (k + 1) * part)
            kept_ref[at, :] = keep_ref[0:part, :].astype(F32) + got_ref[0:part, :].astype(F32)
            sent = keep_ref[part : 2 * part, :].astype(F32) + got_ref[part : 2 * part, :].astype(F32)
            send_ref[at, :] = sent.astype(BF16)


def fold_shards_kernel(own_ref, own_got_ref, other_ref, other_got_ref, sum_ref, send_ref):
    sum_ref[...] = own_ref[...] + own_got_ref[...].astype(F32)
    send_ref[...] = (other_ref[...] + other_got_ref[...].astype(F32)).astype(BF16)


def split_home(flags_ref, value, kept_ref, send_ref, far_ref):
    half = kept_ref.shape[0]
    kept_ref[...] = value[:half]
    far_ref[...] = value[half:].astype(BF16)

    @pl.when(flags_ref[0] == 1)
    def _():
        send_ref[...] = value[:half].astype(BF16)

    @pl.when(flags_ref[0] == 0)
    def _():
        send_ref[...] = value[half:].astype(BF16)


def fold_z_kernel(flags_ref, sum_ref, got_ref, kept_ref, send_ref, far_ref):
    split_home(flags_ref, sum_ref[...] + got_ref[...].astype(F32), kept_ref, send_ref, far_ref)


def fold_parts_kernel(flags_ref, parts_ref, kept_ref, send_ref, far_ref):
    value = parts_ref[0].astype(F32) + parts_ref[1].astype(F32)
    value = value + (parts_ref[2].astype(F32) + parts_ref[3].astype(F32))
    half = kept_ref.shape[0] - 16
    tail = value[2 * half :]
    kept_ref[0:half, :] = value[:half]
    kept_ref[half:, :] = tail
    far_ref[0:half, :] = value[half : 2 * half].astype(BF16)
    far_ref[half:, :] = tail.astype(BF16)
    send_ref[half:, :] = tail.astype(BF16)

    @pl.when(flags_ref[0] == 1)
    def _():
        send_ref[0:half, :] = value[:half].astype(BF16)

    @pl.when(flags_ref[0] == 0)
    def _():
        send_ref[0:half, :] = value[half : 2 * half].astype(BF16)


def gather_small_kernel(flags_ref, attn_ref, ffn_ref, bias_ref, small_ref):
    part = attn_ref.shape[1] // 4
    small_ref[...] = jnp.zeros(small_ref.shape, F32)
    small_ref[0:3, :] = attn_ref[0:3, :]
    small_ref[3:6, :] = ffn_ref[0:3, :]
    wide = 0.0
    for n in range(2):
        slots = [bias_ref[0:1, (2 * k + n) * part : (2 * k + n + 1) * part] for k in range(4)]
        value = jnp.concatenate(plane_slots(flags_ref, slots), 1)
        at = lax.broadcasted_iota(jnp.int32, (4, value.shape[1]), 0) == (flags_ref[4] ^ n)
        wide = wide + jnp.where(at, value, 0.0)
    small_ref[6:10, :] = wide


def fold_inputs_kernel(mine_ref, theirs_ref, result_ref):
    result_ref[...] = (mine_ref[...] + theirs_ref[...].astype(F32)).astype(BF16)


def add_tokens_kernel(mine_ref, theirs_ref, other_ref, result_ref):
    other = theirs_ref[...].astype(F32) + other_ref[...].astype(F32)
    result_ref[...] = (mine_ref[...] + other).astype(BF16)


def fold_home_kernel(flags_ref, kept_ref, got_ref, far_ref, result_ref):
    got = got_ref[...].astype(F32)
    first = jnp.where(flags_ref[0] == 1, far_ref[...].astype(F32), kept_ref[...])
    result_ref[...] = (first + got).astype(result_ref.dtype)


def unit_results_kernel(flags_ref, mine_ref, other_ref, up_ref, down_ref):
    def put(first_ref, second_ref):
        part = first_ref.shape[1]
        for k in range(4):
            down_ref[k * part : (k + 1) * part, :] = second_ref[k].astype(F32)
        up_ref[...] = first_ref[...].reshape(4 * part, first_ref.shape[2]).astype(F32).T

    @pl.when(flags_ref[0] == 1)
    def _():
        put(other_ref, mine_ref)

    @pl.when(flags_ref[0] == 0)
    def _():
        put(mine_ref, other_ref)


def head_results_kernel(flags_ref, mine_ref, other_ref, *results):
    half = mine_ref.shape[1]
    for k, ref in enumerate(results):
        mine, other = mine_ref[k].astype(F32), other_ref[k].astype(F32)
        ref[0:half, :] = jnp.where(flags_ref[0] == 1, other, mine)
        ref[half : 2 * half, :] = jnp.where(flags_ref[0] == 1, mine, other)


def normal_rows(value):
    center = value - jnp.mean(value, -1, keepdims=True)
    root = lax.rsqrt(jnp.mean(center * center, -1, keepdims=True) + EPS)
    return center * root, root


def normal_back(grad, normal, root):
    inner = jnp.mean(grad * normal, -1, keepdims=True)
    return root * (grad - jnp.mean(grad, -1, keepdims=True) - normal * inner)


STEP = 128


def first_norm_kernel(mine_ref, got_ref, token_ref, vector_ref, resid_ref, normed_ref, low_ref):
    def step(k, _):
        at = pl.ds(pl.multiple_of(k * STEP, STEP), STEP)
        attention = mine_ref[at, :] + got_ref[at, :].astype(F32)
        resid = token_ref[at, :].astype(F32) + attention + vector_ref[0:1, :]
        resid_ref[at, :] = resid
        normed = normal_rows(resid)[0] * vector_ref[1:2, :] + vector_ref[2:3, :]
        normed_ref[at, :] = normed
        low_ref[at, :] = normed.astype(BF16)
        return 0

    lax.fori_loop(0, mine_ref.shape[0] // STEP, step, 0)


def second_norm_kernel(
    flags_ref,
    mine_ref,
    got_ref,
    normed_ref,
    cotangent_ref,
    token_ref,
    vector_ref,
    layer_ref,
    dsummed_ref,
    low_ref,
    sums_ref,
):
    keep = flags_ref[1].astype(F32)
    sums_ref[...] = jnp.zeros(sums_ref.shape, F32)

    def step(k, _):
        at = pl.ds(pl.multiple_of(k * STEP, STEP), STEP)
        units = mine_ref[at, :] + got_ref[at, :].astype(F32)
        normal, root = normal_rows(normed_ref[at, :] + units + vector_ref[0:1, :])
        final = normal * vector_ref[1:2, :] + vector_ref[2:3, :]
        token = token_ref[at, :].astype(F32)
        layer_ref[at, :] = (keep * final + (1.0 - keep) * token).astype(BF16)
        cotangent = cotangent_ref[at, :].astype(F32)
        dfinal = keep * cotangent
        dsummed = normal_back(dfinal * vector_ref[1:2, :], normal, root)
        dsummed_ref[at, :] = dsummed
        low_ref[at, :] = dsummed.astype(BF16)
        sums_ref[0:1, :] += jnp.sum(dsummed, 0, keepdims=True)
        sums_ref[1:2, :] += jnp.sum(dfinal * normal, 0, keepdims=True)
        sums_ref[2:3, :] += jnp.sum(dfinal, 0, keepdims=True)
        return 0

    lax.fori_loop(0, mine_ref.shape[0] // STEP, step, 0)


def first_norm_back_kernel(
    mine_ref, got_ref, dsummed_ref, resid_ref, vector_ref, dresid_ref, low_ref, sums_ref
):
    sums_ref[...] = jnp.zeros(sums_ref.shape, F32)

    def step(k, _):
        at = pl.ds(pl.multiple_of(k * STEP, STEP), STEP)
        dnormed = dsummed_ref[at, :] + (mine_ref[at, :] + got_ref[at, :].astype(F32))
        normal, root = normal_rows(resid_ref[at, :])
        dresid = normal_back(dnormed * vector_ref[1:2, :], normal, root)
        dresid_ref[at, :] = dresid
        low_ref[at, :] = dresid.astype(BF16)
        sums_ref[0:1, :] += jnp.sum(dresid, 0, keepdims=True)
        sums_ref[1:2, :] += jnp.sum(dnormed * normal, 0, keepdims=True)
        sums_ref[2:3, :] += jnp.sum(dnormed, 0, keepdims=True)
        return 0

    lax.fori_loop(0, mine_ref.shape[0] // STEP, step, 0)


def vectors(bias, gain, shift):
    return jnp.concatenate([jnp.stack([bias, gain, shift]), jnp.zeros((5,) + bias.shape)]).astype(F32)


def rowwise(kernel, name, kinds, flags, *operands):
    shape = operands[0].shape
    results = tuple(SHAPE(shape if kind else (8, shape[1]), kind or F32) for kind in kinds)
    return pl.pallas_call(
        kernel,
        out_shape=results,
        in_specs=[SMEM] * len(flags) + [VMEM] * len(operands),
        out_specs=(VMEM,) * len(results),
        cost_estimate=cost(2),
        compiler_params=room(16),
        name=name,
    )(*flags, *operands)


def project_kernel(own_ref, core_ref, z_ref, zc_ref, gathered_ref, qkv_ref, weights_ref):
    rows = own_ref.shape[0]
    fourth = weights_ref.shape[0] // 4
    width = weights_ref.shape[0] // 3
    for k in range(4):
        for n in range(3):
            piece = fourth // 3
            to = slice(n * width + k * piece, n * width + (k + 1) * piece)
            weights_ref[to, :] = gathered_ref[k, n * piece : (n + 1) * piece, :]
    weights = weights_ref[...]
    biases = gathered_ref[0, fourth : fourth + 16, 0 : 3 * width]
    first = lax.broadcasted_iota(jnp.int32, (16, rows), 0) == 0
    columns = matmul_left(biases, jnp.where(first, 1.0, 0.0).astype(BF16))
    for k, ref in enumerate((own_ref, core_ref, z_ref, zc_ref)):
        at = slice(k * rows, (k + 1) * rows)
        value = matmul_right(weights, ref[...]) + columns
        qkv_ref[0:width, at] = (value[:width] * 0.125).astype(BF16)
        qkv_ref[width:, at] = value[width:].astype(BF16)


def project(tokens, gathered):
    rows, model = tokens[0].shape
    units = 4 * (gathered.shape[1] - 16)
    return pl.pallas_call(
        project_kernel,
        out_shape=(SHAPE((units, 4 * rows), BF16), SHAPE((units, model), BF16)),
        in_specs=[VMEM] * 5,
        out_specs=(VMEM,) * 2,
        cost_estimate=cost(4),
        compiler_params=room(20),
        name="project",
    )(*tokens, gathered)


def weight_grads_kernel(
    own_ref,
    core_ref,
    z_ref,
    zc_ref,
    dq_own_ref,
    dq_core_ref,
    dq_z_ref,
    dq_zc_ref,
    sums_ref,
    context_ref,
    dresid_ref,
    dresid_core_ref,
    other_ref,
    small_ref,
    packed_ref,
):
    rows = own_ref.shape[0]
    width = dq_own_ref.shape[0]
    tokens = (own_ref, core_ref, z_ref, zc_ref)
    dquery = (dq_own_ref, dq_core_ref, dq_z_ref, dq_zc_ref)
    total, query, bias = 0.0, 0.0, 0.0
    count = jnp.ones((8, rows), BF16)
    for k in range(4):
        value = tokens[k][...]
        query = query + matmul(dquery[k][...], value)
        total = total + matmul(sums_ref[:, k * rows : (k + 1) * rows], value)
        bias = bias + matmul_right(count, dquery[k][...])
    packed_ref[0, 0:width, :] = (query * 0.125).astype(BF16)
    packed_ref[1, 0:width, :] = total[:width].astype(BF16)
    packed_ref[2, 0:width, :] = total[width:].astype(BF16)
    out = matmul(context_ref[:, 0:rows], dresid_ref[...])
    out = out + matmul(context_ref[:, rows : 2 * rows], dresid_core_ref[...])
    packed_ref[3, 0:width, :] = (out + other_ref[...].astype(F32)).astype(BF16)
    count = jnp.ones((8, 4 * rows), BF16)
    values = matmul_right(count, sums_ref[width : 2 * width, :])
    biases = jnp.concatenate([bias * 0.125, values, jnp.zeros_like(bias), jnp.zeros_like(bias)], 1)
    at_row = lax.broadcasted_iota(jnp.int32, (8, 4 * width), 0) == 4
    late = jnp.where(at_row, biases, small_ref[8:16, :])
    tail = jnp.concatenate([small_ref[0:8, :], late], 0).astype(BF16)
    for k in range(4):
        packed_ref[k, width : width + 16, :] = tail


def weight_grads(tokens, dquery, sums, context, dresid, dresid_core, other, small):
    width = dquery[0].shape[0]
    return pl.pallas_call(
        weight_grads_kernel,
        out_shape=SHAPE((4, width + 16, tokens[0].shape[1]), BF16),
        in_specs=[VMEM] * 14,
        out_specs=VMEM,
        cost_estimate=cost(0),
        compiler_params=room(18),
        name="weight_grads",
    )(*tokens, *dquery, sums, context, dresid, dresid_core, other, small)


def solution(mesh):
    ndp, nt = mesh.shape["dp"], mesh.shape["tensor"]
    fine = Mesh(
        mesh.devices.reshape(ndp // 8, 2, 2, 2, nt), ("outer", "y", "x", "core", "tensor")
    )
    DP, AXES = ("outer", "y", "x", "core"), ("outer", "y", "x", "core", "tensor")

    def moved_at(i, t):
        return (i & 1) != (t >> 1)

    def exchange(value, target, only=None):
        pairs = []
        for i in range(ndp):
            for t in range(nt):
                if only is None or only(i, t):
                    j, u = target(i, t)
                    pairs.append((i * nt + t, j * nt + u))
        return lax.ppermute(value, AXES, pairs)

    def swap(value):
        return exchange(value, lambda i, t: (i ^ 1, t ^ 2) if moved_at(i, t) else (i, t))

    def over_core(value):
        return exchange(value, lambda i, t: (i ^ 1, t))

    def over_z(value):
        return exchange(value, lambda i, t: (i, t ^ 1))

    def over_x(value):
        return exchange(value, lambda i, t: (i ^ 2, t))

    def over_y(value):
        return exchange(value, lambda i, t: (i ^ 4, t))

    def shards(
        tokens,
        cotangent,
        segment_ids,
        drop_flags,
        query_weight,
        query_bias,
        key_weight,
        value_weight,
        value_bias,
        out_weight,
        out_bias,
        attn_gain,
        attn_shift,
        up_weight,
        up_bias,
        down_weight,
        down_bias,
        ffn_gain,
        ffn_shift,
    ):
        i, t = lax.axis_index(DP), lax.axis_index("tensor")
        core, zbit, xbit, ybit = i & 1, t & 1, (i >> 1) & 1, (i >> 2) & 1
        moved = core != (t >> 1)
        length = segment_ids.shape[1]
        rows, model = tokens.shape
        width = query_weight.shape[1]
        part = up_weight.shape[1] // 4

        def turned(value, axis, bit):
            return jnp.where(bit == 1, jnp.flip(value, axis), value)

        def over_plane(value):
            copies = jnp.broadcast_to(value[None], (4,) + value.shape)
            return lax.all_to_all(copies, ("y", "x"), split_axis=0, concat_axis=0, tiled=True)

        def absolute(value):
            return turned(turned(value, 0, ybit), 1, xbit)

        token_own = swap(tokens)
        token_z = exchange(tokens, lambda i, t: (i, t ^ 1), lambda i, t: not moved_at(i, t))
        blank = jnp.zeros_like(query_bias)
        biases = jnp.concatenate([query_bias, blank, value_bias, blank])
        extra = jnp.concatenate(
            [jnp.broadcast_to(v[None], (16, model)) for v in (biases, up_bias)], 0
        )
        piece, quarter, local = take(
            jnp.stack([ybit * 2 + xbit, moved.astype(jnp.int32)]),
            (query_weight.T, key_weight.T, value_weight.T),
            extra,
            up_weight,
            down_weight,
        )
        piece = swap(piece)
        notes = jnp.concatenate(
            [segment_ids, jnp.broadcast_to(drop_flags[:, None], (1, 128))], axis=1
        )
        notes_core = over_core(notes)
        token_own, token_z, piece, quarter, out_weight, notes, notes_core = stage(
            token_own, token_z, piece, quarter, out_weight, notes, notes_core
        )
        token_core = over_core(token_own)
        token_zm = exchange(token_own, lambda i, t: (i, t ^ 1), moved_at)
        gathered = over_plane(piece)
        quarter = swap(quarter)
        first_vectors = vectors(out_bias, attn_gain, attn_shift)
        second_vectors = vectors(down_bias, ffn_gain, ffn_shift)
        notes = jnp.where(moved, notes_core, notes)
        shard = 2 * core + zbit
        flags = jnp.stack([moved.astype(jnp.int32), 1 - notes[0, length], xbit, ybit, shard])
        segment = notes[0, :length].reshape(2, 2, length // 4)
        segment = turned(turned(segment, 0, core), 1, zbit)
        segment = jnp.swapaxes(segment, 0, 1).reshape(length)
        marks = (
            *bounds(segment, QUERIES),
            *bounds(segment, KEYS),
            jnp.broadcast_to(segment[None], (8, length)),
            jnp.broadcast_to(segment[:, None], (length, 128)),
        )
        token_zm, token_z, gathered, quarter, out_weight, *rest = stage(
            token_zm,
            token_z,
            gathered,
            quarter,
            out_weight,
            flags,
            first_vectors,
            second_vectors,
            *marks,
        )
        flags, first_vectors, second_vectors, *marks = rest
        token_z = jnp.where(moved, token_zm, token_z)
        token_zc = over_core(token_z)
        group = (token_own, token_core, token_z, token_zc)
        qkv, weights = project(group, gathered)

        qkv, quarter, out_weight = stage(qkv, quarter, out_weight)
        quarter_z = over_z(quarter)
        own_x = exchange(quarter[: 2 * part], lambda i, t: (i ^ 2, t), moved_at)
        own_y = exchange(quarter[: 2 * part], lambda i, t: (i ^ 4, t), moved_at)
        out_own = swap(out_weight)
        half = 2 * rows
        wide_z, context_z, totals_z = attend_forward(qkv, marks, half, half)

        qkv, context_z, quarter_z, own_x, own_y, out_own = stage(
            qkv, context_z, quarter_z, own_x, own_y, out_own
        )
        context_other = over_z(context_z)
        out_other = over_z(out_own)
        units_z = quarter_z[: 2 * part]
        quarter_zy, quarter_zx = over_y(units_z), over_x(units_z)
        own_xy = exchange(own_x, lambda i, t: (i ^ 4, t), moved_at)
        wide_own, context_own, totals_own = attend_forward(qkv, marks, 0, half)

        context_own, context_other, out_other, quarter_zy, quarter_zx, own_xy = stage(
            context_own, context_other, out_other, quarter_zy, quarter_zx, own_xy
        )
        quarter_zxy = over_x(quarter_zy)
        mine, theirs = out_project(context_own, context_other, out_own, out_other)
        theirs = over_core(theirs)
        mine, theirs, cotangent = stage(mine, theirs, cotangent)
        cotangent = swap(cotangent)
        resid, normed, normed_low = rowwise(
            first_norm_kernel,
            "first_norm",
            (F32, F32, BF16),
            (),
            mine,
            theirs,
            token_own,
            first_vectors,
        )
        normed_core = over_core(normed_low)

        normed_low, normed_core, quarter_zxy = stage(normed_low, normed_core, quarter_zxy)
        pieces = (quarter, own_x, own_y, own_xy, quarter_z, quarter_zx, quarter_zy, quarter_zxy)
        hidden, slope, mine, theirs, up_all, down_all = feed_forward(
            flags, normed_low, normed_core, (*pieces, local)
        )
        layer_out, dsummed, dffn, sums_ffn = rowwise(
            second_norm_kernel,
            "second_norm",
            (BF16, F32, BF16, None),
            (flags,),
            mine,
            over_core(theirs),
            normed,
            cotangent,
            token_own,
            second_vectors,
        )
        dffn_core = over_core(dffn)

        dffn, dffn_core, layer_out = stage(dffn, dffn_core, layer_out)
        down_parts = unit_grads(hidden, dffn, dffn_core)
        dffn, dffn_core, *down_parts = stage(dffn, dffn_core, *down_parts)
        down_got = over_x(down_parts[1]), over_y(down_parts[3])
        dpre, mine, theirs, up_bias_grad = hidden_back(dffn, dffn_core, slope, up_all, down_all)
        dpre, theirs = stage(dpre, theirs)
        got = over_core(theirs)
        up_parts = unit_grads(dpre, normed_low, normed_core)
        got, *up_parts = stage(got, *up_parts)
        up_got = over_x(up_parts[1]), over_y(up_parts[3])
        dresid, dresid_low, sums_attn = rowwise(
            first_norm_back_kernel,
            "first_norm_back",
            (F32, BF16, None),
            (),
            mine,
            got,
            dsummed,
            resid,
            first_vectors,
        )
        dresid_core = over_core(dresid_low)
        dresid_low, dresid_core, *down_got = stage(dresid_low, dresid_core, *down_got)
        dcontext_own, dcontext_z, out_grad_z = small_kernel(
            context_back_kernel,
            "context_back",
            (((width, half), BF16), ((width, half), BF16), ((width, model), BF16)),
            (),
            dresid_low,
            dresid_core,
            out_own,
            out_other,
            context_other,
        )

        small = small_kernel(
            gather_small_kernel,
            "gather_small",
            (((16, model), F32),),
            (flags,),
            sums_attn,
            sums_ffn,
            up_bias_grad,
        )[0]
        small_core = over_core(small)

        layer_out = swap(layer_out)
        dcontext_z, dcontext_own, out_grad_z, small, small_core = stage(
            dcontext_z, dcontext_own, out_grad_z, small, small_core
        )
        dcontext_other = over_z(dcontext_z)
        out_grad_other = over_z(out_grad_z)
        small = small + small_core
        around = (dcontext_own, wide_own, totals_own)
        dq_own, sums = attend_backward(qkv, around, marks, 0, 0, rows, None, F32)

        dq_own, sums, layer_out, small, dcontext_other, *up_got = stage(
            dq_own, sums, layer_out, small, dcontext_other, *up_got
        )
        kept_own, send_own, kept_other, send_other = small_kernel(
            fold_plane_kernel,
            "fold_plane",
            (((2 * part, model), F32), ((2 * part, model), BF16)) * 2,
            (),
            up_parts[0],
            up_got[0],
            down_parts[0],
            down_got[0],
            up_parts[2],
            up_got[1],
            down_parts[2],
            down_got[1],
        )
        send_own, send_other = over_y(send_own), over_x(send_other)
        small_z = over_z(small)
        dq_core, sums = attend_backward(qkv, around, marks, rows, rows, rows, sums, F32)

        around = (dcontext_other, wide_z, totals_z)
        dq_z, sums = attend_backward(qkv, around, marks, half, 0, rows, sums, F32)

        dq_z, sums, small, small_z, out_grad_other, send_own, send_other = stage(
            dq_z, sums, small, small_z, out_grad_other, send_own, send_other
        )
        small = small + small_z
        unit_sum, unit_z = small_kernel(
            fold_shards_kernel,
            "fold_shards",
            (((2 * part, model), F32), ((2 * part, model), BF16)),
            (),
            kept_own,
            send_own,
            kept_other,
            send_other,
        )
        unit_z = over_z(unit_z)
        dq_zc, sums = attend_backward(qkv, around, marks, 3 * rows, rows, rows, sums, BF16)

        def home(value):
            kept, send, far = value
            send = exchange(send, lambda i, t: (i, t ^ 2) if moved_at(i, t) else (i ^ 1, t))
            far = exchange(far, lambda i, t: (i ^ 1, t ^ 2), moved_at)
            return kept, send, far

        def outer(value):
            bit = 8
            while bit < ndp:
                value = value + exchange(
                    value.astype(BF16), lambda i, t, bit=bit: (i ^ bit, t)
                ).astype(F32)
                bit *= 2
            return value

        def fold_home(name, value, kind=BF16):
            result = small_kernel(
                fold_home_kernel,
                name,
                ((value[0].shape, kind if ndp == 8 else F32),),
                (flags,),
                *value,
            )[0]
            return outer(result).astype(kind)

        dq_zc, sums = stage(dq_zc, sums)
        input_z, input_zc = input_back(half, dq_z, dq_zc, sums, weights)
        input_z, input_zc, sums, unit_z = stage(input_z, input_zc, sums, unit_z)
        input_zc = over_core(input_zc)
        unit_home = small_kernel(
            fold_z_kernel,
            "fold_z",
            (((part, model), F32), ((part, model), BF16), ((part, model), BF16)),
            (flags,),
            unit_sum,
            unit_z,
        )
        input_z, input_zc, sums, *unit_home = stage(input_z, input_zc, sums, *unit_home)
        unit_home = home(unit_home)
        packed = weight_grads(
            group,
            (dq_own, dq_core, dq_z, dq_zc),
            sums,
            context_own,
            dresid_low,
            dresid_core,
            out_grad_other,
            small,
        )
        packed, input_z, input_zc = stage(packed, input_z, input_zc)
        input_z = small_kernel(
            fold_inputs_kernel, "fold_inputs", (((rows, model), BF16),), (), input_z, input_zc
        )[0]
        input_z, packed = stage(input_z, packed)
        input_other = over_z(input_z)
        parted = lax.all_to_all(packed, ("y", "x"), split_axis=0, concat_axis=0, tiled=True)
        mine, theirs = small_kernel(
            input_own_kernel,
            "input_own",
            (((rows, model), F32), ((rows, model), BF16)),
            (flags,),
            dq_own,
            dq_core,
            sums,
            weights,
            dresid,
            cotangent,
        )
        theirs = over_core(theirs)

        parted, input_other, mine, theirs, *unit_home = stage(
            parted, input_other, mine, theirs, *unit_home
        )
        head_home = small_kernel(
            fold_parts_kernel,
            "fold_parts",
            (
                ((width // 2 + 16, model), F32),
                ((width // 2 + 16, model), BF16),
                ((width // 2 + 16, model), BF16),
            ),
            (flags,),
            parted,
        )
        mine, theirs, input_other, *homes = stage(mine, theirs, input_other, *head_home, *unit_home)
        head_home, unit_home = home(homes[:3]), homes[3:]
        tokens_grad = small_kernel(
            add_tokens_kernel,
            "add_tokens",
            (((rows, model), BF16),),
            (),
            mine,
            theirs,
            input_other,
        )[0]
        tokens_grad, *unit_home = stage(tokens_grad, *unit_home)
        tokens_grad = swap(tokens_grad)
        unit_half = fold_home("fold_units", unit_home)
        unit_all = over_plane(unit_half)

        head_home = stage(*head_home)
        heads = fold_home("fold_heads", head_home, F32)
        heads, unit_all = stage(heads, unit_all)
        head_all = over_plane(heads[: width // 2].astype(BF16))
        small = heads[width // 2 :]
        up_bias_sum = lax.dynamic_slice_in_dim(small[6:10], t, 1, 0)[0]
        unit_other = over_core(unit_all)

        up_sum, down_sum = small_kernel(
            unit_results_kernel,
            "unit_results",
            (((model, 4 * part), F32), ((4 * part, model), F32)),
            (flags,),
            unit_all,
            unit_other,
        )
        head_all, up_sum, down_sum, small, up_bias_sum = stage(
            head_all, up_sum, down_sum, small, up_bias_sum
        )
        head_other = over_core(head_all)
        head_other, tokens_grad = stage(head_other, tokens_grad)
        sums = small_kernel(
            head_results_kernel,
            "head_results",
            (((width, model), F32),) * 4,
            (flags,),
            head_all,
            head_other,
        )
        narrow = small[12, :width], small[12, width : 2 * width]

        return (
            layer_out,
            tokens_grad,
            sums[0].T,
            narrow[0],
            sums[1].T,
            sums[2].T,
            narrow[1],
            sums[3],
            small[0],
            small[1],
            small[2],
            up_sum,
            up_bias_sum,
            down_sum,
            small[3],
            small[4],
            small[5],
        )

    return jax.shard_map(
        shards,
        mesh=fine,
        in_specs=(
            P(AXES, None),
            P(AXES, None),
            P(DP, None),
            P(DP),
            P(None, "tensor"),
            P("tensor"),
            P(None, "tensor"),
            P(None, "tensor"),
            P("tensor"),
            P("tensor", None),
            P(),
            P(),
            P(),
            P(None, "tensor"),
            P("tensor"),
            P("tensor", None),
            P(),
            P(),
            P(),
        ),
        out_specs=(
            P(AXES, None),
            P(AXES, None),
            P(None, "tensor"),
            P("tensor"),
            P(None, "tensor"),
            P(None, "tensor"),
            P("tensor"),
            P("tensor", None),
            P(),
            P(),
            P(),
            P(None, "tensor"),
            P("tensor"),
            P("tensor", None),
            P(),
            P(),
            P(),
        ),
        check_vma=False,
    )
```

```python
import functools

import jax
import jax.numpy as jnp
from jax import lax
from jax.experimental import pallas as pl
from jax.experimental.pallas import tpu as pltpu
from jax.sharding import Mesh
from jax.sharding import PartitionSpec as P

HEAD_DIM = 64
QUERIES, KEYS = 512, 256
EPS = 1e-05
NEG = -1e30
F32 = jnp.float32
BF16 = jnp.bfloat16
SMEM = pl.BlockSpec(memory_space=pltpu.SMEM)
VMEM = pl.BlockSpec(memory_space=pltpu.VMEM)
SHAPE = jax.ShapeDtypeStruct


def matmul(left, right):
    return jnp.dot(left, right, preferred_element_type=F32)


def matmul_left(left, right):
    return lax.dot_general(left, right, (((0,), (0,)), ((), ())), preferred_element_type=F32)


def matmul_right(left, right):
    return lax.dot_general(left, right, (((1,), (1,)), ((), ())), preferred_element_type=F32)


def stage(*values):
    return lax.optimization_barrier(values)


def cost(micros):
    return pl.CostEstimate(flops=int(micros * 1e9), bytes_accessed=1 << 12, transcendentals=0)


def room(mebibytes):
    return pltpu.CompilerParams(vmem_limit_bytes=mebibytes << 20)


def head_parts(width):
    return [slice(h, h + HEAD_DIM) for h in range(0, width, HEAD_DIM)]


def attend_forward_kernel(
    bq,
    bk,
    first,
    qlow_ref,
    qhigh_ref,
    klow_ref,
    khigh_ref,
    qkv_ref,
    row_ref,
    column_ref,
    wide_ref,
    context_ref,
    totals_ref,
    top_ref,
    sum_ref,
    acc_ref,
):
    width, count = wide_ref.shape
    length = qkv_ref.shape[1]
    parts = head_parts(width)
    heads = range(len(parts))
    key_parts = head_parts(2 * width)[len(parts) :]
    value_parts = head_parts(3 * width)[2 * len(parts) :]

    def over_query(i, _):
        at_o = pl.ds(pl.multiple_of(i * bq, bq), bq)
        at_q = pl.ds(pl.multiple_of(first + i * bq, bq), bq)
        block = i + first // bq
        top_ref[...] = jnp.full(top_ref.shape, NEG, F32)
        sum_ref[...] = jnp.zeros(sum_ref.shape, F32)
        acc_ref[...] = jnp.zeros(acc_ref.shape, F32)
        row = row_ref[0:1, at_q]

        def over_keys(j, _):
            @pl.when((klow_ref[j] <= qhigh_ref[block]) & (qlow_ref[block] <= khigh_ref[j]))
            def _():
                at_k = pl.ds(pl.multiple_of(j * bk, bk), bk)
                column = column_ref[at_k, :]
                same = jnp.concatenate([column] * (bq // 128), 1) == row
                scores = [
                    matmul_left(qkv_ref[k, at_k], qkv_ref[q, at_q])
                    for k, q in zip(key_parts, parts)
                ]
                scores = [jnp.where(same, value, NEG) for value in scores]
                old = [top_ref[h : h + 1, :] for h in heads]
                top = [jnp.maximum(o, jnp.max(v, 0, keepdims=True)) for o, v in zip(old, scores)]
                exponent = [jnp.exp(v - m) for v, m in zip(scores, top)]
                scale = [jnp.exp(o - m) for o, m in zip(old, top)]
                total = [
                    sum_ref[h : h + 1, :] * scale[h] + jnp.sum(exponent[h], 0, keepdims=True)
                    for h in heads
                ]
                added = [
                    matmul(qkv_ref[v, at_k], e.astype(BF16)) for v, e in zip(value_parts, exponent)
                ]
                added = [acc_ref[p, :] * c + v for p, c, v in zip(parts, scale, added)]
                for h in heads:
                    top_ref[h : h + 1, :] = top[h]
                    sum_ref[h : h + 1, :] = total[h]
                    acc_ref[parts[h], :] = added[h]

            return 0

        lax.fori_loop(0, length // bk, over_keys, 0)
        for h in heads:
            value = acc_ref[parts[h], :] / sum_ref[h : h + 1, :]
            wide_ref[parts[h], at_o] = value
            context_ref[parts[h], at_o] = value.astype(BF16)
            totals_ref[h : h + 1, at_o] = top_ref[h : h + 1, :] + jnp.log(sum_ref[h : h + 1, :])
        return 0

    lax.fori_loop(0, count // bq, over_query, 0)


def attend_backward_kernel(
    bq,
    bk,
    first,
    base,
    follows,
    qlow_ref,
    qhigh_ref,
    klow_ref,
    khigh_ref,
    qkv_ref,
    dcontext_ref,
    wide_ref,
    totals_ref,
    row_ref,
    column_ref,
    *rest,
):
    if follows:
        before_ref, dquery_ref, sums_ref, delta_ref, dq_ref, dk_ref, dv_ref = rest
    else:
        dquery_ref, sums_ref, delta_ref, dq_ref, dk_ref, dv_ref = rest
    width, count = dquery_ref.shape
    length = qkv_ref.shape[1]
    parts = head_parts(width)
    heads = range(len(parts))
    key_parts = head_parts(2 * width)[len(parts) :]
    value_parts = head_parts(3 * width)[2 * len(parts) :]
    dq_ref[...] = jnp.zeros(dq_ref.shape, F32)
    chunk = slice(base, base + count)
    for h in heads:
        delta_ref[h : h + 1, :] = jnp.sum(
            wide_ref[parts[h], chunk] * dcontext_ref[parts[h], chunk].astype(F32), 0, keepdims=True
        )

    def over_keys(j, _):
        at_k = pl.ds(pl.multiple_of(j * bk, bk), bk)
        if follows:
            dk_ref[...] = before_ref[0:width, at_k]
            dv_ref[...] = before_ref[width : 2 * width, at_k]
        else:
            dk_ref[...] = jnp.zeros(dk_ref.shape, F32)
            dv_ref[...] = jnp.zeros(dv_ref.shape, F32)

        def over_query(i, _):
            block = i + first // bq

            @pl.when((klow_ref[j] <= qhigh_ref[block]) & (qlow_ref[block] <= khigh_ref[j]))
            def _():
                at_o = pl.ds(pl.multiple_of(i * bq, bq), bq)
                at_b = pl.ds(pl.multiple_of(base + i * bq, bq), bq)
                at_q = pl.ds(pl.multiple_of(first + i * bq, bq), bq)
                column = column_ref[at_k, :]
                same = jnp.concatenate([column] * (bq // 128), 1) == row_ref[0:1, at_q]
                scores = [
                    matmul_left(qkv_ref[k, at_k], qkv_ref[q, at_q])
                    for k, q in zip(key_parts, parts)
                ]
                dprobs = [
                    matmul_left(qkv_ref[v, at_k], dcontext_ref[p, at_b])
                    for v, p in zip(value_parts, parts)
                ]
                probs = [
                    jnp.exp(jnp.where(same, scores[h], NEG) - totals_ref[h : h + 1, at_b])
                    for h in heads
                ]
                dscores = [
                    (probs[h] * (dprobs[h] - delta_ref[h : h + 1, at_o])).astype(BF16)
                    for h in heads
                ]
                dv = [
                    matmul_right(dcontext_ref[p, at_b], v.astype(BF16)) for p, v in zip(parts, probs)
                ]
                dk = [matmul_right(qkv_ref[p, at_q], v) for p, v in zip(parts, dscores)]
                dq = [matmul(qkv_ref[k, at_k], v) for k, v in zip(key_parts, dscores)]
                for h in heads:
                    dv_ref[parts[h], :] += dv[h]
                    dk_ref[parts[h], :] += dk[h]
                    dq_ref[parts[h], at_o] += dq[h]

            return 0

        lax.fori_loop(0, count // bq, over_query, 0)
        sums_ref[0:width, at_k] = dk_ref[...].astype(sums_ref.dtype)
        sums_ref[width : 2 * width, at_k] = dv_ref[...].astype(sums_ref.dtype)
        return 0

    lax.fori_loop(0, length // bk, over_keys, 0)
    dquery_ref[...] = dq_ref[...].astype(BF16)


def bounds(segment, block):
    blocks = segment.reshape(-1, block)
    return jnp.min(blocks, 1), jnp.max(blocks, 1)


def attend_forward(qkv, marks, first, count):
    width = qkv.shape[0] // 3
    wide_low, wide_high, low, high, row, column = marks
    bq, bk = QUERIES, KEYS
    return pl.pallas_call(
        functools.partial(attend_forward_kernel, bq, bk, first),
        out_shape=(SHAPE((width, count), F32), SHAPE((width, count), BF16), SHAPE((8, count), F32)),
        in_specs=[SMEM] * 4 + [VMEM] * 3,
        out_specs=(VMEM,) * 3,
        scratch_shapes=[pltpu.VMEM((8, bq), F32)] * 2 + [pltpu.VMEM((width, bq), F32)],
        cost_estimate=cost(15),
        compiler_params=room(16),
        name="attend_forward",
    )(wide_low, wide_high, low, high, qkv, row, column)


def attend_backward(qkv, around, marks, first, base, count, before, kind):
    dcontext, wide, totals = around
    width, length = dcontext.shape[0], qkv.shape[1]
    _, _, low, high, row, column = marks
    bq = bk = KEYS
    follows = before is not None
    return pl.pallas_call(
        functools.partial(attend_backward_kernel, bq, bk, first, base, follows),
        out_shape=(SHAPE((width, count), BF16), SHAPE((2 * width, length), kind)),
        in_specs=[SMEM] * 4 + [VMEM] * (7 if follows else 6),
        out_specs=(VMEM,) * 2,
        scratch_shapes=[
            pltpu.VMEM((8, count), F32),
            pltpu.VMEM((width, count), F32),
            pltpu.VMEM((width, bk), F32),
            pltpu.VMEM((width, bk), F32),
        ],
        cost_estimate=cost(count // 64),
        compiler_params=room(22),
        name="attend_backward",
    )(
        low,
        high,
        low,
        high,
        qkv,
        dcontext,
        wide,
        totals,
        row,
        column,
        *((before,) if follows else ()),
    )


def plane_slots(flags_ref, slots):
    slots = [jnp.where(flags_ref[2] == 1, slots[k ^ 1], slots[k]) for k in range(4)]
    return [jnp.where(flags_ref[3] == 1, slots[k ^ 2], slots[k]) for k in range(4)]


def feed_forward_kernel(flags_ref, own_ref, core_ref, *rest):
    pieces, (hidden_ref, slope_ref, mine_ref, other_ref, up_ref, down_ref) = rest[:-6], rest[-6:]
    rows, cols = own_ref.shape[0], 256
    part = up_ref.shape[0] // 8
    for n in range(2):
        for k in range(4):
            to = slice((2 * k + n) * part, (2 * k + n + 1) * part)
            up, down = pieces[4 * n + k][0:part, :], pieces[4 * n + k][part : 2 * part, :]
            if n == 0 and k > 0:
                up = up + pieces[8][k - 1, 0:part, :]
                down = down + pieces[8][k - 1, part : 2 * part, :]
            up_ref[to, :] = up
            down_ref[to, :] = down
    biases = []
    for n in range(2):
        value = pieces[4 * n][2 * part : 2 * part + 16, :].astype(F32)[0:1]
        biases.append(plane_slots(flags_ref, [value[:, k * part : (k + 1) * part] for k in range(4)]))
    biases = jnp.concatenate([biases[n][k] for k in range(4) for n in range(2)], 1)
    for source, target, start in ((core_ref, other_ref, rows), (own_ref, mine_ref, 0)):
        at = slice(start, start + rows)
        value = source[...]
        for n in range(0, up_ref.shape[0], cols):
            to = slice(n, n + cols)
            pre = matmul_right(value, up_ref[to, :]) + biases[:, to]
            normal = 0.5 * (1.0 + lax.erf(pre * 0.7071067811865476))
            hidden_ref[at, to] = (pre * normal).astype(BF16)
            density = jnp.exp(-0.5 * pre * pre) * 0.3989422804014327
            slope_ref[at, to] = (normal + pre * density).astype(BF16)
        target[...] = matmul(hidden_ref[at, :], down_ref[...]).astype(target.dtype)


def feed_forward(flags, own, core, pieces):
    rows, model = own.shape
    units = 2 * model
    return pl.pallas_call(
        feed_forward_kernel,
        out_shape=(
            SHAPE((2 * rows, units), BF16),
            SHAPE((2 * rows, units), BF16),
            SHAPE((rows, model), F32),
            SHAPE((rows, model), BF16),
            SHAPE((units, model), BF16),
            SHAPE((units, model), BF16),
        ),
        in_specs=[SMEM] + [VMEM] * 11,
        out_specs=(VMEM,) * 6,
        cost_estimate=cost(12),
        compiler_params=room(32),
        name="feed_forward",
    )(flags, own, core, *pieces)


def hidden_back_kernel(
    own_ref, core_ref, slope_ref, up_ref, down_ref, dpre_ref, mine_ref, other_ref, bias_ref
):
    rows, cols = own_ref.shape[0], 256
    for source, target, start in ((core_ref, other_ref, rows), (own_ref, mine_ref, 0)):
        at = slice(start, start + rows)
        value = source[...]
        for n in range(0, up_ref.shape[0], cols):
            to = slice(n, n + cols)
            dhidden = matmul_right(value, down_ref[to, :])
            dpre_ref[at, to] = (dhidden * slope_ref[at, to].astype(F32)).astype(BF16)
        target[...] = matmul(dpre_ref[at, :], up_ref[...]).astype(target.dtype)
    bias_ref[...] = matmul(jnp.ones((8, 2 * rows), BF16), dpre_ref[...])


def hidden_back(own, core, slope, up, down):
    rows, model = own.shape
    units = up.shape[0]
    return pl.pallas_call(
        hidden_back_kernel,
        out_shape=(
            SHAPE((2 * rows, units), BF16),
            SHAPE((rows, model), F32),
            SHAPE((rows, model), BF16),
            SHAPE((8, units), F32),
        ),
        in_specs=[VMEM] * 5,
        out_specs=(VMEM,) * 4,
        cost_estimate=cost(0),
        compiler_params=room(26),
        name="hidden_back",
    )(own, core, slope, up, down)


def unit_grads_kernel(
    dpre_ref, normed_ref, normed_core_ref, hidden_ref, dffn_ref, dffn_core_ref, *refs
):
    rows = normed_ref.shape[0]
    part = dpre_ref.shape[1] // 8
    places = ((0, 0), (1, 0), (0, 1), (1, 1)), ((0, 0), (0, 1), (1, 0), (1, 1))
    halves = (dpre_ref, normed_ref, normed_core_ref), (hidden_ref, dffn_ref, dffn_core_ref)
    for m, (left_ref, own_ref, core_ref) in enumerate(halves):
        for k in range(4):
            at = slice(2 * k * part, 2 * (k + 1) * part)
            total = matmul_left(left_ref[0:rows, at], own_ref[...])
            total = total + matmul_left(left_ref[rows : 2 * rows, at], core_ref[...])
            for n in range(2):
                sent, slot = places[n][k]
                to = slice((2 * m + slot) * part, (2 * m + slot + 1) * part)
                refs[2 * n + sent][to, :] = total[n * part : (n + 1) * part].astype(BF16)


def unit_grads(dpre, normed, normed_core, hidden, dffn, dffn_core):
    return pl.pallas_call(
        unit_grads_kernel,
        out_shape=(SHAPE((dpre.shape[1] // 2, normed.shape[1]), BF16),) * 4,
        in_specs=[VMEM] * 6,
        out_specs=(VMEM,) * 4,
        cost_estimate=cost(5),
        compiler_params=room(24),
        name="unit_grads",
    )(dpre, normed, normed_core, hidden, dffn, dffn_core)


def out_project_kernel(own_ref, other_ref, own_w_ref, other_w_ref, mine_ref, theirs_ref):
    rows = mine_ref.shape[0]
    for target, at in ((theirs_ref, slice(rows, 2 * rows)), (mine_ref, slice(0, rows))):
        value = matmul_left(own_ref[:, at], own_w_ref[...])
        value = value + matmul_left(other_ref[:, at], other_w_ref[...])
        target[...] = value.astype(target.dtype)


def out_project(own, other, own_weight, other_weight):
    rows, model = own.shape[1] // 2, own_weight.shape[1]
    return pl.pallas_call(
        out_project_kernel,
        out_shape=(SHAPE((rows, model), F32), SHAPE((rows, model), BF16)),
        in_specs=[VMEM] * 4,
        out_specs=(VMEM,) * 2,
        cost_estimate=cost(3),
        compiler_params=room(12),
        name="out_project",
    )(own, other, own_weight, other_weight)


def input_back_kernel(start, first_ref, second_ref, sums_ref, weights_ref, mine_ref, theirs_ref):
    rows = first_ref.shape[1]
    width = first_ref.shape[0]
    query_weights = weights_ref[0:width, :] * 0.125
    for k, ref, target in ((1, second_ref, theirs_ref), (0, first_ref, mine_ref)):
        at = slice(start + k * rows, start + (k + 1) * rows)
        value = matmul_left(ref[...], query_weights)
        value = value + matmul_left(sums_ref[:, at], weights_ref[width:, :])
        target[...] = value.astype(target.dtype)


def input_back(start, first, second, sums, weights):
    shape = (first.shape[1], weights.shape[1])
    return pl.pallas_call(
        functools.partial(input_back_kernel, start),
        out_shape=(SHAPE(shape, F32), SHAPE(shape, BF16)),
        in_specs=[VMEM] * 4,
        out_specs=(VMEM,) * 2,
        cost_estimate=cost(0),
        compiler_params=room(14),
        name="input_back",
    )(first, second, sums, weights)


def input_own_kernel(
    flags_ref,
    first_ref,
    second_ref,
    sums_ref,
    weights_ref,
    dresid_ref,
    cotangent_ref,
    mine_ref,
    theirs_ref,
):
    width, rows = first_ref.shape
    query_weights = weights_ref[0:width, :] * 0.125
    for k, ref in ((1, second_ref), (0, first_ref)):
        at = slice(k * rows, (k + 1) * rows)
        value = matmul_left(ref[...], query_weights)
        value = value + matmul_left(sums_ref[:, at], weights_ref[width:, :])
        if k == 1:
            theirs_ref[...] = value.astype(BF16)
        else:
            skipped = (1 - flags_ref[1]).astype(F32)
            mine_ref[...] = value + dresid_ref[...] + skipped * cotangent_ref[...].astype(F32)


def context_back_kernel(
    own_ref,
    core_ref,
    small_ref,
    own_w_ref,
    other_w_ref,
    context_ref,
    mine_ref,
    theirs_ref,
    grad_ref,
    sum_ref,
):
    rows = own_ref.shape[0] - 16
    width = mine_ref.shape[0]
    grad = 0.0
    for k, ref in enumerate((own_ref, core_ref)):
        at = slice(k * rows, (k + 1) * rows)
        value = ref[0:rows, :]
        theirs_ref[:, at] = matmul_right(other_w_ref[...], value).astype(BF16)
        mine_ref[:, at] = matmul_right(own_w_ref[...], value).astype(BF16)
        grad = grad + matmul(context_ref[:, at], value)
    grad_ref[0:width, :] = grad.astype(BF16)
    total = small_ref[...] + core_ref[rows : rows + 16, :].astype(F32)
    sum_ref[...] = total
    grad_ref[width : width + 16, :] = total.astype(BF16)


def take_kernel(
    flags_ref,
    query_ref,
    key_ref,
    value_ref,
    extra_ref,
    up_ref,
    down_ref,
    piece_ref,
    quarter_ref,
    local_ref,
    turned_ref,
):
    place = flags_ref[0]
    held = 1.0 - flags_ref[1].astype(F32)
    fourth = query_ref.shape[0] // 4
    for n, ref in enumerate((query_ref, key_ref, value_ref)):
        at = pl.ds(pl.multiple_of(place * fourth, fourth), fourth)
        piece_ref[n * fourth : (n + 1) * fourth, :] = ref[at, :]
    piece_ref[3 * fourth :, :] = extra_ref[0:16, :]
    turned_ref[...] = up_ref[...].T
    part = local_ref.shape[1] // 2
    quarter_ref[2 * part :, :] = extra_ref[16:32, :]
    for k in range(4):
        at = pl.ds(pl.multiple_of((place ^ k) * part, part), part)
        if k == 0:
            quarter_ref[0:part, :] = turned_ref[at, :]
            quarter_ref[part : 2 * part, :] = down_ref[at, :]
        else:
            local_ref[k - 1, 0:part, :] = (turned_ref[at, :] * held).astype(BF16)
            local_ref[k - 1, part : 2 * part, :] = (down_ref[at, :] * held).astype(BF16)


def take(place, heads, extra, up, down):
    units, model = down.shape
    rows = heads[0].shape[0] // 4 * 3 + 16
    return pl.pallas_call(
        take_kernel,
        out_shape=(
            SHAPE((rows, model), BF16),
            SHAPE((units // 2 + 16, model), BF16),
            SHAPE((3, units // 2, model), BF16),
        ),
        in_specs=[SMEM] + [VMEM] * 6,
        out_specs=(VMEM,) * 3,
        scratch_shapes=[pltpu.VMEM((units, model), BF16)],
        cost_estimate=cost(20),
        compiler_params=room(14),
        name="take",
    )(place, *heads, extra, up, down)


def small_kernel(kernel, name, results, flags, *operands, mebibytes=16):
    return pl.pallas_call(
        kernel,
        out_shape=tuple(SHAPE(shape, kind) for shape, kind in results),
        in_specs=[SMEM] * len(flags) + [VMEM] * len(operands),
        out_specs=(VMEM,) * len(results),
        cost_estimate=cost(0),
        compiler_params=room(mebibytes),
        name=name,
    )(*flags, *operands)


def fold_plane_kernel(*refs):
    part = refs[0].shape[0] // 4
    for n in range(2):
        keep_ref, got_ref = refs[2 * n], refs[2 * n + 1]
        kept_ref, send_ref = refs[4 + 2 * n], refs[5 + 2 * n]
        for m in range(2):
            at = slice(m * part, (m + 1) * part)
            kept, sent = (
                keep_ref[k * part : (k + 1) * part, :].astype(F32)
                + got_ref[k * part : (k + 1) * part, :].astype(F32)
                for k in (2 * m, 2 * m + 1)
            )
            kept_ref[at, :] = kept
            send_ref[at, :] = sent.astype(BF16)


def fold_shards_kernel(own_ref, own_got_ref, other_ref, other_got_ref, sum_ref, send_ref):
    sum_ref[...] = own_ref[...] + own_got_ref[...].astype(F32)
    send_ref[...] = (other_ref[...] + other_got_ref[...].astype(F32)).astype(BF16)


def split_home(flags_ref, value, kept_ref, send_ref, far_ref):
    half = kept_ref.shape[0]
    kept_ref[...] = value[:half]
    far_ref[...] = value[half:].astype(BF16)

    @pl.when(flags_ref[0] == 1)
    def _():
        send_ref[...] = value[:half].astype(BF16)

    @pl.when(flags_ref[0] == 0)
    def _():
        send_ref[...] = value[half:].astype(BF16)


def fold_z_kernel(flags_ref, sum_ref, got_ref, kept_ref, send_ref, far_ref):
    split_home(flags_ref, sum_ref[...] + got_ref[...].astype(F32), kept_ref, send_ref, far_ref)


def fold_parts_kernel(flags_ref, parts_ref, kept_ref, send_ref, far_ref):
    value = parts_ref[0].astype(F32) + parts_ref[1].astype(F32)
    value = value + (parts_ref[2].astype(F32) + parts_ref[3].astype(F32))
    half = kept_ref.shape[0] - 16
    tail = value[2 * half :]
    kept_ref[0:half, :] = value[:half]
    kept_ref[half:, :] = tail
    far_ref[0:half, :] = value[half : 2 * half].astype(BF16)
    far_ref[half:, :] = tail.astype(BF16)
    send_ref[half:, :] = tail.astype(BF16)

    @pl.when(flags_ref[0] == 1)
    def _():
        send_ref[0:half, :] = value[:half].astype(BF16)

    @pl.when(flags_ref[0] == 0)
    def _():
        send_ref[0:half, :] = value[half : 2 * half].astype(BF16)


def fold_inputs_kernel(mine_ref, theirs_ref, result_ref):
    result_ref[...] = (mine_ref[...] + theirs_ref[...].astype(F32)).astype(BF16)


def add_tokens_kernel(mine_ref, theirs_ref, other_ref, result_ref):
    other = theirs_ref[...].astype(F32) + other_ref[...].astype(F32)
    result_ref[...] = (mine_ref[...] + other).astype(BF16)


def fold_home_kernel(flags_ref, kept_ref, got_ref, far_ref, result_ref):
    got = got_ref[...].astype(F32)
    first = jnp.where(flags_ref[0] == 1, far_ref[...].astype(F32), kept_ref[...])
    result_ref[...] = (first + got).astype(result_ref.dtype)


def unit_results_kernel(flags_ref, mine_ref, other_ref, up_ref, down_ref):
    def put(first_ref, second_ref):
        part = first_ref.shape[1]
        for k in range(4):
            down_ref[k * part : (k + 1) * part, :] = second_ref[k].astype(F32)
        up_ref[...] = first_ref[...].reshape(4 * part, first_ref.shape[2]).astype(F32).T

    @pl.when(flags_ref[0] == 1)
    def _():
        put(other_ref, mine_ref)

    @pl.when(flags_ref[0] == 0)
    def _():
        put(mine_ref, other_ref)


def head_results_kernel(flags_ref, mine_ref, other_ref, *results):
    half = mine_ref.shape[1]
    for k, ref in enumerate(results):
        mine, other = mine_ref[k].astype(F32), other_ref[k].astype(F32)
        ref[0:half, :] = jnp.where(flags_ref[0] == 1, other, mine)
        ref[half : 2 * half, :] = jnp.where(flags_ref[0] == 1, mine, other)


def normal_rows(value):
    center = value - jnp.mean(value, -1, keepdims=True)
    root = lax.rsqrt(jnp.mean(center * center, -1, keepdims=True) + EPS)
    return center * root, root


def normal_back(grad, normal, root):
    inner = jnp.mean(grad * normal, -1, keepdims=True)
    return root * (grad - jnp.mean(grad, -1, keepdims=True) - normal * inner)


STEP = 128


def first_norm_kernel(mine_ref, got_ref, token_ref, vector_ref, resid_ref, normed_ref, low_ref):
    def step(k, _):
        at = pl.ds(pl.multiple_of(k * STEP, STEP), STEP)
        attention = mine_ref[at, :] + got_ref[at, :].astype(F32)
        resid = token_ref[at, :].astype(F32) + attention + vector_ref[0:1, :]
        resid_ref[at, :] = resid
        normed = normal_rows(resid)[0] * vector_ref[1:2, :] + vector_ref[2:3, :]
        normed_ref[at, :] = normed
        low_ref[at, :] = normed.astype(BF16)
        return 0

    lax.fori_loop(0, mine_ref.shape[0] // STEP, step, 0)


def second_norm_kernel(
    flags_ref,
    mine_ref,
    got_ref,
    normed_ref,
    cotangent_ref,
    token_ref,
    vector_ref,
    layer_ref,
    dsummed_ref,
    low_ref,
    sums_ref,
):
    keep = flags_ref[1].astype(F32)
    sums_ref[...] = jnp.zeros(sums_ref.shape, F32)

    def step(k, _):
        at = pl.ds(pl.multiple_of(k * STEP, STEP), STEP)
        units = mine_ref[at, :] + got_ref[at, :].astype(F32)
        normal, root = normal_rows(normed_ref[at, :] + units + vector_ref[0:1, :])
        final = normal * vector_ref[1:2, :] + vector_ref[2:3, :]
        token = token_ref[at, :].astype(F32)
        layer_ref[at, :] = (keep * final + (1.0 - keep) * token).astype(BF16)
        cotangent = cotangent_ref[at, :].astype(F32)
        dfinal = keep * cotangent
        dsummed = normal_back(dfinal * vector_ref[1:2, :], normal, root)
        dsummed_ref[at, :] = dsummed
        low_ref[at, :] = dsummed.astype(BF16)
        sums_ref[0:1, :] += jnp.sum(dsummed, 0, keepdims=True)
        sums_ref[1:2, :] += jnp.sum(dfinal * normal, 0, keepdims=True)
        sums_ref[2:3, :] += jnp.sum(dfinal, 0, keepdims=True)
        return 0

    lax.fori_loop(0, mine_ref.shape[0] // STEP, step, 0)


def first_norm_back_kernel(
    flags_ref,
    mine_ref,
    got_ref,
    dsummed_ref,
    resid_ref,
    vector_ref,
    ffn_ref,
    bias_ref,
    dresid_ref,
    low_ref,
    small_ref,
):
    rows, model = mine_ref.shape
    part = model // 4
    small_ref[...] = jnp.zeros(small_ref.shape, F32)

    def step(k, _):
        at = pl.ds(pl.multiple_of(k * STEP, STEP), STEP)
        dnormed = dsummed_ref[at, :] + (mine_ref[at, :] + got_ref[at, :].astype(F32))
        normal, root = normal_rows(resid_ref[at, :])
        dresid = normal_back(dnormed * vector_ref[1:2, :], normal, root)
        dresid_ref[at, :] = dresid
        low_ref[at, :] = dresid.astype(BF16)
        small_ref[0:1, :] += jnp.sum(dresid, 0, keepdims=True)
        small_ref[1:2, :] += jnp.sum(dnormed * normal, 0, keepdims=True)
        small_ref[2:3, :] += jnp.sum(dnormed, 0, keepdims=True)
        return 0

    lax.fori_loop(0, rows // STEP, step, 0)
    small_ref[3:6, :] = ffn_ref[0:3, :]
    wide = 0.0
    for n in range(2):
        slots = [bias_ref[0:1, (2 * k + n) * part : (2 * k + n + 1) * part] for k in range(4)]
        value = jnp.concatenate(plane_slots(flags_ref, slots), 1)
        at = lax.broadcasted_iota(jnp.int32, (4, model), 0) == (flags_ref[4] ^ n)
        wide = wide + jnp.where(at, value, 0.0)
    small_ref[6:10, :] = wide
    low_ref[rows : rows + 16, :] = small_ref[...].astype(BF16)


def vectors(bias, gain, shift):
    return jnp.concatenate([jnp.stack([bias, gain, shift]), jnp.zeros((5,) + bias.shape)]).astype(F32)


def rowwise(kernel, name, kinds, flags, *operands):
    shape = operands[0].shape
    results = tuple(SHAPE(shape if kind else (8, shape[1]), kind or F32) for kind in kinds)
    return pl.pallas_call(
        kernel,
        out_shape=results,
        in_specs=[SMEM] * len(flags) + [VMEM] * len(operands),
        out_specs=(VMEM,) * len(results),
        cost_estimate=cost(2),
        compiler_params=room(16),
        name=name,
    )(*flags, *operands)


def project_kernel(own_ref, core_ref, z_ref, zc_ref, gathered_ref, qkv_ref, weights_ref):
    rows = own_ref.shape[0]
    fourth = weights_ref.shape[0] // 4
    width = weights_ref.shape[0] // 3
    for k in range(4):
        for n in range(3):
            piece = fourth // 3
            to = slice(n * width + k * piece, n * width + (k + 1) * piece)
            weights_ref[to, :] = gathered_ref[k, n * piece : (n + 1) * piece, :]
    weights = weights_ref[...]
    biases = gathered_ref[0, fourth : fourth + 16, 0 : 3 * width]
    first = lax.broadcasted_iota(jnp.int32, (16, rows), 0) == 0
    columns = matmul_left(biases, jnp.where(first, 1.0, 0.0).astype(BF16))
    for k, ref in enumerate((own_ref, core_ref, z_ref, zc_ref)):
        at = slice(k * rows, (k + 1) * rows)
        value = matmul_right(weights, ref[...]) + columns
        qkv_ref[0:width, at] = (value[:width] * 0.125).astype(BF16)
        qkv_ref[width:, at] = value[width:].astype(BF16)


def project(tokens, gathered):
    rows, model = tokens[0].shape
    units = 4 * (gathered.shape[1] - 16)
    return pl.pallas_call(
        project_kernel,
        out_shape=(SHAPE((units, 4 * rows), BF16), SHAPE((units, model), BF16)),
        in_specs=[VMEM] * 5,
        out_specs=(VMEM,) * 2,
        cost_estimate=cost(4),
        compiler_params=room(20),
        name="project",
    )(*tokens, gathered)


def weight_grads_kernel(
    own_ref,
    core_ref,
    z_ref,
    zc_ref,
    dq_own_ref,
    dq_core_ref,
    dq_z_ref,
    dq_zc_ref,
    sums_ref,
    context_ref,
    dresid_ref,
    dresid_core_ref,
    other_ref,
    small_ref,
    packed_ref,
):
    rows = own_ref.shape[0]
    width = dq_own_ref.shape[0]
    tokens = (own_ref, core_ref, z_ref, zc_ref)
    dquery = (dq_own_ref, dq_core_ref, dq_z_ref, dq_zc_ref)
    total, query, bias = 0.0, 0.0, 0.0
    count = jnp.ones((8, rows), BF16)
    for k in range(4):
        value = tokens[k][...]
        query = query + matmul(dquery[k][...], value)
        total = total + matmul(sums_ref[:, k * rows : (k + 1) * rows], value)
        bias = bias + matmul_right(count, dquery[k][...])
    packed_ref[0, 0:width, :] = (query * 0.125).astype(BF16)
    packed_ref[1, 0:width, :] = total[:width].astype(BF16)
    packed_ref[2, 0:width, :] = total[width:].astype(BF16)
    out = matmul(context_ref[:, 0:rows], dresid_ref[0:rows, :])
    out = out + matmul(context_ref[:, rows : 2 * rows], dresid_core_ref[0:rows, :])
    packed_ref[3, 0:width, :] = (out + other_ref[0:width, :].astype(F32)).astype(BF16)
    small = small_ref[...] + other_ref[width : width + 16, :].astype(F32)
    count = jnp.ones((8, 4 * rows), BF16)
    values = matmul_right(count, sums_ref[width : 2 * width, :])
    biases = jnp.concatenate([bias * 0.125, values, jnp.zeros_like(bias), jnp.zeros_like(bias)], 1)
    at_row = lax.broadcasted_iota(jnp.int32, (8, 4 * width), 0) == 4
    late = jnp.where(at_row, biases, small[8:16])
    tail = jnp.concatenate([small[0:8], late], 0).astype(BF16)
    for k in range(4):
        packed_ref[k, width : width + 16, :] = tail


def weight_grads(tokens, dquery, sums, context, dresid, dresid_core, other, small):
    width = dquery[0].shape[0]
    return pl.pallas_call(
        weight_grads_kernel,
        out_shape=SHAPE((4, width + 16, tokens[0].shape[1]), BF16),
        in_specs=[VMEM] * 14,
        out_specs=VMEM,
        cost_estimate=cost(8),
        compiler_params=room(18),
        name="weight_grads",
    )(*tokens, *dquery, sums, context, dresid, dresid_core, other, small)


def solution(mesh):
    ndp, nt = mesh.shape["dp"], mesh.shape["tensor"]
    fine = Mesh(
        mesh.devices.reshape(ndp // 8, 2, 2, 2, nt), ("outer", "y", "x", "core", "tensor")
    )
    DP, AXES = ("outer", "y", "x", "core"), ("outer", "y", "x", "core", "tensor")

    def moved_at(i, t):
        return (i & 1) != (t >> 1)

    def exchange(value, target, only=None):
        pairs = []
        for i in range(ndp):
            for t in range(nt):
                if only is None or only(i, t):
                    j, u = target(i, t)
                    pairs.append((i * nt + t, j * nt + u))
        return lax.ppermute(value, AXES, pairs)

    def swap(value):
        return exchange(value, lambda i, t: (i ^ 1, t ^ 2) if moved_at(i, t) else (i, t))

    def over_core(value):
        return exchange(value, lambda i, t: (i ^ 1, t))

    def over_z(value):
        return exchange(value, lambda i, t: (i, t ^ 1))

    def over_x(value):
        return exchange(value, lambda i, t: (i ^ 2, t))

    def over_y(value):
        return exchange(value, lambda i, t: (i ^ 4, t))

    def shards(
        tokens,
        cotangent,
        segment_ids,
        drop_flags,
        query_weight,
        query_bias,
        key_weight,
        value_weight,
        value_bias,
        out_weight,
        out_bias,
        attn_gain,
        attn_shift,
        up_weight,
        up_bias,
        down_weight,
        down_bias,
        ffn_gain,
        ffn_shift,
    ):
        i, t = lax.axis_index(DP), lax.axis_index("tensor")
        core, zbit, xbit, ybit = i & 1, t & 1, (i >> 1) & 1, (i >> 2) & 1
        moved = core != (t >> 1)
        length = segment_ids.shape[1]
        rows, model = tokens.shape
        width = query_weight.shape[1]
        part = up_weight.shape[1] // 4

        def turned(value, axis, bit):
            return jnp.where(bit == 1, jnp.flip(value, axis), value)

        def over_plane(value):
            copies = jnp.broadcast_to(value[None], (4,) + value.shape)
            return lax.all_to_all(copies, ("y", "x"), split_axis=0, concat_axis=0, tiled=True)

        def absolute(value):
            return turned(turned(value, 0, ybit), 1, xbit)

        token_own = swap(tokens)
        token_z = exchange(tokens, lambda i, t: (i, t ^ 1), lambda i, t: not moved_at(i, t))
        blank = jnp.zeros_like(query_bias)
        biases = jnp.concatenate([query_bias, blank, value_bias, blank])
        extra = jnp.concatenate(
            [jnp.broadcast_to(v[None], (16, model)) for v in (biases, up_bias)], 0
        )
        piece, quarter, local = take(
            jnp.stack([ybit * 2 + xbit, moved.astype(jnp.int32)]),
            (query_weight.T, key_weight.T, value_weight.T),
            extra,
            up_weight,
            down_weight,
        )
        piece = swap(piece)
        notes = jnp.concatenate(
            [segment_ids, jnp.broadcast_to(drop_flags[:, None], (1, 128))], axis=1
        )
        notes_core = over_core(notes)
        token_own, token_z, piece, quarter, out_weight, notes, notes_core = stage(
            token_own, token_z, piece, quarter, out_weight, notes, notes_core
        )
        token_core = over_core(token_own)
        token_zm = exchange(token_own, lambda i, t: (i, t ^ 1), moved_at)
        gathered = over_plane(piece)
        quarter = swap(quarter)
        first_vectors = vectors(out_bias, attn_gain, attn_shift)
        second_vectors = vectors(down_bias, ffn_gain, ffn_shift)
        notes = jnp.where(moved, notes_core, notes)
        shard = 2 * core + zbit
        flags = jnp.stack([moved.astype(jnp.int32), 1 - notes[0, length], xbit, ybit, shard])
        segment = notes[0, :length].reshape(2, 2, length // 4)
        segment = turned(turned(segment, 0, core), 1, zbit)
        segment = jnp.swapaxes(segment, 0, 1).reshape(length)
        marks = (
            *bounds(segment, QUERIES),
            *bounds(segment, KEYS),
            jnp.broadcast_to(segment[None], (8, length)),
            jnp.broadcast_to(segment[:, None], (length, 128)),
        )
        token_zm, token_z, gathered, quarter, out_weight, *rest = stage(
            token_zm,
            token_z,
            gathered,
            quarter,
            out_weight,
            flags,
            first_vectors,
            second_vectors,
            *marks,
        )
        flags, first_vectors, second_vectors, *marks = rest
        token_z = jnp.where(moved, token_zm, token_z)
        token_zc = over_core(token_z)
        group = (token_own, token_core, token_z, token_zc)
        qkv, weights = project(group, gathered)

        qkv, quarter, out_weight = stage(qkv, quarter, out_weight)
        quarter_z = over_z(quarter)
        own_x = exchange(quarter[: 2 * part], lambda i, t: (i ^ 2, t), moved_at)
        own_y = exchange(quarter[: 2 * part], lambda i, t: (i ^ 4, t), moved_at)
        out_own = swap(out_weight)
        half = 2 * rows
        wide_z, context_z, totals_z = attend_forward(qkv, marks, half, half)

        qkv, context_z, quarter_z, own_x, own_y, out_own = stage(
            qkv, context_z, quarter_z, own_x, own_y, out_own
        )
        context_other = over_z(context_z)
        out_other = over_z(out_own)
        units_z = quarter_z[: 2 * part]
        quarter_zy, quarter_zx = over_y(units_z), over_x(units_z)
        own_xy = exchange(own_x, lambda i, t: (i ^ 4, t), moved_at)
        wide_own, context_own, totals_own = attend_forward(qkv, marks, 0, half)

        context_own, context_other, out_other, quarter_zy, quarter_zx, own_xy = stage(
            context_own, context_other, out_other, quarter_zy, quarter_zx, own_xy
        )
        quarter_zxy = over_x(quarter_zy)
        mine, theirs = out_project(context_own, context_other, out_own, out_other)
        theirs = over_core(theirs)
        mine, theirs, cotangent = stage(mine, theirs, cotangent)
        cotangent = swap(cotangent)
        resid, normed, normed_low = rowwise(
            first_norm_kernel,
            "first_norm",
            (F32, F32, BF16),
            (),
            mine,
            theirs,
            token_own,
            first_vectors,
        )
        normed_core = over_core(normed_low)

        normed_low, normed_core, quarter_zxy = stage(normed_low, normed_core, quarter_zxy)
        pieces = (quarter, own_x, own_y, own_xy, quarter_z, quarter_zx, quarter_zy, quarter_zxy)
        hidden, slope, mine, theirs, up_all, down_all = feed_forward(
            flags, normed_low, normed_core, (*pieces, local)
        )
        layer_out, dsummed, dffn, sums_ffn = rowwise(
            second_norm_kernel,
            "second_norm",
            (BF16, F32, BF16, None),
            (flags,),
            mine,
            over_core(theirs),
            normed,
            cotangent,
            token_own,
            second_vectors,
        )
        dffn_core = over_core(dffn)

        dffn, dffn_core, layer_out = stage(dffn, dffn_core, layer_out)
        dpre, mine, theirs, up_bias_grad = hidden_back(dffn, dffn_core, slope, up_all, down_all)
        dpre, theirs = stage(dpre, theirs)
        got = over_core(theirs)
        parts = unit_grads(dpre, normed_low, normed_core, hidden, dffn, dffn_core)
        got, *parts = stage(got, *parts)
        plane_got = over_x(parts[1]), over_y(parts[3])
        dresid, dresid_low, small = small_kernel(
            first_norm_back_kernel,
            "first_norm_back",
            (((rows, model), F32), ((rows + 16, model), BF16), ((16, model), F32)),
            (flags,),
            mine,
            got,
            dsummed,
            resid,
            first_vectors,
            sums_ffn,
            up_bias_grad,
        )
        dresid_core = over_core(dresid_low)
        dcontext_own, dcontext_z, out_grad_z, small = small_kernel(
            context_back_kernel,
            "context_back",
            (
                ((width, half), BF16),
                ((width, half), BF16),
                ((width + 16, model), BF16),
                ((16, model), F32),
            ),
            (),
            dresid_low,
            dresid_core,
            small,
            out_own,
            out_other,
            context_other,
        )
        dcontext_z, dcontext_own, out_grad_z, layer_out = stage(
            dcontext_z, dcontext_own, out_grad_z, layer_out
        )
        dcontext_other = over_z(dcontext_z)
        layer_out = swap(layer_out)
        around = (dcontext_own, wide_own, totals_own)
        dq_own, sums = attend_backward(qkv, around, marks, 0, 0, rows, None, F32)

        dq_core, sums = attend_backward(qkv, around, marks, rows, rows, rows, sums, F32)
        dq_core, sums, dcontext_other, out_grad_z = stage(
            dq_core, sums, dcontext_other, out_grad_z
        )
        out_grad_other = over_z(out_grad_z)
        around = (dcontext_other, wide_z, totals_z)
        dq_z, sums = attend_backward(qkv, around, marks, half, 0, rows, sums, F32)

        dq_z, sums, layer_out, *plane_got = stage(dq_z, sums, layer_out, *plane_got)
        kept_own, send_own, kept_other, send_other = small_kernel(
            fold_plane_kernel,
            "fold_plane",
            (((2 * part, model), F32), ((2 * part, model), BF16)) * 2,
            (),
            parts[0],
            plane_got[0],
            parts[2],
            plane_got[1],
        )
        send_own, send_other = over_y(send_own), over_x(send_other)
        dq_zc, sums = attend_backward(qkv, around, marks, 3 * rows, rows, rows, sums, BF16)

        def home(value):
            kept, send, far = value
            send = exchange(send, lambda i, t: (i, t ^ 2) if moved_at(i, t) else (i ^ 1, t))
            far = exchange(far, lambda i, t: (i ^ 1, t ^ 2), moved_at)
            return kept, send, far

        def outer(value):
            bit = 8
            while bit < ndp:
                value = value + exchange(
                    value.astype(BF16), lambda i, t, bit=bit: (i ^ bit, t)
                ).astype(F32)
                bit *= 2
            return value

        def fold_home(name, value, kind=BF16):
            result = small_kernel(
                fold_home_kernel,
                name,
                ((value[0].shape, kind if ndp == 8 else F32),),
                (flags,),
                *value,
            )[0]
            return outer(result).astype(kind)

        dq_zc, sums, out_grad_other = stage(dq_zc, sums, out_grad_other)
        input_z, input_zc = input_back(half, dq_z, dq_zc, sums, weights)
        input_z, input_zc, sums, send_own, send_other = stage(
            input_z, input_zc, sums, send_own, send_other
        )
        unit_sum, unit_z = small_kernel(
            fold_shards_kernel,
            "fold_shards",
            (((2 * part, model), F32), ((2 * part, model), BF16)),
            (),
            kept_own,
            send_own,
            kept_other,
            send_other,
        )
        unit_z, input_zc, sums = stage(unit_z, input_zc, sums)
        unit_z = over_z(unit_z)
        input_zc = over_core(input_zc)
        mine, theirs = small_kernel(
            input_own_kernel,
            "input_own",
            (((rows, model), F32), ((rows, model), BF16)),
            (flags,),
            dq_own,
            dq_core,
            sums,
            weights,
            dresid,
            cotangent,
        )
        packed = weight_grads(
            group,
            (dq_own, dq_core, dq_z, dq_zc),
            sums,
            context_own,
            dresid_low,
            dresid_core,
            out_grad_other,
            small,
        )
        packed, input_z, input_zc, mine, theirs = stage(packed, input_z, input_zc, mine, theirs)
        input_z = small_kernel(
            fold_inputs_kernel, "fold_inputs", (((rows, model), BF16),), (), input_z, input_zc
        )[0]
        input_z, packed, theirs, unit_z = stage(input_z, packed, theirs, unit_z)
        input_other = over_z(input_z)
        parted = lax.all_to_all(packed, ("y", "x"), split_axis=0, concat_axis=0, tiled=True)
        theirs = over_core(theirs)
        unit_home = small_kernel(
            fold_z_kernel,
            "fold_z",
            (((part, model), F32), ((part, model), BF16), ((part, model), BF16)),
            (flags,),
            unit_sum,
            unit_z,
        )
        mine, theirs, *unit_home = stage(mine, theirs, *unit_home)
        unit_home = home(unit_home)

        parted, mine, theirs, *unit_home = stage(parted, mine, theirs, *unit_home)
        head_home = small_kernel(
            fold_parts_kernel,
            "fold_parts",
            (
                ((width // 2 + 16, model), F32),
                ((width // 2 + 16, model), BF16),
                ((width // 2 + 16, model), BF16),
            ),
            (flags,),
            parted,
        )
        mine, theirs, kept, send, far, *head_home = stage(mine, theirs, *unit_home, *head_home)
        head_home = home(head_home)
        unit_all = over_plane(fold_home("fold_units", (kept, send, far)))
        mine, theirs, input_other = stage(mine, theirs, input_other)
        tokens_grad = small_kernel(
            add_tokens_kernel,
            "add_tokens",
            (((rows, model), BF16),),
            (),
            mine,
            theirs,
            input_other,
        )[0]
        tokens_grad, *head_home = stage(tokens_grad, *head_home)
        tokens_grad = swap(tokens_grad)
        heads = fold_home("fold_heads", head_home, F32)
        heads, unit_all = stage(heads, unit_all)
        head_all = over_plane(heads[: width // 2].astype(BF16))
        small = heads[width // 2 :]
        up_bias_sum = lax.dynamic_slice_in_dim(small[6:10], t, 1, 0)[0]
        unit_other = over_core(unit_all)
        up_sum, down_sum = small_kernel(
            unit_results_kernel,
            "unit_results",
            (((model, 4 * part), F32), ((4 * part, model), F32)),
            (flags,),
            unit_all,
            unit_other,
        )
        head_all, up_sum, down_sum, tokens_grad, small, up_bias_sum = stage(
            head_all, up_sum, down_sum, tokens_grad, small, up_bias_sum
        )
        head_other = over_core(head_all)
        sums = small_kernel(
            head_results_kernel,
            "head_results",
            (((width, model), F32),) * 4,
            (flags,),
            head_all,
            head_other,
        )
        narrow = small[12, :width], small[12, width : 2 * width]

        return (
            layer_out,
            tokens_grad,
            sums[0].T,
            narrow[0],
            sums[1].T,
            sums[2].T,
            narrow[1],
            sums[3],
            small[0],
            small[1],
            small[2],
            up_sum,
            up_bias_sum,
            down_sum,
            small[3],
            small[4],
            small[5],
        )

    return jax.shard_map(
        shards,
        mesh=fine,
        in_specs=(
            P(AXES, None),
            P(AXES, None),
            P(DP, None),
            P(DP),
            P(None, "tensor"),
            P("tensor"),
            P(None, "tensor"),
            P(None, "tensor"),
            P("tensor"),
            P("tensor", None),
            P(),
            P(),
            P(),
            P(None, "tensor"),
            P("tensor"),
            P("tensor", None),
            P(),
            P(),
            P(),
        ),
        out_specs=(
            P(AXES, None),
            P(AXES, None),
            P(None, "tensor"),
            P("tensor"),
            P(None, "tensor"),
            P(None, "tensor"),
            P("tensor"),
            P("tensor", None),
            P(),
            P(),
            P(),
            P(None, "tensor"),
            P("tensor"),
            P("tensor", None),
            P(),
            P(),
            P(),
        ),
        check_vma=False,
    )
```

```python
import functools

import jax
import jax.numpy as jnp
from jax import lax
from jax.experimental import pallas as pl
from jax.experimental.pallas import tpu as pltpu
from jax.sharding import Mesh
from jax.sharding import PartitionSpec as P

HEAD_DIM = 64
QUERIES, KEYS = 512, 256
EPS = 1e-05
NEG = -1e30
F32 = jnp.float32
BF16 = jnp.bfloat16
SMEM = pl.BlockSpec(memory_space=pltpu.SMEM)
VMEM = pl.BlockSpec(memory_space=pltpu.VMEM)
SHAPE = jax.ShapeDtypeStruct


def matmul(left, right):
    return jnp.dot(left, right, preferred_element_type=F32)


def matmul_left(left, right):
    return lax.dot_general(left, right, (((0,), (0,)), ((), ())), preferred_element_type=F32)


def matmul_right(left, right):
    return lax.dot_general(left, right, (((1,), (1,)), ((), ())), preferred_element_type=F32)


def stage(*values):
    return lax.optimization_barrier(values)


def cost(micros):
    return pl.CostEstimate(flops=int(micros * 1e9), bytes_accessed=1 << 12, transcendentals=0)


def room(mebibytes):
    return pltpu.CompilerParams(vmem_limit_bytes=mebibytes << 20)


def head_parts(width):
    return [slice(h, h + HEAD_DIM) for h in range(0, width, HEAD_DIM)]


def attend_forward_kernel(
    bq,
    bk,
    first,
    qlow_ref,
    qhigh_ref,
    klow_ref,
    khigh_ref,
    qkv_ref,
    row_ref,
    column_ref,
    wide_ref,
    context_ref,
    totals_ref,
    top_ref,
    sum_ref,
    acc_ref,
):
    width, count = wide_ref.shape
    length = qkv_ref.shape[1]
    parts = head_parts(width)
    heads = range(len(parts))
    key_parts = head_parts(2 * width)[len(parts) :]
    value_parts = head_parts(3 * width)[2 * len(parts) :]

    def over_query(i, _):
        at_o = pl.ds(pl.multiple_of(i * bq, bq), bq)
        at_q = pl.ds(pl.multiple_of(first + i * bq, bq), bq)
        block = i + first // bq
        top_ref[...] = jnp.full(top_ref.shape, NEG, F32)
        sum_ref[...] = jnp.zeros(sum_ref.shape, F32)
        acc_ref[...] = jnp.zeros(acc_ref.shape, F32)
        row = row_ref[0:1, at_q]

        def over_keys(j, _):
            @pl.when((klow_ref[j] <= qhigh_ref[block]) & (qlow_ref[block] <= khigh_ref[j]))
            def _():
                at_k = pl.ds(pl.multiple_of(j * bk, bk), bk)
                column = column_ref[at_k, :]
                same = jnp.concatenate([column] * (bq // 128), 1) == row
                scores = [
                    matmul_left(qkv_ref[k, at_k], qkv_ref[q, at_q])
                    for k, q in zip(key_parts, parts)
                ]
                scores = [jnp.where(same, value, NEG) for value in scores]
                old = [top_ref[h : h + 1, :] for h in heads]
                top = [jnp.maximum(o, jnp.max(v, 0, keepdims=True)) for o, v in zip(old, scores)]
                exponent = [jnp.exp(v - m) for v, m in zip(scores, top)]
                scale = [jnp.exp(o - m) for o, m in zip(old, top)]
                total = [
                    sum_ref[h : h + 1, :] * scale[h] + jnp.sum(exponent[h], 0, keepdims=True)
                    for h in heads
                ]
                added = [
                    matmul(qkv_ref[v, at_k], e.astype(BF16)) for v, e in zip(value_parts, exponent)
                ]
                added = [acc_ref[p, :] * c + v for p, c, v in zip(parts, scale, added)]
                for h in heads:
                    top_ref[h : h + 1, :] = top[h]
                    sum_ref[h : h + 1, :] = total[h]
                    acc_ref[parts[h], :] = added[h]

            return 0

        lax.fori_loop(0, length // bk, over_keys, 0)
        for h in heads:
            value = acc_ref[parts[h], :] / sum_ref[h : h + 1, :]
            wide_ref[parts[h], at_o] = value
            context_ref[parts[h], at_o] = value.astype(BF16)
            totals_ref[h : h + 1, at_o] = top_ref[h : h + 1, :] + jnp.log(sum_ref[h : h + 1, :])
        return 0

    lax.fori_loop(0, count // bq, over_query, 0)


def attend_backward_kernel(
    bq,
    bk,
    first,
    base,
    follows,
    qlow_ref,
    qhigh_ref,
    klow_ref,
    khigh_ref,
    qkv_ref,
    dcontext_ref,
    wide_ref,
    totals_ref,
    row_ref,
    column_ref,
    *rest,
):
    if follows:
        before_ref, dquery_ref, sums_ref, delta_ref, dq_ref, dk_ref, dv_ref = rest
    else:
        dquery_ref, sums_ref, delta_ref, dq_ref, dk_ref, dv_ref = rest
    width, count = dquery_ref.shape
    length = qkv_ref.shape[1]
    parts = head_parts(width)
    heads = range(len(parts))
    key_parts = head_parts(2 * width)[len(parts) :]
    value_parts = head_parts(3 * width)[2 * len(parts) :]
    dq_ref[...] = jnp.zeros(dq_ref.shape, F32)
    chunk = slice(base, base + count)
    for h in heads:
        delta_ref[h : h + 1, :] = jnp.sum(
            wide_ref[parts[h], chunk] * dcontext_ref[parts[h], chunk].astype(F32), 0, keepdims=True
        )

    def over_keys(j, _):
        at_k = pl.ds(pl.multiple_of(j * bk, bk), bk)
        if follows:
            dk_ref[...] = before_ref[0:width, at_k]
            dv_ref[...] = before_ref[width : 2 * width, at_k]
        else:
            dk_ref[...] = jnp.zeros(dk_ref.shape, F32)
            dv_ref[...] = jnp.zeros(dv_ref.shape, F32)

        def over_query(i, _):
            block = i + first // bq

            @pl.when((klow_ref[j] <= qhigh_ref[block]) & (qlow_ref[block] <= khigh_ref[j]))
            def _():
                at_o = pl.ds(pl.multiple_of(i * bq, bq), bq)
                at_b = pl.ds(pl.multiple_of(base + i * bq, bq), bq)
                at_q = pl.ds(pl.multiple_of(first + i * bq, bq), bq)
                column = column_ref[at_k, :]
                same = jnp.concatenate([column] * (bq // 128), 1) == row_ref[0:1, at_q]
                scores = [
                    matmul_left(qkv_ref[k, at_k], qkv_ref[q, at_q])
                    for k, q in zip(key_parts, parts)
                ]
                dprobs = [
                    matmul_left(qkv_ref[v, at_k], dcontext_ref[p, at_b])
                    for v, p in zip(value_parts, parts)
                ]
                probs = [
                    jnp.exp(jnp.where(same, scores[h], NEG) - totals_ref[h : h + 1, at_b])
                    for h in heads
                ]
                dscores = [
                    (probs[h] * (dprobs[h] - delta_ref[h : h + 1, at_o])).astype(BF16)
                    for h in heads
                ]
                dv = [
                    matmul_right(dcontext_ref[p, at_b], v.astype(BF16)) for p, v in zip(parts, probs)
                ]
                dk = [matmul_right(qkv_ref[p, at_q], v) for p, v in zip(parts, dscores)]
                dq = [matmul(qkv_ref[k, at_k], v) for k, v in zip(key_parts, dscores)]
                for h in heads:
                    dv_ref[parts[h], :] += dv[h]
                    dk_ref[parts[h], :] += dk[h]
                    dq_ref[parts[h], at_o] += dq[h]

            return 0

        lax.fori_loop(0, count // bq, over_query, 0)
        sums_ref[0:width, at_k] = dk_ref[...].astype(sums_ref.dtype)
        sums_ref[width : 2 * width, at_k] = dv_ref[...].astype(sums_ref.dtype)
        return 0

    lax.fori_loop(0, length // bk, over_keys, 0)
    dquery_ref[...] = dq_ref[...].astype(BF16)


def bounds(segment, block):
    blocks = segment.reshape(-1, block)
    return jnp.min(blocks, 1), jnp.max(blocks, 1)


def attend_forward(qkv, marks, first, count):
    width = qkv.shape[0] // 3
    wide_low, wide_high, low, high, row, column = marks
    bq, bk = QUERIES, KEYS
    return pl.pallas_call(
        functools.partial(attend_forward_kernel, bq, bk, first),
        out_shape=(SHAPE((width, count), F32), SHAPE((width, count), BF16), SHAPE((8, count), F32)),
        in_specs=[SMEM] * 4 + [VMEM] * 3,
        out_specs=(VMEM,) * 3,
        scratch_shapes=[pltpu.VMEM((8, bq), F32)] * 2 + [pltpu.VMEM((width, bq), F32)],
        cost_estimate=cost(15),
        compiler_params=room(16),
        name="attend_forward",
    )(wide_low, wide_high, low, high, qkv, row, column)


def attend_backward(qkv, around, marks, first, base, count, before, kind):
    dcontext, wide, totals = around
    width, length = dcontext.shape[0], qkv.shape[1]
    _, _, low, high, row, column = marks
    bq = bk = KEYS
    follows = before is not None
    return pl.pallas_call(
        functools.partial(attend_backward_kernel, bq, bk, first, base, follows),
        out_shape=(SHAPE((width, count), BF16), SHAPE((2 * width, length), kind)),
        in_specs=[SMEM] * 4 + [VMEM] * (7 if follows else 6),
        out_specs=(VMEM,) * 2,
        scratch_shapes=[
            pltpu.VMEM((8, count), F32),
            pltpu.VMEM((width, count), F32),
            pltpu.VMEM((width, bk), F32),
            pltpu.VMEM((width, bk), F32),
        ],
        cost_estimate=cost(count // 64),
        compiler_params=room(22),
        name="attend_backward",
    )(
        low,
        high,
        low,
        high,
        qkv,
        dcontext,
        wide,
        totals,
        row,
        column,
        *((before,) if follows else ()),
    )


def plane_slots(flags_ref, slots):
    slots = [jnp.where(flags_ref[2] == 1, slots[k ^ 1], slots[k]) for k in range(4)]
    return [jnp.where(flags_ref[3] == 1, slots[k ^ 2], slots[k]) for k in range(4)]


def feed_forward_kernel(flags_ref, own_ref, core_ref, *rest):
    pieces, (hidden_ref, slope_ref, mine_ref, other_ref, up_ref, down_ref) = rest[:-6], rest[-6:]
    rows, cols = own_ref.shape[0], 256
    part = up_ref.shape[0] // 8
    for n in range(2):
        for k in range(4):
            to = slice((2 * k + n) * part, (2 * k + n + 1) * part)
            up, down = pieces[4 * n + k][0:part, :], pieces[4 * n + k][part : 2 * part, :]
            if n == 0 and k > 0:
                up = up + pieces[8][k - 1, 0:part, :]
                down = down + pieces[8][k - 1, part : 2 * part, :]
            up_ref[to, :] = up
            down_ref[to, :] = down
    biases = []
    for n in range(2):
        value = pieces[4 * n][2 * part : 2 * part + 16, :].astype(F32)[0:1]
        biases.append(plane_slots(flags_ref, [value[:, k * part : (k + 1) * part] for k in range(4)]))
    biases = jnp.concatenate([biases[n][k] for k in range(4) for n in range(2)], 1)
    for source, target, start in ((core_ref, other_ref, rows), (own_ref, mine_ref, 0)):
        at = slice(start, start + rows)
        value = source[...]
        for n in range(0, up_ref.shape[0], cols):
            to = slice(n, n + cols)
            pre = matmul_right(value, up_ref[to, :]) + biases[:, to]
            normal = 0.5 * (1.0 + lax.erf(pre * 0.7071067811865476))
            hidden_ref[at, to] = (pre * normal).astype(BF16)
            density = jnp.exp(-0.5 * pre * pre) * 0.3989422804014327
            slope_ref[at, to] = (normal + pre * density).astype(BF16)
        target[...] = matmul(hidden_ref[at, :], down_ref[...]).astype(target.dtype)


def feed_forward(flags, own, core, pieces):
    rows, model = own.shape
    units = 2 * model
    return pl.pallas_call(
        feed_forward_kernel,
        out_shape=(
            SHAPE((2 * rows, units), BF16),
            SHAPE((2 * rows, units), BF16),
            SHAPE((rows, model), F32),
            SHAPE((rows, model), BF16),
            SHAPE((units, model), BF16),
            SHAPE((units, model), BF16),
        ),
        in_specs=[SMEM] + [VMEM] * 11,
        out_specs=(VMEM,) * 6,
        cost_estimate=cost(12),
        compiler_params=room(32),
        name="feed_forward",
    )(flags, own, core, *pieces)


def hidden_back_kernel(
    own_ref, core_ref, slope_ref, up_ref, down_ref, dpre_ref, mine_ref, other_ref, bias_ref
):
    rows, cols = own_ref.shape[0], 256
    for source, target, start in ((core_ref, other_ref, rows), (own_ref, mine_ref, 0)):
        at = slice(start, start + rows)
        value = source[...]
        for n in range(0, up_ref.shape[0], cols):
            to = slice(n, n + cols)
            dhidden = matmul_right(value, down_ref[to, :])
            dpre_ref[at, to] = (dhidden * slope_ref[at, to].astype(F32)).astype(BF16)
        target[...] = matmul(dpre_ref[at, :], up_ref[...]).astype(target.dtype)
    bias_ref[...] = matmul(jnp.ones((8, 2 * rows), BF16), dpre_ref[...])


def hidden_back(own, core, slope, up, down):
    rows, model = own.shape
    units = up.shape[0]
    return pl.pallas_call(
        hidden_back_kernel,
        out_shape=(
            SHAPE((2 * rows, units), BF16),
            SHAPE((rows, model), F32),
            SHAPE((rows, model), BF16),
            SHAPE((8, units), F32),
        ),
        in_specs=[VMEM] * 5,
        out_specs=(VMEM,) * 4,
        cost_estimate=cost(0),
        compiler_params=room(26),
        name="hidden_back",
    )(own, core, slope, up, down)


def unit_grads_kernel(
    dpre_ref, normed_ref, normed_core_ref, hidden_ref, dffn_ref, dffn_core_ref, *refs
):
    rows = normed_ref.shape[0]
    part = dpre_ref.shape[1] // 8
    places = ((0, 0), (1, 0), (0, 1), (1, 1)), ((0, 0), (0, 1), (1, 0), (1, 1))
    halves = (dpre_ref, normed_ref, normed_core_ref), (hidden_ref, dffn_ref, dffn_core_ref)
    for m, (left_ref, own_ref, core_ref) in enumerate(halves):
        for k in range(4):
            at = slice(2 * k * part, 2 * (k + 1) * part)
            total = matmul_left(left_ref[0:rows, at], own_ref[...])
            total = total + matmul_left(left_ref[rows : 2 * rows, at], core_ref[...])
            for n in range(2):
                sent, slot = places[n][k]
                to = slice((2 * m + slot) * part, (2 * m + slot + 1) * part)
                refs[2 * n + sent][to, :] = total[n * part : (n + 1) * part].astype(BF16)


def unit_grads(dpre, normed, normed_core, hidden, dffn, dffn_core):
    return pl.pallas_call(
        unit_grads_kernel,
        out_shape=(SHAPE((dpre.shape[1] // 2, normed.shape[1]), BF16),) * 4,
        in_specs=[VMEM] * 6,
        out_specs=(VMEM,) * 4,
        cost_estimate=cost(5),
        compiler_params=room(24),
        name="unit_grads",
    )(dpre, normed, normed_core, hidden, dffn, dffn_core)


def out_project_kernel(own_ref, other_ref, own_w_ref, other_w_ref, mine_ref, theirs_ref):
    rows = mine_ref.shape[0]
    for target, at in ((theirs_ref, slice(rows, 2 * rows)), (mine_ref, slice(0, rows))):
        value = matmul_left(own_ref[:, at], own_w_ref[...])
        value = value + matmul_left(other_ref[:, at], other_w_ref[...])
        target[...] = value.astype(target.dtype)


def out_project(own, other, own_weight, other_weight):
    rows, model = own.shape[1] // 2, own_weight.shape[1]
    return pl.pallas_call(
        out_project_kernel,
        out_shape=(SHAPE((rows, model), F32), SHAPE((rows, model), BF16)),
        in_specs=[VMEM] * 4,
        out_specs=(VMEM,) * 2,
        cost_estimate=cost(3),
        compiler_params=room(12),
        name="out_project",
    )(own, other, own_weight, other_weight)


def input_back_kernel(start, first_ref, second_ref, sums_ref, weights_ref, mine_ref, theirs_ref):
    rows = first_ref.shape[1]
    width = first_ref.shape[0]
    query_weights = weights_ref[0:width, :] * 0.125
    for k, ref, target in ((1, second_ref, theirs_ref), (0, first_ref, mine_ref)):
        at = slice(start + k * rows, start + (k + 1) * rows)
        value = matmul_left(ref[...], query_weights)
        value = value + matmul_left(sums_ref[:, at], weights_ref[width:, :])
        target[...] = value.astype(target.dtype)


def input_back(start, first, second, sums, weights):
    shape = (first.shape[1], weights.shape[1])
    return pl.pallas_call(
        functools.partial(input_back_kernel, start),
        out_shape=(SHAPE(shape, F32), SHAPE(shape, BF16)),
        in_specs=[VMEM] * 4,
        out_specs=(VMEM,) * 2,
        cost_estimate=cost(0),
        compiler_params=room(14),
        name="input_back",
    )(first, second, sums, weights)


def input_own_kernel(
    flags_ref,
    first_ref,
    second_ref,
    sums_ref,
    weights_ref,
    dresid_ref,
    cotangent_ref,
    mine_ref,
    theirs_ref,
):
    width, rows = first_ref.shape
    query_weights = weights_ref[0:width, :] * 0.125
    for k, ref in ((1, second_ref), (0, first_ref)):
        at = slice(k * rows, (k + 1) * rows)
        value = matmul_left(ref[...], query_weights)
        value = value + matmul_left(sums_ref[:, at], weights_ref[width:, :])
        if k == 1:
            theirs_ref[...] = value.astype(BF16)
        else:
            skipped = (1 - flags_ref[1]).astype(F32)
            mine_ref[...] = value + dresid_ref[...] + skipped * cotangent_ref[...].astype(F32)


def context_back_kernel(
    own_ref,
    core_ref,
    small_ref,
    own_w_ref,
    other_w_ref,
    context_ref,
    mine_ref,
    theirs_ref,
    grad_ref,
    sum_ref,
):
    rows = own_ref.shape[0] - 16
    width = mine_ref.shape[0]
    grad = 0.0
    for k, ref in enumerate((own_ref, core_ref)):
        at = slice(k * rows, (k + 1) * rows)
        value = ref[0:rows, :]
        theirs_ref[:, at] = matmul_right(other_w_ref[...], value).astype(BF16)
        mine_ref[:, at] = matmul_right(own_w_ref[...], value).astype(BF16)
        grad = grad + matmul(context_ref[:, at], value)
    grad_ref[0:width, :] = grad.astype(BF16)
    total = small_ref[...] + core_ref[rows : rows + 16, :].astype(F32)
    sum_ref[...] = total
    grad_ref[width : width + 16, :] = total.astype(BF16)


def take_kernel(
    flags_ref,
    query_ref,
    key_ref,
    value_ref,
    extra_ref,
    up_ref,
    down_ref,
    piece_ref,
    quarter_ref,
    local_ref,
    turned_ref,
):
    place = flags_ref[0]
    held = 1.0 - flags_ref[1].astype(F32)
    fourth = query_ref.shape[0] // 4
    for n, ref in enumerate((query_ref, key_ref, value_ref)):
        at = pl.ds(pl.multiple_of(place * fourth, fourth), fourth)
        piece_ref[n * fourth : (n + 1) * fourth, :] = ref[at, :]
    piece_ref[3 * fourth :, :] = extra_ref[0:16, :]
    turned_ref[...] = up_ref[...].T
    part = local_ref.shape[1] // 2
    quarter_ref[2 * part :, :] = extra_ref[16:32, :]
    for k in range(4):
        at = pl.ds(pl.multiple_of((place ^ k) * part, part), part)
        if k == 0:
            quarter_ref[0:part, :] = turned_ref[at, :]
            quarter_ref[part : 2 * part, :] = down_ref[at, :]
        else:
            local_ref[k - 1, 0:part, :] = (turned_ref[at, :] * held).astype(BF16)
            local_ref[k - 1, part : 2 * part, :] = (down_ref[at, :] * held).astype(BF16)


def take(place, heads, extra, up, down):
    units, model = down.shape
    rows = heads[0].shape[0] // 4 * 3 + 16
    return pl.pallas_call(
        take_kernel,
        out_shape=(
            SHAPE((rows, model), BF16),
            SHAPE((units // 2 + 16, model), BF16),
            SHAPE((3, units // 2, model), BF16),
        ),
        in_specs=[SMEM] + [VMEM] * 6,
        out_specs=(VMEM,) * 3,
        scratch_shapes=[pltpu.VMEM((units, model), BF16)],
        cost_estimate=cost(20),
        compiler_params=room(14),
        name="take",
    )(place, *heads, extra, up, down)


def small_kernel(kernel, name, results, flags, *operands, mebibytes=16):
    return pl.pallas_call(
        kernel,
        out_shape=tuple(SHAPE(shape, kind) for shape, kind in results),
        in_specs=[SMEM] * len(flags) + [VMEM] * len(operands),
        out_specs=(VMEM,) * len(results),
        cost_estimate=cost(0),
        compiler_params=room(mebibytes),
        name=name,
    )(*flags, *operands)


def fold_plane_kernel(*refs):
    part = refs[0].shape[0] // 4
    for n in range(2):
        keep_ref, got_ref = refs[2 * n], refs[2 * n + 1]
        kept_ref, send_ref = refs[4 + 2 * n], refs[5 + 2 * n]
        for m in range(2):
            at = slice(m * part, (m + 1) * part)
            kept, sent = (
                keep_ref[k * part : (k + 1) * part, :].astype(F32)
                + got_ref[k * part : (k + 1) * part, :].astype(F32)
                for k in (2 * m, 2 * m + 1)
            )
            kept_ref[at, :] = kept
            send_ref[at, :] = sent.astype(BF16)


def fold_shards_kernel(own_ref, own_got_ref, other_ref, other_got_ref, sum_ref, send_ref):
    sum_ref[...] = own_ref[...] + own_got_ref[...].astype(F32)
    send_ref[...] = (other_ref[...] + other_got_ref[...].astype(F32)).astype(BF16)


def split_home(flags_ref, value, kept_ref, send_ref, far_ref):
    half = kept_ref.shape[0]
    kept_ref[...] = value[:half]
    far_ref[...] = value[half:].astype(BF16)

    @pl.when(flags_ref[0] == 1)
    def _():
        send_ref[...] = value[:half].astype(BF16)

    @pl.when(flags_ref[0] == 0)
    def _():
        send_ref[...] = value[half:].astype(BF16)


def fold_z_kernel(flags_ref, sum_ref, got_ref, kept_ref, send_ref, far_ref):
    split_home(flags_ref, sum_ref[...] + got_ref[...].astype(F32), kept_ref, send_ref, far_ref)


def fold_parts_kernel(flags_ref, parts_ref, kept_ref, send_ref, far_ref):
    value = parts_ref[0].astype(F32) + parts_ref[1].astype(F32)
    value = value + (parts_ref[2].astype(F32) + parts_ref[3].astype(F32))
    half = kept_ref.shape[0] - 16
    tail = value[2 * half :]
    kept_ref[0:half, :] = value[:half]
    kept_ref[half:, :] = tail
    far_ref[0:half, :] = value[half : 2 * half].astype(BF16)
    far_ref[half:, :] = tail.astype(BF16)
    send_ref[half:, :] = tail.astype(BF16)

    @pl.when(flags_ref[0] == 1)
    def _():
        send_ref[0:half, :] = value[:half].astype(BF16)

    @pl.when(flags_ref[0] == 0)
    def _():
        send_ref[0:half, :] = value[half : 2 * half].astype(BF16)


def fold_inputs_kernel(mine_ref, theirs_ref, result_ref):
    result_ref[...] = (mine_ref[...] + theirs_ref[...].astype(F32)).astype(BF16)


def add_tokens_kernel(mine_ref, theirs_ref, other_ref, result_ref):
    other = theirs_ref[...].astype(F32) + other_ref[...].astype(F32)
    result_ref[...] = (mine_ref[...] + other).astype(BF16)


def fold_home_kernel(flags_ref, kept_ref, got_ref, far_ref, result_ref):
    got = got_ref[...].astype(F32)
    first = jnp.where(flags_ref[0] == 1, far_ref[...].astype(F32), kept_ref[...])
    result_ref[...] = (first + got).astype(result_ref.dtype)


def unit_results_kernel(flags_ref, mine_ref, other_ref, up_ref, down_ref):
    def put(first_ref, second_ref):
        part = first_ref.shape[1]
        for k in range(4):
            down_ref[k * part : (k + 1) * part, :] = second_ref[k].astype(F32)
        up_ref[...] = first_ref[...].reshape(4 * part, first_ref.shape[2]).astype(F32).T

    @pl.when(flags_ref[0] == 1)
    def _():
        put(other_ref, mine_ref)

    @pl.when(flags_ref[0] == 0)
    def _():
        put(mine_ref, other_ref)


def head_results_kernel(flags_ref, mine_ref, other_ref, layer_ref, tokens_ref, *results):
    half = mine_ref.shape[1]
    results[4][...] = layer_ref[...]
    results[5][...] = tokens_ref[...]
    for k, ref in enumerate(results[:4]):
        mine, other = mine_ref[k].astype(F32), other_ref[k].astype(F32)
        ref[0:half, :] = jnp.where(flags_ref[0] == 1, other, mine)
        ref[half : 2 * half, :] = jnp.where(flags_ref[0] == 1, mine, other)


def normal_rows(value):
    center = value - jnp.mean(value, -1, keepdims=True)
    root = lax.rsqrt(jnp.mean(center * center, -1, keepdims=True) + EPS)
    return center * root, root


def normal_back(grad, normal, root):
    inner = jnp.mean(grad * normal, -1, keepdims=True)
    return root * (grad - jnp.mean(grad, -1, keepdims=True) - normal * inner)


STEP = 128


def first_norm_kernel(mine_ref, got_ref, token_ref, vector_ref, resid_ref, normed_ref, low_ref):
    def step(k, _):
        at = pl.ds(pl.multiple_of(k * STEP, STEP), STEP)
        attention = mine_ref[at, :] + got_ref[at, :].astype(F32)
        resid = token_ref[at, :].astype(F32) + attention + vector_ref[0:1, :]
        resid_ref[at, :] = resid
        normed = normal_rows(resid)[0] * vector_ref[1:2, :] + vector_ref[2:3, :]
        normed_ref[at, :] = normed
        low_ref[at, :] = normed.astype(BF16)
        return 0

    lax.fori_loop(0, mine_ref.shape[0] // STEP, step, 0)


def second_norm_kernel(
    flags_ref,
    mine_ref,
    got_ref,
    normed_ref,
    cotangent_ref,
    token_ref,
    vector_ref,
    layer_ref,
    dsummed_ref,
    low_ref,
    sums_ref,
):
    keep = flags_ref[1].astype(F32)
    sums_ref[...] = jnp.zeros(sums_ref.shape, F32)

    def step(k, _):
        at = pl.ds(pl.multiple_of(k * STEP, STEP), STEP)
        units = mine_ref[at, :] + got_ref[at, :].astype(F32)
        normal, root = normal_rows(normed_ref[at, :] + units + vector_ref[0:1, :])
        final = normal * vector_ref[1:2, :] + vector_ref[2:3, :]
        token = token_ref[at, :].astype(F32)
        layer_ref[at, :] = (keep * final + (1.0 - keep) * token).astype(BF16)
        cotangent = cotangent_ref[at, :].astype(F32)
        dfinal = keep * cotangent
        dsummed = normal_back(dfinal * vector_ref[1:2, :], normal, root)
        dsummed_ref[at, :] = dsummed
        low_ref[at, :] = dsummed.astype(BF16)
        sums_ref[0:1, :] += jnp.sum(dsummed, 0, keepdims=True)
        sums_ref[1:2, :] += jnp.sum(dfinal * normal, 0, keepdims=True)
        sums_ref[2:3, :] += jnp.sum(dfinal, 0, keepdims=True)
        return 0

    lax.fori_loop(0, mine_ref.shape[0] // STEP, step, 0)


def first_norm_back_kernel(
    flags_ref,
    mine_ref,
    got_ref,
    dsummed_ref,
    resid_ref,
    vector_ref,
    ffn_ref,
    bias_ref,
    dresid_ref,
    low_ref,
    small_ref,
):
    rows, model = mine_ref.shape
    part = model // 4
    small_ref[...] = jnp.zeros(small_ref.shape, F32)

    def step(k, _):
        at = pl.ds(pl.multiple_of(k * STEP, STEP), STEP)
        dnormed = dsummed_ref[at, :] + (mine_ref[at, :] + got_ref[at, :].astype(F32))
        normal, root = normal_rows(resid_ref[at, :])
        dresid = normal_back(dnormed * vector_ref[1:2, :], normal, root)
        dresid_ref[at, :] = dresid
        low_ref[at, :] = dresid.astype(BF16)
        small_ref[0:1, :] += jnp.sum(dresid, 0, keepdims=True)
        small_ref[1:2, :] += jnp.sum(dnormed * normal, 0, keepdims=True)
        small_ref[2:3, :] += jnp.sum(dnormed, 0, keepdims=True)
        return 0

    lax.fori_loop(0, rows // STEP, step, 0)
    small_ref[3:6, :] = ffn_ref[0:3, :]
    wide = 0.0
    for n in range(2):
        slots = [bias_ref[0:1, (2 * k + n) * part : (2 * k + n + 1) * part] for k in range(4)]
        value = jnp.concatenate(plane_slots(flags_ref, slots), 1)
        at = lax.broadcasted_iota(jnp.int32, (4, model), 0) == (flags_ref[4] ^ n)
        wide = wide + jnp.where(at, value, 0.0)
    small_ref[6:10, :] = wide
    low_ref[rows : rows + 16, :] = small_ref[...].astype(BF16)


def vectors(bias, gain, shift):
    return jnp.concatenate([jnp.stack([bias, gain, shift]), jnp.zeros((5,) + bias.shape)]).astype(F32)


def rowwise(kernel, name, kinds, flags, *operands):
    shape = operands[0].shape
    results = tuple(SHAPE(shape if kind else (8, shape[1]), kind or F32) for kind in kinds)
    return pl.pallas_call(
        kernel,
        out_shape=results,
        in_specs=[SMEM] * len(flags) + [VMEM] * len(operands),
        out_specs=(VMEM,) * len(results),
        cost_estimate=cost(2),
        compiler_params=room(16),
        name=name,
    )(*flags, *operands)


def project_kernel(own_ref, core_ref, z_ref, zc_ref, gathered_ref, qkv_ref, weights_ref):
    rows = own_ref.shape[0]
    fourth = weights_ref.shape[0] // 4
    width = weights_ref.shape[0] // 3
    for k in range(4):
        for n in range(3):
            piece = fourth // 3
            to = slice(n * width + k * piece, n * width + (k + 1) * piece)
            weights_ref[to, :] = gathered_ref[k, n * piece : (n + 1) * piece, :]
    weights = weights_ref[...]
    biases = gathered_ref[0, fourth : fourth + 16, 0 : 3 * width]
    first = lax.broadcasted_iota(jnp.int32, (16, rows), 0) == 0
    columns = matmul_left(biases, jnp.where(first, 1.0, 0.0).astype(BF16))
    for k, ref in enumerate((own_ref, core_ref, z_ref, zc_ref)):
        at = slice(k * rows, (k + 1) * rows)
        value = matmul_right(weights, ref[...]) + columns
        qkv_ref[0:width, at] = (value[:width] * 0.125).astype(BF16)
        qkv_ref[width:, at] = value[width:].astype(BF16)


def project(tokens, gathered):
    rows, model = tokens[0].shape
    units = 4 * (gathered.shape[1] - 16)
    return pl.pallas_call(
        project_kernel,
        out_shape=(SHAPE((units, 4 * rows), BF16), SHAPE((units, model), BF16)),
        in_specs=[VMEM] * 5,
        out_specs=(VMEM,) * 2,
        cost_estimate=cost(4),
        compiler_params=room(20),
        name="project",
    )(*tokens, gathered)


def weight_grads_kernel(
    own_ref,
    core_ref,
    z_ref,
    zc_ref,
    dq_own_ref,
    dq_core_ref,
    dq_z_ref,
    dq_zc_ref,
    sums_ref,
    context_ref,
    dresid_ref,
    dresid_core_ref,
    other_ref,
    small_ref,
    packed_ref,
):
    rows = own_ref.shape[0]
    width = dq_own_ref.shape[0]
    tokens = (own_ref, core_ref, z_ref, zc_ref)
    dquery = (dq_own_ref, dq_core_ref, dq_z_ref, dq_zc_ref)
    total, query, bias = 0.0, 0.0, 0.0
    count = jnp.ones((8, rows), BF16)
    for k in range(4):
        value = tokens[k][...]
        query = query + matmul(dquery[k][...], value)
        total = total + matmul(sums_ref[:, k * rows : (k + 1) * rows], value)
        bias = bias + matmul_right(count, dquery[k][...])
    packed_ref[0, 0:width, :] = (query * 0.125).astype(BF16)
    packed_ref[1, 0:width, :] = total[:width].astype(BF16)
    packed_ref[2, 0:width, :] = total[width:].astype(BF16)
    out = matmul(context_ref[:, 0:rows], dresid_ref[0:rows, :])
    out = out + matmul(context_ref[:, rows : 2 * rows], dresid_core_ref[0:rows, :])
    packed_ref[3, 0:width, :] = (out + other_ref[0:width, :].astype(F32)).astype(BF16)
    small = small_ref[...] + other_ref[width : width + 16, :].astype(F32)
    count = jnp.ones((8, 4 * rows), BF16)
    values = matmul_right(count, sums_ref[width : 2 * width, :])
    biases = jnp.concatenate([bias * 0.125, values, jnp.zeros_like(bias), jnp.zeros_like(bias)], 1)
    at_row = lax.broadcasted_iota(jnp.int32, (8, 4 * width), 0) == 4
    late = jnp.where(at_row, biases, small[8:16])
    tail = jnp.concatenate([small[0:8], late], 0).astype(BF16)
    for k in range(4):
        packed_ref[k, width : width + 16, :] = tail


def weight_grads(tokens, dquery, sums, context, dresid, dresid_core, other, small):
    width = dquery[0].shape[0]
    return pl.pallas_call(
        weight_grads_kernel,
        out_shape=SHAPE((4, width + 16, tokens[0].shape[1]), BF16),
        in_specs=[VMEM] * 14,
        out_specs=VMEM,
        cost_estimate=cost(8),
        compiler_params=room(18),
        name="weight_grads",
    )(*tokens, *dquery, sums, context, dresid, dresid_core, other, small)


def solution(mesh):
    ndp, nt = mesh.shape["dp"], mesh.shape["tensor"]
    fine = Mesh(
        mesh.devices.reshape(ndp // 8, 2, 2, 2, nt), ("outer", "y", "x", "core", "tensor")
    )
    DP, AXES = ("outer", "y", "x", "core"), ("outer", "y", "x", "core", "tensor")

    def moved_at(i, t):
        return (i & 1) != (t >> 1)

    def exchange(value, target, only=None):
        pairs = []
        for i in range(ndp):
            for t in range(nt):
                if only is None or only(i, t):
                    j, u = target(i, t)
                    pairs.append((i * nt + t, j * nt + u))
        return lax.ppermute(value, AXES, pairs)

    def swap(value):
        return exchange(value, lambda i, t: (i ^ 1, t ^ 2) if moved_at(i, t) else (i, t))

    def over_core(value):
        return exchange(value, lambda i, t: (i ^ 1, t))

    def over_z(value):
        return exchange(value, lambda i, t: (i, t ^ 1))

    def over_x(value):
        return exchange(value, lambda i, t: (i ^ 2, t))

    def over_y(value):
        return exchange(value, lambda i, t: (i ^ 4, t))

    def shards(
        tokens,
        cotangent,
        segment_ids,
        drop_flags,
        query_weight,
        query_bias,
        key_weight,
        value_weight,
        value_bias,
        out_weight,
        out_bias,
        attn_gain,
        attn_shift,
        up_weight,
        up_bias,
        down_weight,
        down_bias,
        ffn_gain,
        ffn_shift,
    ):
        i, t = lax.axis_index(DP), lax.axis_index("tensor")
        core, zbit, xbit, ybit = i & 1, t & 1, (i >> 1) & 1, (i >> 2) & 1
        moved = core != (t >> 1)
        length = segment_ids.shape[1]
        rows, model = tokens.shape
        width = query_weight.shape[1]
        part = up_weight.shape[1] // 4

        def turned(value, axis, bit):
            return jnp.where(bit == 1, jnp.flip(value, axis), value)

        def over_plane(value):
            copies = jnp.broadcast_to(value[None], (4,) + value.shape)
            return lax.all_to_all(copies, ("y", "x"), split_axis=0, concat_axis=0, tiled=True)

        def absolute(value):
            return turned(turned(value, 0, ybit), 1, xbit)

        token_own = swap(tokens)
        token_z = exchange(tokens, lambda i, t: (i, t ^ 1), lambda i, t: not moved_at(i, t))
        blank = jnp.zeros_like(query_bias)
        biases = jnp.concatenate([query_bias, blank, value_bias, blank])
        extra = jnp.concatenate(
            [jnp.broadcast_to(v[None], (16, model)) for v in (biases, up_bias)], 0
        )
        piece, quarter, local = take(
            jnp.stack([ybit * 2 + xbit, moved.astype(jnp.int32)]),
            (query_weight.T, key_weight.T, value_weight.T),
            extra,
            up_weight,
            down_weight,
        )
        piece = swap(piece)
        notes = jnp.concatenate(
            [segment_ids, jnp.broadcast_to(drop_flags[:, None], (1, 128))], axis=1
        )
        notes_core = over_core(notes)
        token_own, token_z, piece, quarter, out_weight, notes, notes_core = stage(
            token_own, token_z, piece, quarter, out_weight, notes, notes_core
        )
        token_core = over_core(token_own)
        token_zm = exchange(token_own, lambda i, t: (i, t ^ 1), moved_at)
        gathered = over_plane(piece)
        quarter = swap(quarter)
        first_vectors = vectors(out_bias, attn_gain, attn_shift)
        second_vectors = vectors(down_bias, ffn_gain, ffn_shift)
        notes = jnp.where(moved, notes_core, notes)
        shard = 2 * core + zbit
        flags = jnp.stack([moved.astype(jnp.int32), 1 - notes[0, length], xbit, ybit, shard])
        segment = notes[0, :length].reshape(2, 2, length // 4)
        segment = turned(turned(segment, 0, core), 1, zbit)
        segment = jnp.swapaxes(segment, 0, 1).reshape(length)
        marks = (
            *bounds(segment, QUERIES),
            *bounds(segment, KEYS),
            jnp.broadcast_to(segment[None], (8, length)),
            jnp.broadcast_to(segment[:, None], (length, 128)),
        )
        token_zm, token_z, gathered, quarter, out_weight, *rest = stage(
            token_zm,
            token_z,
            gathered,
            quarter,
            out_weight,
            flags,
            first_vectors,
            second_vectors,
            *marks,
        )
        flags, first_vectors, second_vectors, *marks = rest
        token_z = jnp.where(moved, token_zm, token_z)
        token_zc = over_core(token_z)
        group = (token_own, token_core, token_z, token_zc)
        qkv, weights = project(group, gathered)

        qkv, quarter, out_weight = stage(qkv, quarter, out_weight)
        quarter_z = over_z(quarter)
        own_x = exchange(quarter[: 2 * part], lambda i, t: (i ^ 2, t), moved_at)
        own_y = exchange(quarter[: 2 * part], lambda i, t: (i ^ 4, t), moved_at)
        out_own = swap(out_weight)
        half = 2 * rows
        wide_z, context_z, totals_z = attend_forward(qkv, marks, half, half)

        qkv, context_z, quarter_z, own_x, own_y, out_own = stage(
            qkv, context_z, quarter_z, own_x, own_y, out_own
        )
        context_other = over_z(context_z)
        out_other = over_z(out_own)
        units_z = quarter_z[: 2 * part]
        quarter_zy, quarter_zx = over_y(units_z), over_x(units_z)
        own_xy = exchange(own_x, lambda i, t: (i ^ 4, t), moved_at)
        wide_own, context_own, totals_own = attend_forward(qkv, marks, 0, half)

        context_own, context_other, out_other, quarter_zy, quarter_zx, own_xy = stage(
            context_own, context_other, out_other, quarter_zy, quarter_zx, own_xy
        )
        quarter_zxy = over_x(quarter_zy)
        mine, theirs = out_project(context_own, context_other, out_own, out_other)
        theirs = over_core(theirs)
        mine, theirs, cotangent = stage(mine, theirs, cotangent)
        cotangent = swap(cotangent)
        resid, normed, normed_low = rowwise(
            first_norm_kernel,
            "first_norm",
            (F32, F32, BF16),
            (),
            mine,
            theirs,
            token_own,
            first_vectors,
        )
        normed_core = over_core(normed_low)

        normed_low, normed_core, quarter_zxy = stage(normed_low, normed_core, quarter_zxy)
        pieces = (quarter, own_x, own_y, own_xy, quarter_z, quarter_zx, quarter_zy, quarter_zxy)
        hidden, slope, mine, theirs, up_all, down_all = feed_forward(
            flags, normed_low, normed_core, (*pieces, local)
        )
        layer_out, dsummed, dffn, sums_ffn = rowwise(
            second_norm_kernel,
            "second_norm",
            (BF16, F32, BF16, None),
            (flags,),
            mine,
            over_core(theirs),
            normed,
            cotangent,
            token_own,
            second_vectors,
        )
        dffn_core = over_core(dffn)

        dffn, dffn_core, layer_out = stage(dffn, dffn_core, layer_out)
        dpre, mine, theirs, up_bias_grad = hidden_back(dffn, dffn_core, slope, up_all, down_all)
        dpre, theirs = stage(dpre, theirs)
        got = over_core(theirs)
        parts = unit_grads(dpre, normed_low, normed_core, hidden, dffn, dffn_core)
        got, *parts = stage(got, *parts)
        plane_got = over_x(parts[1]), over_y(parts[3])
        dresid, dresid_low, small = small_kernel(
            first_norm_back_kernel,
            "first_norm_back",
            (((rows, model), F32), ((rows + 16, model), BF16), ((16, model), F32)),
            (flags,),
            mine,
            got,
            dsummed,
            resid,
            first_vectors,
            sums_ffn,
            up_bias_grad,
        )
        dresid_core = over_core(dresid_low)
        dcontext_own, dcontext_z, out_grad_z, small = small_kernel(
            context_back_kernel,
            "context_back",
            (
                ((width, half), BF16),
                ((width, half), BF16),
                ((width + 16, model), BF16),
                ((16, model), F32),
            ),
            (),
            dresid_low,
            dresid_core,
            small,
            out_own,
            out_other,
            context_other,
        )
        dcontext_z, dcontext_own, out_grad_z, layer_out = stage(
            dcontext_z, dcontext_own, out_grad_z, layer_out
        )
        dcontext_other = over_z(dcontext_z)
        layer_out = swap(layer_out)
        around = (dcontext_own, wide_own, totals_own)
        dq_own, sums = attend_backward(qkv, around, marks, 0, 0, rows, None, F32)

        dq_core, sums = attend_backward(qkv, around, marks, rows, rows, rows, sums, F32)
        dq_core, sums, dcontext_other, out_grad_z = stage(
            dq_core, sums, dcontext_other, out_grad_z
        )
        out_grad_other = over_z(out_grad_z)
        around = (dcontext_other, wide_z, totals_z)
        dq_z, sums = attend_backward(qkv, around, marks, half, 0, rows, sums, F32)

        dq_z, sums, layer_out, *plane_got = stage(dq_z, sums, layer_out, *plane_got)
        kept_own, send_own, kept_other, send_other = small_kernel(
            fold_plane_kernel,
            "fold_plane",
            (((2 * part, model), F32), ((2 * part, model), BF16)) * 2,
            (),
            parts[0],
            plane_got[0],
            parts[2],
            plane_got[1],
        )
        send_own, send_other = over_y(send_own), over_x(send_other)
        dq_zc, sums = attend_backward(qkv, around, marks, 3 * rows, rows, rows, sums, BF16)

        def home(value):
            kept, send, far = value
            send = exchange(send, lambda i, t: (i, t ^ 2) if moved_at(i, t) else (i ^ 1, t))
            far = exchange(far, lambda i, t: (i ^ 1, t ^ 2), moved_at)
            return kept, send, far

        def outer(value):
            bit = 8
            while bit < ndp:
                value = value + exchange(
                    value.astype(BF16), lambda i, t, bit=bit: (i ^ bit, t)
                ).astype(F32)
                bit *= 2
            return value

        def fold_home(name, value, kind=BF16):
            result = small_kernel(
                fold_home_kernel,
                name,
                ((value[0].shape, kind if ndp == 8 else F32),),
                (flags,),
                *value,
            )[0]
            return outer(result).astype(kind)

        dq_zc, sums, out_grad_other = stage(dq_zc, sums, out_grad_other)
        input_z, input_zc = input_back(half, dq_z, dq_zc, sums, weights)
        input_z, input_zc, sums, send_own, send_other = stage(
            input_z, input_zc, sums, send_own, send_other
        )
        unit_sum, unit_z = small_kernel(
            fold_shards_kernel,
            "fold_shards",
            (((2 * part, model), F32), ((2 * part, model), BF16)),
            (),
            kept_own,
            send_own,
            kept_other,
            send_other,
        )
        unit_z, input_zc, sums = stage(unit_z, input_zc, sums)
        unit_z = over_z(unit_z)
        input_zc = over_core(input_zc)
        mine, theirs = small_kernel(
            input_own_kernel,
            "input_own",
            (((rows, model), F32), ((rows, model), BF16)),
            (flags,),
            dq_own,
            dq_core,
            sums,
            weights,
            dresid,
            cotangent,
        )
        packed = weight_grads(
            group,
            (dq_own, dq_core, dq_z, dq_zc),
            sums,
            context_own,
            dresid_low,
            dresid_core,
            out_grad_other,
            small,
        )
        packed, input_z, input_zc, mine, theirs = stage(packed, input_z, input_zc, mine, theirs)
        input_z = small_kernel(
            fold_inputs_kernel, "fold_inputs", (((rows, model), BF16),), (), input_z, input_zc
        )[0]
        input_z, packed, theirs, unit_z = stage(input_z, packed, theirs, unit_z)
        input_other = over_z(input_z)
        parted = lax.all_to_all(packed, ("y", "x"), split_axis=0, concat_axis=0, tiled=True)
        theirs = over_core(theirs)
        unit_home = small_kernel(
            fold_z_kernel,
            "fold_z",
            (((part, model), F32), ((part, model), BF16), ((part, model), BF16)),
            (flags,),
            unit_sum,
            unit_z,
        )
        mine, theirs, *unit_home = stage(mine, theirs, *unit_home)
        unit_home = home(unit_home)

        parted, input_other, mine, theirs, *unit_home = stage(
            parted, input_other, mine, theirs, *unit_home
        )
        head_home = small_kernel(
            fold_parts_kernel,
            "fold_parts",
            (
                ((width // 2 + 16, model), F32),
                ((width // 2 + 16, model), BF16),
                ((width // 2 + 16, model), BF16),
            ),
            (flags,),
            parted,
        )
        mine, theirs, kept, send, far, *head_home = stage(mine, theirs, *unit_home, *head_home)
        head_home = home(head_home)
        unit_all = over_plane(fold_home("fold_units", (kept, send, far)))
        mine, theirs, input_other = stage(mine, theirs, input_other)
        tokens_grad = small_kernel(
            add_tokens_kernel,
            "add_tokens",
            (((rows, model), BF16),),
            (),
            mine,
            theirs,
            input_other,
        )[0]
        tokens_grad, *head_home = stage(tokens_grad, *head_home)
        tokens_grad = swap(tokens_grad)
        heads = fold_home("fold_heads", head_home, F32)
        heads, unit_all = stage(heads, unit_all)
        head_all = over_plane(heads[: width // 2].astype(BF16))
        small = heads[width // 2 :]
        up_bias_sum = lax.dynamic_slice_in_dim(small[6:10], t, 1, 0)[0]
        unit_other = over_core(unit_all)
        up_sum, down_sum = small_kernel(
            unit_results_kernel,
            "unit_results",
            (((model, 4 * part), F32), ((4 * part, model), F32)),
            (flags,),
            unit_all,
            unit_other,
        )
        head_all, up_sum, down_sum, tokens_grad, small, up_bias_sum = stage(
            head_all, up_sum, down_sum, tokens_grad, small, up_bias_sum
        )
        head_other = over_core(head_all)
        sums = small_kernel(
            head_results_kernel,
            "head_results",
            (((width, model), F32),) * 4 + (((rows, model), BF16),) * 2,
            (flags,),
            head_all,
            head_other,
            layer_out,
            tokens_grad,
        )
        layer_out, tokens_grad = sums[4:]
        narrow = small[12, :width], small[12, width : 2 * width]

        return (
            layer_out,
            tokens_grad,
            sums[0].T,
            narrow[0],
            sums[1].T,
            sums[2].T,
            narrow[1],
            sums[3],
            small[0],
            small[1],
            small[2],
            up_sum,
            up_bias_sum,
            down_sum,
            small[3],
            small[4],
            small[5],
        )

    return jax.shard_map(
        shards,
        mesh=fine,
        in_specs=(
            P(AXES, None),
            P(AXES, None),
            P(DP, None),
            P(DP),
            P(None, "tensor"),
            P("tensor"),
            P(None, "tensor"),
            P(None, "tensor"),
            P("tensor"),
            P("tensor", None),
            P(),
            P(),
            P(),
            P(None, "tensor"),
            P("tensor"),
            P("tensor", None),
            P(),
            P(),
            P(),
        ),
        out_specs=(
            P(AXES, None),
            P(AXES, None),
            P(None, "tensor"),
            P("tensor"),
            P(None, "tensor"),
            P(None, "tensor"),
            P("tensor"),
            P("tensor", None),
            P(),
            P(),
            P(),
            P(None, "tensor"),
            P("tensor"),
            P("tensor", None),
            P(),
            P(),
            P(),
        ),
        check_vma=False,
    )
```

```python
import functools

import jax
import jax.numpy as jnp
from jax import lax
from jax.experimental import pallas as pl
from jax.experimental.pallas import tpu as pltpu
from jax.sharding import Mesh
from jax.sharding import PartitionSpec as P

HEAD_DIM = 64
QUERIES, KEYS = 512, 256
EPS = 1e-05
NEG = -1e30
F32 = jnp.float32
BF16 = jnp.bfloat16
SMEM = pl.BlockSpec(memory_space=pltpu.SMEM)
VMEM = pl.BlockSpec(memory_space=pltpu.VMEM)
SHAPE = jax.ShapeDtypeStruct


def matmul(left, right):
    return jnp.dot(left, right, preferred_element_type=F32)


def matmul_left(left, right):
    return lax.dot_general(left, right, (((0,), (0,)), ((), ())), preferred_element_type=F32)


def matmul_right(left, right):
    return lax.dot_general(left, right, (((1,), (1,)), ((), ())), preferred_element_type=F32)


def stage(*values):
    return lax.optimization_barrier(values)


def cost(micros):
    return pl.CostEstimate(flops=int(micros * 1e9), bytes_accessed=1 << 12, transcendentals=0)


def room(mebibytes):
    return pltpu.CompilerParams(vmem_limit_bytes=mebibytes << 20)


def head_parts(width):
    return [slice(h, h + HEAD_DIM) for h in range(0, width, HEAD_DIM)]


def attend_forward_kernel(
    bq,
    bk,
    first,
    qlow_ref,
    qhigh_ref,
    klow_ref,
    khigh_ref,
    qkv_ref,
    row_ref,
    column_ref,
    wide_ref,
    context_ref,
    totals_ref,
    top_ref,
    sum_ref,
    acc_ref,
):
    width, count = wide_ref.shape
    length = qkv_ref.shape[1]
    parts = head_parts(width)
    heads = range(len(parts))
    key_parts = head_parts(2 * width)[len(parts) :]
    value_parts = head_parts(3 * width)[2 * len(parts) :]

    def over_query(i, _):
        at_o = pl.ds(pl.multiple_of(i * bq, bq), bq)
        at_q = pl.ds(pl.multiple_of(first + i * bq, bq), bq)
        block = i + first // bq
        top_ref[...] = jnp.full(top_ref.shape, NEG, F32)
        sum_ref[...] = jnp.zeros(sum_ref.shape, F32)
        acc_ref[...] = jnp.zeros(acc_ref.shape, F32)
        row = row_ref[0:1, at_q]

        def over_keys(j, _):
            @pl.when((klow_ref[j] <= qhigh_ref[block]) & (qlow_ref[block] <= khigh_ref[j]))
            def _():
                at_k = pl.ds(pl.multiple_of(j * bk, bk), bk)
                column = column_ref[at_k, :]
                same = jnp.concatenate([column] * (bq // 128), 1) == row
                scores = [
                    matmul_left(qkv_ref[k, at_k], qkv_ref[q, at_q])
                    for k, q in zip(key_parts, parts)
                ]
                scores = [jnp.where(same, value, NEG) for value in scores]
                old = [top_ref[h : h + 1, :] for h in heads]
                top = [jnp.maximum(o, jnp.max(v, 0, keepdims=True)) for o, v in zip(old, scores)]
                exponent = [jnp.exp(v - m) for v, m in zip(scores, top)]
                scale = [jnp.exp(o - m) for o, m in zip(old, top)]
                total = [
                    sum_ref[h : h + 1, :] * scale[h] + jnp.sum(exponent[h], 0, keepdims=True)
                    for h in heads
                ]
                added = [
                    matmul(qkv_ref[v, at_k], e.astype(BF16)) for v, e in zip(value_parts, exponent)
                ]
                added = [acc_ref[p, :] * c + v for p, c, v in zip(parts, scale, added)]
                for h in heads:
                    top_ref[h : h + 1, :] = top[h]
                    sum_ref[h : h + 1, :] = total[h]
                    acc_ref[parts[h], :] = added[h]

            return 0

        lax.fori_loop(0, length // bk, over_keys, 0)
        for h in heads:
            value = acc_ref[parts[h], :] / sum_ref[h : h + 1, :]
            wide_ref[parts[h], at_o] = value
            context_ref[parts[h], at_o] = value.astype(BF16)
            totals_ref[h : h + 1, at_o] = top_ref[h : h + 1, :] + jnp.log(sum_ref[h : h + 1, :])
        return 0

    lax.fori_loop(0, count // bq, over_query, 0)


def attend_backward_kernel(
    bq,
    bk,
    first,
    base,
    follows,
    qlow_ref,
    qhigh_ref,
    klow_ref,
    khigh_ref,
    qkv_ref,
    dcontext_ref,
    wide_ref,
    totals_ref,
    row_ref,
    column_ref,
    *rest,
):
    if follows:
        before_ref, dquery_ref, sums_ref, delta_ref, dq_ref, dk_ref, dv_ref = rest
    else:
        dquery_ref, sums_ref, delta_ref, dq_ref, dk_ref, dv_ref = rest
    width, count = dquery_ref.shape
    length = qkv_ref.shape[1]
    parts = head_parts(width)
    heads = range(len(parts))
    key_parts = head_parts(2 * width)[len(parts) :]
    value_parts = head_parts(3 * width)[2 * len(parts) :]
    dq_ref[...] = jnp.zeros(dq_ref.shape, F32)
    chunk = slice(base, base + count)
    for h in heads:
        delta_ref[h : h + 1, :] = jnp.sum(
            wide_ref[parts[h], chunk] * dcontext_ref[parts[h], chunk].astype(F32), 0, keepdims=True
        )

    def over_keys(j, _):
        at_k = pl.ds(pl.multiple_of(j * bk, bk), bk)
        if follows:
            dk_ref[...] = before_ref[0:width, at_k]
            dv_ref[...] = before_ref[width : 2 * width, at_k]
        else:
            dk_ref[...] = jnp.zeros(dk_ref.shape, F32)
            dv_ref[...] = jnp.zeros(dv_ref.shape, F32)

        def over_query(i, _):
            block = i + first // bq

            @pl.when((klow_ref[j] <= qhigh_ref[block]) & (qlow_ref[block] <= khigh_ref[j]))
            def _():
                at_o = pl.ds(pl.multiple_of(i * bq, bq), bq)
                at_b = pl.ds(pl.multiple_of(base + i * bq, bq), bq)
                at_q = pl.ds(pl.multiple_of(first + i * bq, bq), bq)
                column = column_ref[at_k, :]
                same = jnp.concatenate([column] * (bq // 128), 1) == row_ref[0:1, at_q]
                scores = [
                    matmul_left(qkv_ref[k, at_k], qkv_ref[q, at_q])
                    for k, q in zip(key_parts, parts)
                ]
                dprobs = [
                    matmul_left(qkv_ref[v, at_k], dcontext_ref[p, at_b])
                    for v, p in zip(value_parts, parts)
                ]
                probs = [
                    jnp.exp(jnp.where(same, scores[h], NEG) - totals_ref[h : h + 1, at_b])
                    for h in heads
                ]
                dscores = [
                    (probs[h] * (dprobs[h] - delta_ref[h : h + 1, at_o])).astype(BF16)
                    for h in heads
                ]
                dv = [
                    matmul_right(dcontext_ref[p, at_b], v.astype(BF16)) for p, v in zip(parts, probs)
                ]
                dk = [matmul_right(qkv_ref[p, at_q], v) for p, v in zip(parts, dscores)]
                dq = [matmul(qkv_ref[k, at_k], v) for k, v in zip(key_parts, dscores)]
                for h in heads:
                    dv_ref[parts[h], :] += dv[h]
                    dk_ref[parts[h], :] += dk[h]
                    dq_ref[parts[h], at_o] += dq[h]

            return 0

        lax.fori_loop(0, count // bq, over_query, 0)
        sums_ref[0:width, at_k] = dk_ref[...].astype(sums_ref.dtype)
        sums_ref[width : 2 * width, at_k] = dv_ref[...].astype(sums_ref.dtype)
        return 0

    lax.fori_loop(0, length // bk, over_keys, 0)
    dquery_ref[...] = dq_ref[...].astype(BF16)


def bounds(segment, block):
    blocks = segment.reshape(-1, block)
    return jnp.min(blocks, 1), jnp.max(blocks, 1)


def attend_forward(qkv, marks, first, count):
    width = qkv.shape[0] // 3
    wide_low, wide_high, low, high, row, column = marks
    bq, bk = QUERIES, KEYS
    return pl.pallas_call(
        functools.partial(attend_forward_kernel, bq, bk, first),
        out_shape=(SHAPE((width, count), F32), SHAPE((width, count), BF16), SHAPE((8, count), F32)),
        in_specs=[SMEM] * 4 + [VMEM] * 3,
        out_specs=(VMEM,) * 3,
        scratch_shapes=[pltpu.VMEM((8, bq), F32)] * 2 + [pltpu.VMEM((width, bq), F32)],
        cost_estimate=cost(15),
        compiler_params=room(16),
        name="attend_forward",
    )(wide_low, wide_high, low, high, qkv, row, column)


def attend_backward(qkv, around, marks, first, base, count, before, kind):
    dcontext, wide, totals = around
    width, length = dcontext.shape[0], qkv.shape[1]
    _, _, low, high, row, column = marks
    bq = bk = KEYS
    follows = before is not None
    return pl.pallas_call(
        functools.partial(attend_backward_kernel, bq, bk, first, base, follows),
        out_shape=(SHAPE((width, count), BF16), SHAPE((2 * width, length), kind)),
        in_specs=[SMEM] * 4 + [VMEM] * (7 if follows else 6),
        out_specs=(VMEM,) * 2,
        scratch_shapes=[
            pltpu.VMEM((8, count), F32),
            pltpu.VMEM((width, count), F32),
            pltpu.VMEM((width, bk), F32),
            pltpu.VMEM((width, bk), F32),
        ],
        cost_estimate=cost(count // 64),
        compiler_params=room(22),
        name="attend_backward",
    )(
        low,
        high,
        low,
        high,
        qkv,
        dcontext,
        wide,
        totals,
        row,
        column,
        *((before,) if follows else ()),
    )


def plane_slots(flags_ref, slots):
    slots = [jnp.where(flags_ref[2] == 1, slots[k ^ 1], slots[k]) for k in range(4)]
    return [jnp.where(flags_ref[3] == 1, slots[k ^ 2], slots[k]) for k in range(4)]


def feed_forward_kernel(flags_ref, own_ref, core_ref, *rest):
    pieces, (hidden_ref, slope_ref, mine_ref, other_ref, up_ref, down_ref) = rest[:-6], rest[-6:]
    rows, cols = own_ref.shape[0], 256
    part = up_ref.shape[0] // 8
    for n in range(2):
        for k in range(4):
            to = slice((2 * k + n) * part, (2 * k + n + 1) * part)
            if n == 1 and k == 3:
                up, down = pieces[7][...], pieces[8][...]
            else:
                up, down = pieces[4 * n + k][0:part, :], pieces[4 * n + k][part : 2 * part, :]
            if n == 0 and k > 0:
                up = up + pieces[9][k - 1, 0:part, :]
                down = down + pieces[9][k - 1, part : 2 * part, :]
            up_ref[to, :] = up
            down_ref[to, :] = down
    biases = []
    for n in range(2):
        value = pieces[4 * n][2 * part : 2 * part + 16, :].astype(F32)[0:1]
        biases.append(plane_slots(flags_ref, [value[:, k * part : (k + 1) * part] for k in range(4)]))
    biases = jnp.concatenate([biases[n][k] for k in range(4) for n in range(2)], 1)
    for source, target, start in ((core_ref, other_ref, rows), (own_ref, mine_ref, 0)):
        at = slice(start, start + rows)
        value = source[...]
        for n in range(0, up_ref.shape[0], cols):
            to = slice(n, n + cols)
            pre = matmul_right(value, up_ref[to, :]) + biases[:, to]
            normal = 0.5 * (1.0 + lax.erf(pre * 0.7071067811865476))
            hidden_ref[at, to] = (pre * normal).astype(BF16)
            density = jnp.exp(-0.5 * pre * pre) * 0.3989422804014327
            slope_ref[at, to] = (normal + pre * density).astype(BF16)
        target[...] = matmul(hidden_ref[at, :], down_ref[...]).astype(target.dtype)


def feed_forward(flags, own, core, pieces):
    rows, model = own.shape
    units = 2 * model
    return pl.pallas_call(
        feed_forward_kernel,
        out_shape=(
            SHAPE((2 * rows, units), BF16),
            SHAPE((2 * rows, units), BF16),
            SHAPE((rows, model), F32),
            SHAPE((rows, model), BF16),
            SHAPE((units, model), BF16),
            SHAPE((units, model), BF16),
        ),
        in_specs=[SMEM] + [VMEM] * 12,
        out_specs=(VMEM,) * 6,
        cost_estimate=cost(12),
        compiler_params=room(32),
        name="feed_forward",
    )(flags, own, core, *pieces)


def hidden_back_kernel(
    own_ref, core_ref, slope_ref, up_ref, down_ref, dpre_ref, mine_ref, other_ref, bias_ref
):
    rows, cols = own_ref.shape[0], 256
    for source, target, start in ((core_ref, other_ref, rows), (own_ref, mine_ref, 0)):
        at = slice(start, start + rows)
        value = source[...]
        for n in range(0, up_ref.shape[0], cols):
            to = slice(n, n + cols)
            dhidden = matmul_right(value, down_ref[to, :])
            dpre_ref[at, to] = (dhidden * slope_ref[at, to].astype(F32)).astype(BF16)
        target[...] = matmul(dpre_ref[at, :], up_ref[...]).astype(target.dtype)
    bias_ref[...] = matmul(jnp.ones((8, 2 * rows), BF16), dpre_ref[...])


def hidden_back(own, core, slope, up, down):
    rows, model = own.shape
    units = up.shape[0]
    return pl.pallas_call(
        hidden_back_kernel,
        out_shape=(
            SHAPE((2 * rows, units), BF16),
            SHAPE((rows, model), F32),
            SHAPE((rows, model), BF16),
            SHAPE((8, units), F32),
        ),
        in_specs=[VMEM] * 5,
        out_specs=(VMEM,) * 4,
        cost_estimate=cost(0),
        compiler_params=room(26),
        name="hidden_back",
    )(own, core, slope, up, down)


def unit_grads_kernel(
    dpre_ref, normed_ref, normed_core_ref, hidden_ref, dffn_ref, dffn_core_ref, *refs
):
    rows = normed_ref.shape[0]
    part = dpre_ref.shape[1] // 8
    places = ((0, 0), (1, 0), (0, 1), (1, 1)), ((0, 0), (0, 1), (1, 0), (1, 1))
    halves = (dpre_ref, normed_ref, normed_core_ref), (hidden_ref, dffn_ref, dffn_core_ref)
    for m, (left_ref, own_ref, core_ref) in enumerate(halves):
        for k in range(4):
            at = slice(2 * k * part, 2 * (k + 1) * part)
            total = matmul_left(left_ref[0:rows, at], own_ref[...])
            total = total + matmul_left(left_ref[rows : 2 * rows, at], core_ref[...])
            for n in range(2):
                sent, slot = places[n][k]
                to = slice((2 * m + slot) * part, (2 * m + slot + 1) * part)
                refs[2 * n + sent][to, :] = total[n * part : (n + 1) * part].astype(BF16)


def unit_grads(dpre, normed, normed_core, hidden, dffn, dffn_core):
    return pl.pallas_call(
        unit_grads_kernel,
        out_shape=(SHAPE((dpre.shape[1] // 2, normed.shape[1]), BF16),) * 4,
        in_specs=[VMEM] * 6,
        out_specs=(VMEM,) * 4,
        cost_estimate=cost(5),
        compiler_params=room(24),
        name="unit_grads",
    )(dpre, normed, normed_core, hidden, dffn, dffn_core)


def out_project_kernel(own_ref, other_ref, own_w_ref, other_w_ref, mine_ref, theirs_ref):
    rows = mine_ref.shape[0]
    for target, at in ((theirs_ref, slice(rows, 2 * rows)), (mine_ref, slice(0, rows))):
        value = matmul_left(own_ref[:, at], own_w_ref[...])
        value = value + matmul_left(other_ref[:, at], other_w_ref[...])
        target[...] = value.astype(target.dtype)


def out_project(own, other, own_weight, other_weight):
    rows, model = own.shape[1] // 2, own_weight.shape[1]
    return pl.pallas_call(
        out_project_kernel,
        out_shape=(SHAPE((rows, model), F32), SHAPE((rows, model), BF16)),
        in_specs=[VMEM] * 4,
        out_specs=(VMEM,) * 2,
        cost_estimate=cost(3),
        compiler_params=room(12),
        name="out_project",
    )(own, other, own_weight, other_weight)


def input_back_kernel(start, first_ref, second_ref, sums_ref, weights_ref, mine_ref, theirs_ref):
    rows = first_ref.shape[1]
    width = first_ref.shape[0]
    query_weights = weights_ref[0:width, :] * 0.125
    for k, ref, target in ((1, second_ref, theirs_ref), (0, first_ref, mine_ref)):
        at = slice(start + k * rows, start + (k + 1) * rows)
        value = matmul_left(ref[...], query_weights)
        value = value + matmul_left(sums_ref[:, at], weights_ref[width:, :])
        target[...] = value.astype(target.dtype)


def input_back(start, first, second, sums, weights):
    shape = (first.shape[1], weights.shape[1])
    return pl.pallas_call(
        functools.partial(input_back_kernel, start),
        out_shape=(SHAPE(shape, F32), SHAPE(shape, BF16)),
        in_specs=[VMEM] * 4,
        out_specs=(VMEM,) * 2,
        cost_estimate=cost(0),
        compiler_params=room(14),
        name="input_back",
    )(first, second, sums, weights)


def input_own_kernel(
    flags_ref,
    first_ref,
    second_ref,
    sums_ref,
    weights_ref,
    dresid_ref,
    cotangent_ref,
    mine_ref,
    theirs_ref,
):
    width, rows = first_ref.shape
    query_weights = weights_ref[0:width, :] * 0.125
    for k, ref in ((1, second_ref), (0, first_ref)):
        at = slice(k * rows, (k + 1) * rows)
        value = matmul_left(ref[...], query_weights)
        value = value + matmul_left(sums_ref[:, at], weights_ref[width:, :])
        if k == 1:
            theirs_ref[...] = value.astype(BF16)
        else:
            skipped = (1 - flags_ref[1]).astype(F32)
            mine_ref[...] = value + dresid_ref[...] + skipped * cotangent_ref[...].astype(F32)


def context_back_kernel(
    own_ref,
    core_ref,
    small_ref,
    own_w_ref,
    other_w_ref,
    context_ref,
    mine_ref,
    theirs_ref,
    grad_ref,
    sum_ref,
):
    rows = own_ref.shape[0] - 16
    width = mine_ref.shape[0]
    grad = 0.0
    for k, ref in enumerate((own_ref, core_ref)):
        at = slice(k * rows, (k + 1) * rows)
        value = ref[0:rows, :]
        theirs_ref[:, at] = matmul_right(other_w_ref[...], value).astype(BF16)
        mine_ref[:, at] = matmul_right(own_w_ref[...], value).astype(BF16)
        grad = grad + matmul(context_ref[:, at], value)
    grad_ref[0:width, :] = grad.astype(BF16)
    total = small_ref[...] + core_ref[rows : rows + 16, :].astype(F32)
    sum_ref[...] = total
    grad_ref[width : width + 16, :] = total.astype(BF16)


def take_kernel(
    flags_ref,
    query_ref,
    key_ref,
    value_ref,
    extra_ref,
    up_ref,
    down_ref,
    piece_ref,
    quarter_ref,
    local_ref,
    turned_ref,
):
    place = flags_ref[0]
    held = 1.0 - flags_ref[1].astype(F32)
    fourth = query_ref.shape[0] // 4
    for n, ref in enumerate((query_ref, key_ref, value_ref)):
        at = pl.ds(pl.multiple_of(place * fourth, fourth), fourth)
        piece_ref[n * fourth : (n + 1) * fourth, :] = ref[at, :]
    piece_ref[3 * fourth :, :] = extra_ref[0:16, :]
    turned_ref[...] = up_ref[...].T
    part = local_ref.shape[1] // 2
    quarter_ref[2 * part :, :] = extra_ref[16:32, :]
    for k in range(4):
        at = pl.ds(pl.multiple_of((place ^ k) * part, part), part)
        if k == 0:
            quarter_ref[0:part, :] = turned_ref[at, :]
            quarter_ref[part : 2 * part, :] = down_ref[at, :]
        else:
            local_ref[k - 1, 0:part, :] = (turned_ref[at, :] * held).astype(BF16)
            local_ref[k - 1, part : 2 * part, :] = (down_ref[at, :] * held).astype(BF16)


def take(place, heads, extra, up, down):
    units, model = down.shape
    rows = heads[0].shape[0] // 4 * 3 + 16
    return pl.pallas_call(
        take_kernel,
        out_shape=(
            SHAPE((rows, model), BF16),
            SHAPE((units // 2 + 16, model), BF16),
            SHAPE((3, units // 2, model), BF16),
        ),
        in_specs=[SMEM] + [VMEM] * 6,
        out_specs=(VMEM,) * 3,
        scratch_shapes=[pltpu.VMEM((units, model), BF16)],
        cost_estimate=cost(20),
        compiler_params=room(14),
        name="take",
    )(place, *heads, extra, up, down)


def small_kernel(kernel, name, results, flags, *operands, mebibytes=16):
    return pl.pallas_call(
        kernel,
        out_shape=tuple(SHAPE(shape, kind) for shape, kind in results),
        in_specs=[SMEM] * len(flags) + [VMEM] * len(operands),
        out_specs=(VMEM,) * len(results),
        cost_estimate=cost(0),
        compiler_params=room(mebibytes),
        name=name,
    )(*flags, *operands)


def fold_plane_kernel(*refs):
    part = refs[0].shape[0] // 4
    for n in range(2):
        keep_ref, got_ref = refs[2 * n], refs[2 * n + 1]
        kept_ref, send_ref = refs[4 + 2 * n], refs[5 + 2 * n]
        for m in range(2):
            at = slice(m * part, (m + 1) * part)
            kept, sent = (
                keep_ref[k * part : (k + 1) * part, :].astype(F32)
                + got_ref[k * part : (k + 1) * part, :].astype(F32)
                for k in (2 * m, 2 * m + 1)
            )
            kept_ref[at, :] = kept
            send_ref[at, :] = sent.astype(BF16)


def fold_shards_kernel(own_ref, own_got_ref, other_ref, other_got_ref, sum_ref, send_ref):
    sum_ref[...] = own_ref[...] + own_got_ref[...].astype(F32)
    send_ref[...] = (other_ref[...] + other_got_ref[...].astype(F32)).astype(BF16)


def split_home(flags_ref, value, kept_ref, send_ref, far_ref):
    half = kept_ref.shape[0]
    kept_ref[...] = value[:half]
    far_ref[...] = value[half:].astype(BF16)

    @pl.when(flags_ref[0] == 1)
    def _():
        send_ref[...] = value[:half].astype(BF16)

    @pl.when(flags_ref[0] == 0)
    def _():
        send_ref[...] = value[half:].astype(BF16)


def fold_z_kernel(flags_ref, sum_ref, got_ref, kept_ref, send_ref, far_ref):
    split_home(flags_ref, sum_ref[...] + got_ref[...].astype(F32), kept_ref, send_ref, far_ref)


def fold_parts_kernel(flags_ref, parts_ref, kept_ref, send_ref, far_ref):
    value = parts_ref[0].astype(F32) + parts_ref[1].astype(F32)
    value = value + (parts_ref[2].astype(F32) + parts_ref[3].astype(F32))
    half = kept_ref.shape[0] - 16
    tail = value[2 * half :]
    kept_ref[0:half, :] = value[:half]
    kept_ref[half:, :] = tail
    far_ref[0:half, :] = value[half : 2 * half].astype(BF16)
    far_ref[half:, :] = tail.astype(BF16)
    send_ref[half:, :] = tail.astype(BF16)

    @pl.when(flags_ref[0] == 1)
    def _():
        send_ref[0:half, :] = value[:half].astype(BF16)

    @pl.when(flags_ref[0] == 0)
    def _():
        send_ref[0:half, :] = value[half : 2 * half].astype(BF16)


def fold_inputs_kernel(mine_ref, theirs_ref, result_ref):
    result_ref[...] = (mine_ref[...] + theirs_ref[...].astype(F32)).astype(BF16)


def add_tokens_kernel(mine_ref, theirs_ref, other_ref, result_ref):
    other = theirs_ref[...].astype(F32) + other_ref[...].astype(F32)
    result_ref[...] = (mine_ref[...] + other).astype(BF16)


def fold_home_kernel(flags_ref, kept_ref, got_ref, far_ref, result_ref):
    got = got_ref[...].astype(F32)
    first = jnp.where(flags_ref[0] == 1, far_ref[...].astype(F32), kept_ref[...])
    result_ref[...] = (first + got).astype(result_ref.dtype)


def unit_results_kernel(flags_ref, mine_ref, other_ref, up_ref, down_ref):
    def put(first_ref, second_ref):
        part = first_ref.shape[1]
        for k in range(4):
            down_ref[k * part : (k + 1) * part, :] = second_ref[k].astype(F32)
        up_ref[...] = first_ref[...].reshape(4 * part, first_ref.shape[2]).astype(F32).T

    @pl.when(flags_ref[0] == 1)
    def _():
        put(other_ref, mine_ref)

    @pl.when(flags_ref[0] == 0)
    def _():
        put(mine_ref, other_ref)


def head_results_kernel(flags_ref, mine_ref, other_ref, layer_ref, tokens_ref, *results):
    half = mine_ref.shape[1]
    results[4][...] = layer_ref[...]
    results[5][...] = tokens_ref[...]
    for k, ref in enumerate(results[:4]):
        mine, other = mine_ref[k].astype(F32), other_ref[k].astype(F32)
        ref[0:half, :] = jnp.where(flags_ref[0] == 1, other, mine)
        ref[half : 2 * half, :] = jnp.where(flags_ref[0] == 1, mine, other)


def normal_rows(value):
    center = value - jnp.mean(value, -1, keepdims=True)
    root = lax.rsqrt(jnp.mean(center * center, -1, keepdims=True) + EPS)
    return center * root, root


def normal_back(grad, normal, root):
    inner = jnp.mean(grad * normal, -1, keepdims=True)
    return root * (grad - jnp.mean(grad, -1, keepdims=True) - normal * inner)


STEP = 128


def first_norm_kernel(mine_ref, got_ref, token_ref, vector_ref, resid_ref, normed_ref, low_ref):
    def step(k, _):
        at = pl.ds(pl.multiple_of(k * STEP, STEP), STEP)
        attention = mine_ref[at, :] + got_ref[at, :].astype(F32)
        resid = token_ref[at, :].astype(F32) + attention + vector_ref[0:1, :]
        resid_ref[at, :] = resid
        normed = normal_rows(resid)[0] * vector_ref[1:2, :] + vector_ref[2:3, :]
        normed_ref[at, :] = normed
        low_ref[at, :] = normed.astype(BF16)
        return 0

    lax.fori_loop(0, mine_ref.shape[0] // STEP, step, 0)


def second_norm_kernel(
    flags_ref,
    mine_ref,
    got_ref,
    normed_ref,
    cotangent_ref,
    token_ref,
    vector_ref,
    layer_ref,
    dsummed_ref,
    low_ref,
    sums_ref,
):
    keep = flags_ref[1].astype(F32)
    sums_ref[...] = jnp.zeros(sums_ref.shape, F32)

    def step(k, _):
        at = pl.ds(pl.multiple_of(k * STEP, STEP), STEP)
        units = mine_ref[at, :] + got_ref[at, :].astype(F32)
        normal, root = normal_rows(normed_ref[at, :] + units + vector_ref[0:1, :])
        final = normal * vector_ref[1:2, :] + vector_ref[2:3, :]
        token = token_ref[at, :].astype(F32)
        layer_ref[at, :] = (keep * final + (1.0 - keep) * token).astype(BF16)
        cotangent = cotangent_ref[at, :].astype(F32)
        dfinal = keep * cotangent
        dsummed = normal_back(dfinal * vector_ref[1:2, :], normal, root)
        dsummed_ref[at, :] = dsummed
        low_ref[at, :] = dsummed.astype(BF16)
        sums_ref[0:1, :] += jnp.sum(dsummed, 0, keepdims=True)
        sums_ref[1:2, :] += jnp.sum(dfinal * normal, 0, keepdims=True)
        sums_ref[2:3, :] += jnp.sum(dfinal, 0, keepdims=True)
        return 0

    lax.fori_loop(0, mine_ref.shape[0] // STEP, step, 0)


def first_norm_back_kernel(
    flags_ref,
    mine_ref,
    got_ref,
    dsummed_ref,
    resid_ref,
    vector_ref,
    ffn_ref,
    bias_ref,
    dresid_ref,
    low_ref,
    small_ref,
):
    rows, model = mine_ref.shape
    part = model // 4
    small_ref[...] = jnp.zeros(small_ref.shape, F32)

    def step(k, _):
        at = pl.ds(pl.multiple_of(k * STEP, STEP), STEP)
        dnormed = dsummed_ref[at, :] + (mine_ref[at, :] + got_ref[at, :].astype(F32))
        normal, root = normal_rows(resid_ref[at, :])
        dresid = normal_back(dnormed * vector_ref[1:2, :], normal, root)
        dresid_ref[at, :] = dresid
        low_ref[at, :] = dresid.astype(BF16)
        small_ref[0:1, :] += jnp.sum(dresid, 0, keepdims=True)
        small_ref[1:2, :] += jnp.sum(dnormed * normal, 0, keepdims=True)
        small_ref[2:3, :] += jnp.sum(dnormed, 0, keepdims=True)
        return 0

    lax.fori_loop(0, rows // STEP, step, 0)
    small_ref[3:6, :] = ffn_ref[0:3, :]
    wide = 0.0
    for n in range(2):
        slots = [bias_ref[0:1, (2 * k + n) * part : (2 * k + n + 1) * part] for k in range(4)]
        value = jnp.concatenate(plane_slots(flags_ref, slots), 1)
        at = lax.broadcasted_iota(jnp.int32, (4, model), 0) == (flags_ref[4] ^ n)
        wide = wide + jnp.where(at, value, 0.0)
    small_ref[6:10, :] = wide
    low_ref[rows : rows + 16, :] = small_ref[...].astype(BF16)


def vectors(bias, gain, shift):
    return jnp.concatenate([jnp.stack([bias, gain, shift]), jnp.zeros((5,) + bias.shape)]).astype(F32)


def rowwise(kernel, name, kinds, flags, *operands):
    shape = operands[0].shape
    results = tuple(SHAPE(shape if kind else (8, shape[1]), kind or F32) for kind in kinds)
    return pl.pallas_call(
        kernel,
        out_shape=results,
        in_specs=[SMEM] * len(flags) + [VMEM] * len(operands),
        out_specs=(VMEM,) * len(results),
        cost_estimate=cost(2),
        compiler_params=room(16),
        name=name,
    )(*flags, *operands)


def project_kernel(own_ref, core_ref, z_ref, zc_ref, gathered_ref, qkv_ref, weights_ref):
    rows = own_ref.shape[0]
    fourth = weights_ref.shape[0] // 4
    width = weights_ref.shape[0] // 3
    for k in range(4):
        for n in range(3):
            piece = fourth // 3
            to = slice(n * width + k * piece, n * width + (k + 1) * piece)
            weights_ref[to, :] = gathered_ref[k, n * piece : (n + 1) * piece, :]
    weights = weights_ref[...]
    biases = gathered_ref[0, fourth : fourth + 16, 0 : 3 * width]
    first = lax.broadcasted_iota(jnp.int32, (16, rows), 0) == 0
    columns = matmul_left(biases, jnp.where(first, 1.0, 0.0).astype(BF16))
    for k, ref in enumerate((own_ref, core_ref, z_ref, zc_ref)):
        at = slice(k * rows, (k + 1) * rows)
        value = matmul_right(weights, ref[...]) + columns
        qkv_ref[0:width, at] = (value[:width] * 0.125).astype(BF16)
        qkv_ref[width:, at] = value[width:].astype(BF16)


def project(tokens, gathered):
    rows, model = tokens[0].shape
    units = 4 * (gathered.shape[1] - 16)
    return pl.pallas_call(
        project_kernel,
        out_shape=(SHAPE((units, 4 * rows), BF16), SHAPE((units, model), BF16)),
        in_specs=[VMEM] * 5,
        out_specs=(VMEM,) * 2,
        cost_estimate=cost(4),
        compiler_params=room(20),
        name="project",
    )(*tokens, gathered)


def weight_grads_kernel(
    own_ref,
    core_ref,
    z_ref,
    zc_ref,
    dq_own_ref,
    dq_core_ref,
    dq_z_ref,
    dq_zc_ref,
    sums_ref,
    context_ref,
    dresid_ref,
    dresid_core_ref,
    other_ref,
    small_ref,
    packed_ref,
):
    rows = own_ref.shape[0]
    width = dq_own_ref.shape[0]
    tokens = (own_ref, core_ref, z_ref, zc_ref)
    dquery = (dq_own_ref, dq_core_ref, dq_z_ref, dq_zc_ref)
    total, query, bias = 0.0, 0.0, 0.0
    count = jnp.ones((8, rows), BF16)
    for k in range(4):
        value = tokens[k][...]
        query = query + matmul(dquery[k][...], value)
        total = total + matmul(sums_ref[:, k * rows : (k + 1) * rows], value)
        bias = bias + matmul_right(count, dquery[k][...])
    packed_ref[0, 0:width, :] = (query * 0.125).astype(BF16)
    packed_ref[1, 0:width, :] = total[:width].astype(BF16)
    packed_ref[2, 0:width, :] = total[width:].astype(BF16)
    out = matmul(context_ref[:, 0:rows], dresid_ref[0:rows, :])
    out = out + matmul(context_ref[:, rows : 2 * rows], dresid_core_ref[0:rows, :])
    packed_ref[3, 0:width, :] = (out + other_ref[0:width, :].astype(F32)).astype(BF16)
    small = small_ref[...] + other_ref[width : width + 16, :].astype(F32)
    count = jnp.ones((8, 4 * rows), BF16)
    values = matmul_right(count, sums_ref[width : 2 * width, :])
    biases = jnp.concatenate([bias * 0.125, values, jnp.zeros_like(bias), jnp.zeros_like(bias)], 1)
    at_row = lax.broadcasted_iota(jnp.int32, (8, 4 * width), 0) == 4
    late = jnp.where(at_row, biases, small[8:16])
    tail = jnp.concatenate([small[0:8], late], 0).astype(BF16)
    for k in range(4):
        packed_ref[k, width : width + 16, :] = tail


def weight_grads(tokens, dquery, sums, context, dresid, dresid_core, other, small):
    width = dquery[0].shape[0]
    return pl.pallas_call(
        weight_grads_kernel,
        out_shape=SHAPE((4, width + 16, tokens[0].shape[1]), BF16),
        in_specs=[VMEM] * 14,
        out_specs=VMEM,
        cost_estimate=cost(8),
        compiler_params=room(18),
        name="weight_grads",
    )(*tokens, *dquery, sums, context, dresid, dresid_core, other, small)


def solution(mesh):
    ndp, nt = mesh.shape["dp"], mesh.shape["tensor"]
    fine = Mesh(
        mesh.devices.reshape(ndp // 8, 2, 2, 2, nt), ("outer", "y", "x", "core", "tensor")
    )
    DP, AXES = ("outer", "y", "x", "core"), ("outer", "y", "x", "core", "tensor")

    def moved_at(i, t):
        return (i & 1) != (t >> 1)

    def exchange(value, target, only=None):
        pairs = []
        for i in range(ndp):
            for t in range(nt):
                if only is None or only(i, t):
                    j, u = target(i, t)
                    pairs.append((i * nt + t, j * nt + u))
        return lax.ppermute(value, AXES, pairs)

    def swap(value):
        return exchange(value, lambda i, t: (i ^ 1, t ^ 2) if moved_at(i, t) else (i, t))

    def over_core(value):
        return exchange(value, lambda i, t: (i ^ 1, t))

    def over_z(value):
        return exchange(value, lambda i, t: (i, t ^ 1))

    def over_x(value):
        return exchange(value, lambda i, t: (i ^ 2, t))

    def over_y(value):
        return exchange(value, lambda i, t: (i ^ 4, t))

    def shards(
        tokens,
        cotangent,
        segment_ids,
        drop_flags,
        query_weight,
        query_bias,
        key_weight,
        value_weight,
        value_bias,
        out_weight,
        out_bias,
        attn_gain,
        attn_shift,
        up_weight,
        up_bias,
        down_weight,
        down_bias,
        ffn_gain,
        ffn_shift,
    ):
        i, t = lax.axis_index(DP), lax.axis_index("tensor")
        core, zbit, xbit, ybit = i & 1, t & 1, (i >> 1) & 1, (i >> 2) & 1
        moved = core != (t >> 1)
        length = segment_ids.shape[1]
        rows, model = tokens.shape
        width = query_weight.shape[1]
        part = up_weight.shape[1] // 4

        def turned(value, axis, bit):
            return jnp.where(bit == 1, jnp.flip(value, axis), value)

        def over_plane(value):
            copies = jnp.broadcast_to(value[None], (4,) + value.shape)
            return lax.all_to_all(copies, ("y", "x"), split_axis=0, concat_axis=0, tiled=True)

        def absolute(value):
            return turned(turned(value, 0, ybit), 1, xbit)

        token_own = swap(tokens)
        token_z = exchange(tokens, lambda i, t: (i, t ^ 1), lambda i, t: not moved_at(i, t))
        blank = jnp.zeros_like(query_bias)
        biases = jnp.concatenate([query_bias, blank, value_bias, blank])
        extra = jnp.concatenate(
            [jnp.broadcast_to(v[None], (16, model)) for v in (biases, up_bias)], 0
        )
        piece, quarter, local = take(
            jnp.stack([ybit * 2 + xbit, moved.astype(jnp.int32)]),
            (query_weight.T, key_weight.T, value_weight.T),
            extra,
            up_weight,
            down_weight,
        )
        piece = swap(piece)
        notes = jnp.concatenate(
            [segment_ids, jnp.broadcast_to(drop_flags[:, None], (1, 128))], axis=1
        )
        notes_core = over_core(notes)
        token_own, token_z, piece, quarter, out_weight, notes, notes_core = stage(
            token_own, token_z, piece, quarter, out_weight, notes, notes_core
        )
        token_core = over_core(token_own)
        token_zm = exchange(token_own, lambda i, t: (i, t ^ 1), moved_at)
        gathered = over_plane(piece)
        quarter = swap(quarter)
        first_vectors = vectors(out_bias, attn_gain, attn_shift)
        second_vectors = vectors(down_bias, ffn_gain, ffn_shift)
        notes = jnp.where(moved, notes_core, notes)
        shard = 2 * core + zbit
        flags = jnp.stack([moved.astype(jnp.int32), 1 - notes[0, length], xbit, ybit, shard])
        segment = notes[0, :length].reshape(2, 2, length // 4)
        segment = turned(turned(segment, 0, core), 1, zbit)
        segment = jnp.swapaxes(segment, 0, 1).reshape(length)
        marks = (
            *bounds(segment, QUERIES),
            *bounds(segment, KEYS),
            jnp.broadcast_to(segment[None], (8, length)),
            jnp.broadcast_to(segment[:, None], (length, 128)),
        )
        token_zm, token_z, gathered, quarter, out_weight, *rest = stage(
            token_zm,
            token_z,
            gathered,
            quarter,
            out_weight,
            flags,
            first_vectors,
            second_vectors,
            *marks,
        )
        flags, first_vectors, second_vectors, *marks = rest
        token_z = jnp.where(moved, token_zm, token_z)
        token_zc = over_core(token_z)
        group = (token_own, token_core, token_z, token_zc)
        qkv, weights = project(group, gathered)

        qkv, quarter, out_weight = stage(qkv, quarter, out_weight)
        quarter_z = over_z(quarter)
        own_x = exchange(quarter[: 2 * part], lambda i, t: (i ^ 2, t), moved_at)
        own_y = exchange(quarter[: 2 * part], lambda i, t: (i ^ 4, t), moved_at)
        out_own = swap(out_weight)
        half = 2 * rows
        wide_z, context_z, totals_z = attend_forward(qkv, marks, half, half)

        qkv, context_z, quarter_z, own_x, own_y, out_own = stage(
            qkv, context_z, quarter_z, own_x, own_y, out_own
        )
        context_other = over_z(context_z)
        out_other = over_z(out_own)
        units_z = quarter_z[: 2 * part]
        quarter_zy, quarter_zx = over_y(units_z), over_x(units_z)
        own_xy = exchange(own_x, lambda i, t: (i ^ 4, t), moved_at)
        wide_own, context_own, totals_own = attend_forward(qkv, marks, 0, half)

        context_own, context_other, out_other, quarter_zy, quarter_zx, own_xy = stage(
            context_own, context_other, out_other, quarter_zy, quarter_zx, own_xy
        )
        up_zxy = over_y(quarter_zx[:part])
        down_zxy = over_x(quarter_zy[part : 2 * part])
        mine, theirs = out_project(context_own, context_other, out_own, out_other)
        theirs = over_core(theirs)
        mine, theirs, cotangent = stage(mine, theirs, cotangent)
        cotangent = swap(cotangent)
        resid, normed, normed_low = rowwise(
            first_norm_kernel,
            "first_norm",
            (F32, F32, BF16),
            (),
            mine,
            theirs,
            token_own,
            first_vectors,
        )
        normed_core = over_core(normed_low)

        normed_low, normed_core, up_zxy, down_zxy = stage(
            normed_low, normed_core, up_zxy, down_zxy
        )
        pieces = (quarter, own_x, own_y, own_xy, quarter_z, quarter_zx, quarter_zy)
        pieces = (*pieces, up_zxy, down_zxy)
        hidden, slope, mine, theirs, up_all, down_all = feed_forward(
            flags, normed_low, normed_core, (*pieces, local)
        )
        layer_out, dsummed, dffn, sums_ffn = rowwise(
            second_norm_kernel,
            "second_norm",
            (BF16, F32, BF16, None),
            (flags,),
            mine,
            over_core(theirs),
            normed,
            cotangent,
            token_own,
            second_vectors,
        )
        dffn_core = over_core(dffn)

        dffn, dffn_core, layer_out = stage(dffn, dffn_core, layer_out)
        dpre, mine, theirs, up_bias_grad = hidden_back(dffn, dffn_core, slope, up_all, down_all)
        dpre, theirs = stage(dpre, theirs)
        got = over_core(theirs)
        parts = unit_grads(dpre, normed_low, normed_core, hidden, dffn, dffn_core)
        got, *parts = stage(got, *parts)
        plane_got = over_x(parts[1]), over_y(parts[3])
        dresid, dresid_low, small = small_kernel(
            first_norm_back_kernel,
            "first_norm_back",
            (((rows, model), F32), ((rows + 16, model), BF16), ((16, model), F32)),
            (flags,),
            mine,
            got,
            dsummed,
            resid,
            first_vectors,
            sums_ffn,
            up_bias_grad,
        )
        dresid_core = over_core(dresid_low)
        dcontext_own, dcontext_z, out_grad_z, small = small_kernel(
            context_back_kernel,
            "context_back",
            (
                ((width, half), BF16),
                ((width, half), BF16),
                ((width + 16, model), BF16),
                ((16, model), F32),
            ),
            (),
            dresid_low,
            dresid_core,
            small,
            out_own,
            out_other,
            context_other,
        )
        dcontext_z, dcontext_own, out_grad_z, layer_out = stage(
            dcontext_z, dcontext_own, out_grad_z, layer_out
        )
        dcontext_other = over_z(dcontext_z)
        layer_out = swap(layer_out)
        around = (dcontext_own, wide_own, totals_own)
        dq_own, sums = attend_backward(qkv, around, marks, 0, 0, rows, None, F32)

        dq_core, sums = attend_backward(qkv, around, marks, rows, rows, rows, sums, F32)
        dq_core, sums, dcontext_other, out_grad_z = stage(
            dq_core, sums, dcontext_other, out_grad_z
        )
        out_grad_other = over_z(out_grad_z)
        around = (dcontext_other, wide_z, totals_z)
        dq_z, sums = attend_backward(qkv, around, marks, half, 0, rows, sums, F32)

        dq_z, sums, layer_out, *plane_got = stage(dq_z, sums, layer_out, *plane_got)
        kept_own, send_own, kept_other, send_other = small_kernel(
            fold_plane_kernel,
            "fold_plane",
            (((2 * part, model), F32), ((2 * part, model), BF16)) * 2,
            (),
            parts[0],
            plane_got[0],
            parts[2],
            plane_got[1],
        )
        send_own, send_other = over_y(send_own), over_x(send_other)
        dq_zc, sums = attend_backward(qkv, around, marks, 3 * rows, rows, rows, sums, BF16)

        def home(value):
            kept, send, far = value
            send = exchange(send, lambda i, t: (i, t ^ 2) if moved_at(i, t) else (i ^ 1, t))
            far = exchange(far, lambda i, t: (i ^ 1, t ^ 2), moved_at)
            return kept, send, far

        def outer(value):
            bit = 8
            while bit < ndp:
                value = value + exchange(
                    value.astype(BF16), lambda i, t, bit=bit: (i ^ bit, t)
                ).astype(F32)
                bit *= 2
            return value

        def fold_home(name, value, kind=BF16):
            result = small_kernel(
                fold_home_kernel,
                name,
                ((value[0].shape, kind if ndp == 8 else F32),),
                (flags,),
                *value,
            )[0]
            return outer(result).astype(kind)

        dq_zc, sums, out_grad_other = stage(dq_zc, sums, out_grad_other)
        input_z, input_zc = input_back(half, dq_z, dq_zc, sums, weights)
        input_z, input_zc, sums, send_own, send_other = stage(
            input_z, input_zc, sums, send_own, send_other
        )
        unit_sum, unit_z = small_kernel(
            fold_shards_kernel,
            "fold_shards",
            (((2 * part, model), F32), ((2 * part, model), BF16)),
            (),
            kept_own,
            send_own,
            kept_other,
            send_other,
        )
        unit_z, input_zc, sums = stage(unit_z, input_zc, sums)
        unit_z = over_z(unit_z)
        input_zc = over_core(input_zc)
        mine, theirs = small_kernel(
            input_own_kernel,
            "input_own",
            (((rows, model), F32), ((rows, model), BF16)),
            (flags,),
            dq_own,
            dq_core,
            sums,
            weights,
            dresid,
            cotangent,
        )
        packed = weight_grads(
            group,
            (dq_own, dq_core, dq_z, dq_zc),
            sums,
            context_own,
            dresid_low,
            dresid_core,
            out_grad_other,
            small,
        )
        packed, input_z, input_zc, mine, theirs = stage(packed, input_z, input_zc, mine, theirs)
        input_z = small_kernel(
            fold_inputs_kernel, "fold_inputs", (((rows, model), BF16),), (), input_z, input_zc
        )[0]
        input_z, packed, theirs, unit_z = stage(input_z, packed, theirs, unit_z)
        input_other = over_z(input_z)
        parted = lax.all_to_all(packed, ("y", "x"), split_axis=0, concat_axis=0, tiled=True)
        theirs = over_core(theirs)
        unit_home = small_kernel(
            fold_z_kernel,
            "fold_z",
            (((part, model), F32), ((part, model), BF16), ((part, model), BF16)),
            (flags,),
            unit_sum,
            unit_z,
        )
        mine, theirs, *unit_home = stage(mine, theirs, *unit_home)
        unit_home = home(unit_home)

        parted, input_other, mine, theirs, *unit_home = stage(
            parted, input_other, mine, theirs, *unit_home
        )
        head_home = small_kernel(
            fold_parts_kernel,
            "fold_parts",
            (
                ((width // 2 + 16, model), F32),
                ((width // 2 + 16, model), BF16),
                ((width // 2 + 16, model), BF16),
            ),
            (flags,),
            parted,
        )
        mine, theirs, kept, send, far, *head_home = stage(mine, theirs, *unit_home, *head_home)
        head_home = home(head_home)
        unit_all = over_plane(fold_home("fold_units", (kept, send, far)))
        mine, theirs, input_other = stage(mine, theirs, input_other)
        tokens_grad = small_kernel(
            add_tokens_kernel,
            "add_tokens",
            (((rows, model), BF16),),
            (),
            mine,
            theirs,
            input_other,
        )[0]
        tokens_grad, *head_home = stage(tokens_grad, *head_home)
        tokens_grad = swap(tokens_grad)
        heads = fold_home("fold_heads", head_home, F32)
        heads, unit_all = stage(heads, unit_all)
        head_all = over_plane(heads[: width // 2].astype(BF16))
        small = heads[width // 2 :]
        up_bias_sum = lax.dynamic_slice_in_dim(small[6:10], t, 1, 0)[0]
        unit_other = over_core(unit_all)
        up_sum, down_sum = small_kernel(
            unit_results_kernel,
            "unit_results",
            (((model, 4 * part), F32), ((4 * part, model), F32)),
            (flags,),
            unit_all,
            unit_other,
        )
        head_all, up_sum, down_sum, tokens_grad, small, up_bias_sum = stage(
            head_all, up_sum, down_sum, tokens_grad, small, up_bias_sum
        )
        head_other = over_core(head_all)
        sums = small_kernel(
            head_results_kernel,
            "head_results",
            (((width, model), F32),) * 4 + (((rows, model), BF16),) * 2,
            (flags,),
            head_all,
            head_other,
            layer_out,
            tokens_grad,
        )
        layer_out, tokens_grad = sums[4:]
        narrow = small[12, :width], small[12, width : 2 * width]

        return (
            layer_out,
            tokens_grad,
            sums[0].T,
            narrow[0],
            sums[1].T,
            sums[2].T,
            narrow[1],
            sums[3],
            small[0],
            small[1],
            small[2],
            up_sum,
            up_bias_sum,
            down_sum,
            small[3],
            small[4],
            small[5],
        )

    return jax.shard_map(
        shards,
        mesh=fine,
        in_specs=(
            P(AXES, None),
            P(AXES, None),
            P(DP, None),
            P(DP),
            P(None, "tensor"),
            P("tensor"),
            P(None, "tensor"),
            P(None, "tensor"),
            P("tensor"),
            P("tensor", None),
            P(),
            P(),
            P(),
            P(None, "tensor"),
            P("tensor"),
            P("tensor", None),
            P(),
            P(),
            P(),
        ),
        out_specs=(
            P(AXES, None),
            P(AXES, None),
            P(None, "tensor"),
            P("tensor"),
            P(None, "tensor"),
            P(None, "tensor"),
            P("tensor"),
            P("tensor", None),
            P(),
            P(),
            P(),
            P(None, "tensor"),
            P("tensor"),
            P("tensor", None),
            P(),
            P(),
            P(),
        ),
        check_vma=False,
    )
```

```python
import functools

import jax
import jax.numpy as jnp
from jax import lax
from jax.experimental import pallas as pl
from jax.experimental.pallas import tpu as pltpu
from jax.sharding import Mesh
from jax.sharding import PartitionSpec as P

HEAD_DIM = 64
QUERIES, KEYS = 512, 256
EPS = 1e-05
NEG = -1e30
F32 = jnp.float32
BF16 = jnp.bfloat16
SMEM = pl.BlockSpec(memory_space=pltpu.SMEM)
VMEM = pl.BlockSpec(memory_space=pltpu.VMEM)
SHAPE = jax.ShapeDtypeStruct


def matmul(left, right):
    return jnp.dot(left, right, preferred_element_type=F32)


def matmul_left(left, right):
    return lax.dot_general(left, right, (((0,), (0,)), ((), ())), preferred_element_type=F32)


def matmul_right(left, right):
    return lax.dot_general(left, right, (((1,), (1,)), ((), ())), preferred_element_type=F32)


def stage(*values):
    return lax.optimization_barrier(values)


def cost(micros):
    return pl.CostEstimate(flops=int(micros * 1e9), bytes_accessed=1 << 12, transcendentals=0)


def room(mebibytes):
    return pltpu.CompilerParams(vmem_limit_bytes=mebibytes << 20)


def head_parts(width):
    return [slice(h, h + HEAD_DIM) for h in range(0, width, HEAD_DIM)]


def attend_forward_kernel(
    bq,
    bk,
    first,
    qlow_ref,
    qhigh_ref,
    klow_ref,
    khigh_ref,
    qkv_ref,
    row_ref,
    column_ref,
    wide_ref,
    context_ref,
    totals_ref,
    top_ref,
    sum_ref,
    acc_ref,
):
    width, count = wide_ref.shape
    length = qkv_ref.shape[1]
    parts = head_parts(width)
    heads = range(len(parts))
    key_parts = head_parts(2 * width)[len(parts) :]
    value_parts = head_parts(3 * width)[2 * len(parts) :]

    def over_query(i, _):
        at_o = pl.ds(pl.multiple_of(i * bq, bq), bq)
        at_q = pl.ds(pl.multiple_of(first + i * bq, bq), bq)
        block = i + first // bq
        top_ref[...] = jnp.full(top_ref.shape, NEG, F32)
        sum_ref[...] = jnp.zeros(sum_ref.shape, F32)
        acc_ref[...] = jnp.zeros(acc_ref.shape, F32)
        row = row_ref[0:1, at_q]

        def over_keys(j, _):
            @pl.when((klow_ref[j] <= qhigh_ref[block]) & (qlow_ref[block] <= khigh_ref[j]))
            def _():
                at_k = pl.ds(pl.multiple_of(j * bk, bk), bk)
                column = column_ref[at_k, :]
                same = jnp.concatenate([column] * (bq // 128), 1) == row
                scores = [
                    matmul_left(qkv_ref[k, at_k], qkv_ref[q, at_q])
                    for k, q in zip(key_parts, parts)
                ]
                scores = [jnp.where(same, value, NEG) for value in scores]
                old = [top_ref[h : h + 1, :] for h in heads]
                top = [jnp.maximum(o, jnp.max(v, 0, keepdims=True)) for o, v in zip(old, scores)]
                exponent = [jnp.exp(v - m) for v, m in zip(scores, top)]
                scale = [jnp.exp(o - m) for o, m in zip(old, top)]
                total = [
                    sum_ref[h : h + 1, :] * scale[h] + jnp.sum(exponent[h], 0, keepdims=True)
                    for h in heads
                ]
                added = [
                    matmul(qkv_ref[v, at_k], e.astype(BF16)) for v, e in zip(value_parts, exponent)
                ]
                added = [acc_ref[p, :] * c + v for p, c, v in zip(parts, scale, added)]
                for h in heads:
                    top_ref[h : h + 1, :] = top[h]
                    sum_ref[h : h + 1, :] = total[h]
                    acc_ref[parts[h], :] = added[h]

            return 0

        lax.fori_loop(0, length // bk, over_keys, 0)
        for h in heads:
            value = acc_ref[parts[h], :] / sum_ref[h : h + 1, :]
            wide_ref[parts[h], at_o] = value
            context_ref[parts[h], at_o] = value.astype(BF16)
            totals_ref[h : h + 1, at_o] = top_ref[h : h + 1, :] + jnp.log(sum_ref[h : h + 1, :])
        return 0

    lax.fori_loop(0, count // bq, over_query, 0)


def attend_backward_kernel(
    bq,
    bk,
    first,
    base,
    follows,
    qlow_ref,
    qhigh_ref,
    klow_ref,
    khigh_ref,
    qkv_ref,
    dcontext_ref,
    wide_ref,
    totals_ref,
    row_ref,
    column_ref,
    *rest,
):
    if follows:
        before_ref, dquery_ref, sums_ref, delta_ref, dq_ref, dk_ref, dv_ref = rest
    else:
        dquery_ref, sums_ref, delta_ref, dq_ref, dk_ref, dv_ref = rest
    width, count = dquery_ref.shape
    length = qkv_ref.shape[1]
    parts = head_parts(width)
    heads = range(len(parts))
    key_parts = head_parts(2 * width)[len(parts) :]
    value_parts = head_parts(3 * width)[2 * len(parts) :]
    dq_ref[...] = jnp.zeros(dq_ref.shape, F32)
    chunk = slice(base, base + count)
    for h in heads:
        delta_ref[h : h + 1, :] = jnp.sum(
            wide_ref[parts[h], chunk] * dcontext_ref[parts[h], chunk].astype(F32), 0, keepdims=True
        )

    def over_keys(j, _):
        at_k = pl.ds(pl.multiple_of(j * bk, bk), bk)
        if follows:
            dk_ref[...] = before_ref[0:width, at_k]
            dv_ref[...] = before_ref[width : 2 * width, at_k]
        else:
            dk_ref[...] = jnp.zeros(dk_ref.shape, F32)
            dv_ref[...] = jnp.zeros(dv_ref.shape, F32)

        def over_query(i, _):
            block = i + first // bq

            @pl.when((klow_ref[j] <= qhigh_ref[block]) & (qlow_ref[block] <= khigh_ref[j]))
            def _():
                at_o = pl.ds(pl.multiple_of(i * bq, bq), bq)
                at_b = pl.ds(pl.multiple_of(base + i * bq, bq), bq)
                at_q = pl.ds(pl.multiple_of(first + i * bq, bq), bq)
                column = column_ref[at_k, :]
                same = jnp.concatenate([column] * (bq // 128), 1) == row_ref[0:1, at_q]
                scores = [
                    matmul_left(qkv_ref[k, at_k], qkv_ref[q, at_q])
                    for k, q in zip(key_parts, parts)
                ]
                dprobs = [
                    matmul_left(qkv_ref[v, at_k], dcontext_ref[p, at_b])
                    for v, p in zip(value_parts, parts)
                ]
                probs = [
                    jnp.exp(jnp.where(same, scores[h], NEG) - totals_ref[h : h + 1, at_b])
                    for h in heads
                ]
                dscores = [
                    (probs[h] * (dprobs[h] - delta_ref[h : h + 1, at_o])).astype(BF16)
                    for h in heads
                ]
                dv = [
                    matmul_right(dcontext_ref[p, at_b], v.astype(BF16)) for p, v in zip(parts, probs)
                ]
                dk = [matmul_right(qkv_ref[p, at_q], v) for p, v in zip(parts, dscores)]
                dq = [matmul(qkv_ref[k, at_k], v) for k, v in zip(key_parts, dscores)]
                for h in heads:
                    dv_ref[parts[h], :] += dv[h]
                    dk_ref[parts[h], :] += dk[h]
                    dq_ref[parts[h], at_o] += dq[h]

            return 0

        lax.fori_loop(0, count // bq, over_query, 0)
        sums_ref[0:width, at_k] = dk_ref[...].astype(sums_ref.dtype)
        sums_ref[width : 2 * width, at_k] = dv_ref[...].astype(sums_ref.dtype)
        return 0

    lax.fori_loop(0, length // bk, over_keys, 0)
    dquery_ref[...] = dq_ref[...].astype(BF16)


def bounds(segment, block):
    blocks = segment.reshape(-1, block)
    return jnp.min(blocks, 1), jnp.max(blocks, 1)


def attend_forward(qkv, marks, first, count):
    width = qkv.shape[0] // 3
    wide_low, wide_high, low, high, row, column = marks
    bq, bk = QUERIES, KEYS
    return pl.pallas_call(
        functools.partial(attend_forward_kernel, bq, bk, first),
        out_shape=(SHAPE((width, count), F32), SHAPE((width, count), BF16), SHAPE((8, count), F32)),
        in_specs=[SMEM] * 4 + [VMEM] * 3,
        out_specs=(VMEM,) * 3,
        scratch_shapes=[pltpu.VMEM((8, bq), F32)] * 2 + [pltpu.VMEM((width, bq), F32)],
        cost_estimate=cost(15),
        compiler_params=room(16),
        name="attend_forward",
    )(wide_low, wide_high, low, high, qkv, row, column)


def attend_backward(qkv, around, marks, first, base, count, before, kind):
    dcontext, wide, totals = around
    width, length = dcontext.shape[0], qkv.shape[1]
    _, _, low, high, row, column = marks
    bq = bk = KEYS
    follows = before is not None
    return pl.pallas_call(
        functools.partial(attend_backward_kernel, bq, bk, first, base, follows),
        out_shape=(SHAPE((width, count), BF16), SHAPE((2 * width, length), kind)),
        in_specs=[SMEM] * 4 + [VMEM] * (7 if follows else 6),
        out_specs=(VMEM,) * 2,
        scratch_shapes=[
            pltpu.VMEM((8, count), F32),
            pltpu.VMEM((width, count), F32),
            pltpu.VMEM((width, bk), F32),
            pltpu.VMEM((width, bk), F32),
        ],
        cost_estimate=cost(count // 64),
        compiler_params=room(22),
        name="attend_backward",
    )(
        low,
        high,
        low,
        high,
        qkv,
        dcontext,
        wide,
        totals,
        row,
        column,
        *((before,) if follows else ()),
    )


def plane_slots(flags_ref, slots):
    slots = [jnp.where(flags_ref[2] == 1, slots[k ^ 1], slots[k]) for k in range(4)]
    return [jnp.where(flags_ref[3] == 1, slots[k ^ 2], slots[k]) for k in range(4)]


def feed_forward_kernel(flags_ref, own_ref, core_ref, *rest):
    pieces, (hidden_ref, slope_ref, mine_ref, other_ref, up_ref, down_ref) = rest[:-6], rest[-6:]
    rows, cols = own_ref.shape[0], 256
    part = up_ref.shape[0] // 8
    for n in range(2):
        for k in range(4):
            to = slice((2 * k + n) * part, (2 * k + n + 1) * part)
            if n == 1 and k == 3:
                up, down = pieces[7][...], pieces[8][...]
            else:
                up, down = pieces[4 * n + k][0:part, :], pieces[4 * n + k][part : 2 * part, :]
            if n == 0 and k > 0:
                up = up + pieces[9][k - 1, 0:part, :]
                down = down + pieces[9][k - 1, part : 2 * part, :]
            up_ref[to, :] = up
            down_ref[to, :] = down
    biases = []
    for n in range(2):
        value = pieces[4 * n][2 * part : 2 * part + 16, :].astype(F32)[0:1]
        biases.append(plane_slots(flags_ref, [value[:, k * part : (k + 1) * part] for k in range(4)]))
    biases = jnp.concatenate([biases[n][k] for k in range(4) for n in range(2)], 1)
    for source, target, start in ((core_ref, other_ref, rows), (own_ref, mine_ref, 0)):
        at = slice(start, start + rows)
        value = source[...]
        for n in range(0, up_ref.shape[0], cols):
            to = slice(n, n + cols)
            pre = matmul_right(value, up_ref[to, :]) + biases[:, to]
            normal = 0.5 * (1.0 + lax.erf(pre * 0.7071067811865476))
            hidden_ref[at, to] = (pre * normal).astype(BF16)
            density = jnp.exp(-0.5 * pre * pre) * 0.3989422804014327
            slope_ref[at, to] = (normal + pre * density).astype(BF16)
        target[...] = matmul(hidden_ref[at, :], down_ref[...]).astype(target.dtype)


def feed_forward(flags, own, core, pieces):
    rows, model = own.shape
    units = 2 * model
    return pl.pallas_call(
        feed_forward_kernel,
        out_shape=(
            SHAPE((2 * rows, units), BF16),
            SHAPE((2 * rows, units), BF16),
            SHAPE((rows, model), F32),
            SHAPE((rows, model), BF16),
            SHAPE((units, model), BF16),
            SHAPE((units, model), BF16),
        ),
        in_specs=[SMEM] + [VMEM] * 12,
        out_specs=(VMEM,) * 6,
        cost_estimate=cost(12),
        compiler_params=room(32),
        name="feed_forward",
    )(flags, own, core, *pieces)


def hidden_back_kernel(
    own_ref, core_ref, slope_ref, up_ref, down_ref, dpre_ref, mine_ref, other_ref, bias_ref
):
    rows, cols = own_ref.shape[0], 256
    for source, target, start in ((core_ref, other_ref, rows), (own_ref, mine_ref, 0)):
        at = slice(start, start + rows)
        value = source[...]
        for n in range(0, up_ref.shape[0], cols):
            to = slice(n, n + cols)
            dhidden = matmul_right(value, down_ref[to, :])
            dpre_ref[at, to] = (dhidden * slope_ref[at, to].astype(F32)).astype(BF16)
        target[...] = matmul(dpre_ref[at, :], up_ref[...]).astype(target.dtype)
    bias_ref[...] = matmul(jnp.ones((8, 2 * rows), BF16), dpre_ref[...])


def hidden_back(own, core, slope, up, down):
    rows, model = own.shape
    units = up.shape[0]
    return pl.pallas_call(
        hidden_back_kernel,
        out_shape=(
            SHAPE((2 * rows, units), BF16),
            SHAPE((rows, model), F32),
            SHAPE((rows, model), BF16),
            SHAPE((8, units), F32),
        ),
        in_specs=[VMEM] * 5,
        out_specs=(VMEM,) * 4,
        cost_estimate=cost(0),
        compiler_params=room(26),
        name="hidden_back",
    )(own, core, slope, up, down)


def unit_grads_kernel(
    dpre_ref, normed_ref, normed_core_ref, hidden_ref, dffn_ref, dffn_core_ref, *refs
):
    rows = normed_ref.shape[0]
    part = dpre_ref.shape[1] // 8
    places = ((0, 0), (1, 0), (0, 1), (1, 1)), ((0, 0), (0, 1), (1, 0), (1, 1))
    halves = (dpre_ref, normed_ref, normed_core_ref), (hidden_ref, dffn_ref, dffn_core_ref)
    for m, (left_ref, own_ref, core_ref) in enumerate(halves):
        for k in range(4):
            at = slice(2 * k * part, 2 * (k + 1) * part)
            total = matmul_left(left_ref[0:rows, at], own_ref[...])
            total = total + matmul_left(left_ref[rows : 2 * rows, at], core_ref[...])
            for n in range(2):
                sent, slot = places[n][k]
                to = slice((2 * m + slot) * part, (2 * m + slot + 1) * part)
                refs[2 * n + sent][to, :] = total[n * part : (n + 1) * part].astype(BF16)


def unit_grads(dpre, normed, normed_core, hidden, dffn, dffn_core):
    return pl.pallas_call(
        unit_grads_kernel,
        out_shape=(SHAPE((dpre.shape[1] // 2, normed.shape[1]), BF16),) * 4,
        in_specs=[VMEM] * 6,
        out_specs=(VMEM,) * 4,
        cost_estimate=cost(5),
        compiler_params=room(24),
        name="unit_grads",
    )(dpre, normed, normed_core, hidden, dffn, dffn_core)


def out_project_kernel(own_ref, other_ref, own_w_ref, other_w_ref, mine_ref, theirs_ref):
    rows = mine_ref.shape[0]
    for target, at in ((theirs_ref, slice(rows, 2 * rows)), (mine_ref, slice(0, rows))):
        first = own_w_ref.shape[0] - own_ref.shape[0]
        value = matmul_left(own_ref[:, at], own_w_ref[first:, :])
        value = value + matmul_left(other_ref[:, at], other_w_ref[first:, :])
        target[...] = value.astype(target.dtype)


def out_project(own, other, own_weight, other_weight):
    rows, model = own.shape[1] // 2, own_weight.shape[1]
    return pl.pallas_call(
        out_project_kernel,
        out_shape=(SHAPE((rows, model), F32), SHAPE((rows, model), BF16)),
        in_specs=[VMEM] * 4,
        out_specs=(VMEM,) * 2,
        cost_estimate=cost(3),
        compiler_params=room(12),
        name="out_project",
    )(own, other, own_weight, other_weight)


def input_back_kernel(start, first_ref, second_ref, sums_ref, weights_ref, mine_ref, theirs_ref):
    rows = first_ref.shape[1]
    width = first_ref.shape[0]
    query_weights = weights_ref[0:width, :] * 0.125
    for k, ref, target in ((1, second_ref, theirs_ref), (0, first_ref, mine_ref)):
        at = slice(start + k * rows, start + (k + 1) * rows)
        value = matmul_left(ref[...], query_weights)
        value = value + matmul_left(sums_ref[:, at], weights_ref[width:, :])
        target[...] = value.astype(target.dtype)


def input_back(start, first, second, sums, weights):
    shape = (first.shape[1], weights.shape[1])
    return pl.pallas_call(
        functools.partial(input_back_kernel, start),
        out_shape=(SHAPE(shape, F32), SHAPE(shape, BF16)),
        in_specs=[VMEM] * 4,
        out_specs=(VMEM,) * 2,
        cost_estimate=cost(0),
        compiler_params=room(14),
        name="input_back",
    )(first, second, sums, weights)


def input_own_kernel(
    flags_ref,
    first_ref,
    second_ref,
    sums_ref,
    weights_ref,
    dresid_ref,
    cotangent_ref,
    mine_ref,
    theirs_ref,
):
    width, rows = first_ref.shape
    query_weights = weights_ref[0:width, :] * 0.125
    for k, ref in ((1, second_ref), (0, first_ref)):
        at = slice(k * rows, (k + 1) * rows)
        value = matmul_left(ref[...], query_weights)
        value = value + matmul_left(sums_ref[:, at], weights_ref[width:, :])
        if k == 1:
            theirs_ref[...] = value.astype(BF16)
        else:
            skipped = (1 - flags_ref[1]).astype(F32)
            mine_ref[...] = value + dresid_ref[...] + skipped * cotangent_ref[...].astype(F32)


def context_back_kernel(
    own_ref,
    core_ref,
    small_ref,
    own_w_ref,
    other_w_ref,
    context_ref,
    mine_ref,
    theirs_ref,
    grad_ref,
    sum_ref,
):
    rows = own_ref.shape[0] - 16
    width = mine_ref.shape[0]
    grad = 0.0
    for k, ref in enumerate((own_ref, core_ref)):
        at = slice(k * rows, (k + 1) * rows)
        value = ref[0:rows, :]
        first = own_w_ref.shape[0] - width
        theirs_ref[:, at] = matmul_right(other_w_ref[first:, :], value).astype(BF16)
        mine_ref[:, at] = matmul_right(own_w_ref[first:, :], value).astype(BF16)
        grad = grad + matmul(context_ref[:, at], value)
    grad_ref[0:width, :] = grad.astype(BF16)
    total = small_ref[...] + core_ref[rows : rows + 16, :].astype(F32)
    sum_ref[...] = total
    grad_ref[width : width + 16, :] = total.astype(BF16)


def take_kernel(
    flags_ref,
    query_ref,
    key_ref,
    value_ref,
    extra_ref,
    up_ref,
    down_ref,
    out_ref,
    piece_ref,
    quarter_ref,
    local_ref,
    turned_ref,
):
    place = flags_ref[0]
    held = 1.0 - flags_ref[1].astype(F32)
    fourth = query_ref.shape[0] // 4
    for n, ref in enumerate((query_ref, key_ref, value_ref)):
        at = pl.ds(pl.multiple_of(place * fourth, fourth), fourth)
        piece_ref[n * fourth : (n + 1) * fourth, :] = ref[at, :]
    piece_ref[3 * fourth :, :] = extra_ref[0:16, :]
    turned_ref[...] = up_ref[...].T
    part = local_ref.shape[1] // 2
    quarter_ref[2 * part : 2 * part + 16, :] = extra_ref[16:32, :]
    quarter_ref[2 * part + 16 :, :] = out_ref[...]
    for k in range(4):
        at = pl.ds(pl.multiple_of((place ^ k) * part, part), part)
        if k == 0:
            quarter_ref[0:part, :] = turned_ref[at, :]
            quarter_ref[part : 2 * part, :] = down_ref[at, :]
        else:
            local_ref[k - 1, 0:part, :] = (turned_ref[at, :] * held).astype(BF16)
            local_ref[k - 1, part : 2 * part, :] = (down_ref[at, :] * held).astype(BF16)


def take(place, heads, extra, up, down, out):
    units, model = down.shape
    rows = heads[0].shape[0] // 4 * 3 + 16
    return pl.pallas_call(
        take_kernel,
        out_shape=(
            SHAPE((rows, model), BF16),
            SHAPE((units // 2 + 16 + out.shape[0], model), BF16),
            SHAPE((3, units // 2, model), BF16),
        ),
        in_specs=[SMEM] + [VMEM] * 7,
        out_specs=(VMEM,) * 3,
        scratch_shapes=[pltpu.VMEM((units, model), BF16)],
        cost_estimate=cost(20),
        compiler_params=room(14),
        name="take",
    )(place, *heads, extra, up, down, out)


def small_kernel(kernel, name, results, flags, *operands, mebibytes=16):
    return pl.pallas_call(
        kernel,
        out_shape=tuple(SHAPE(shape, kind) for shape, kind in results),
        in_specs=[SMEM] * len(flags) + [VMEM] * len(operands),
        out_specs=(VMEM,) * len(results),
        cost_estimate=cost(0),
        compiler_params=room(mebibytes),
        name=name,
    )(*flags, *operands)


def fold_plane_kernel(*refs):
    part = refs[0].shape[0] // 4
    for n in range(2):
        keep_ref, got_ref = refs[2 * n], refs[2 * n + 1]
        kept_ref, send_ref = refs[4 + 2 * n], refs[5 + 2 * n]
        for m in range(2):
            at = slice(m * part, (m + 1) * part)
            kept, sent = (
                keep_ref[k * part : (k + 1) * part, :].astype(F32)
                + got_ref[k * part : (k + 1) * part, :].astype(F32)
                for k in (2 * m, 2 * m + 1)
            )
            kept_ref[at, :] = kept
            send_ref[at, :] = sent.astype(BF16)


def fold_shards_kernel(own_ref, own_got_ref, other_ref, other_got_ref, sum_ref, send_ref):
    sum_ref[...] = own_ref[...] + own_got_ref[...].astype(F32)
    send_ref[...] = (other_ref[...] + other_got_ref[...].astype(F32)).astype(BF16)


def split_home(flags_ref, value, kept_ref, send_ref, far_ref):
    half = kept_ref.shape[0]
    kept_ref[...] = value[:half]
    far_ref[...] = value[half:].astype(BF16)

    @pl.when(flags_ref[0] == 1)
    def _():
        send_ref[...] = value[:half].astype(BF16)

    @pl.when(flags_ref[0] == 0)
    def _():
        send_ref[...] = value[half:].astype(BF16)


def fold_z_kernel(flags_ref, sum_ref, got_ref, kept_ref, send_ref, far_ref):
    split_home(flags_ref, sum_ref[...] + got_ref[...].astype(F32), kept_ref, send_ref, far_ref)


def fold_parts_kernel(flags_ref, parts_ref, kept_ref, send_ref, far_ref):
    value = parts_ref[0].astype(F32) + parts_ref[1].astype(F32)
    value = value + (parts_ref[2].astype(F32) + parts_ref[3].astype(F32))
    half = kept_ref.shape[0] - 16
    tail = value[2 * half :]
    kept_ref[0:half, :] = value[:half]
    kept_ref[half:, :] = tail
    far_ref[0:half, :] = value[half : 2 * half].astype(BF16)
    far_ref[half:, :] = tail.astype(BF16)
    send_ref[half:, :] = tail.astype(BF16)

    @pl.when(flags_ref[0] == 1)
    def _():
        send_ref[0:half, :] = value[:half].astype(BF16)

    @pl.when(flags_ref[0] == 0)
    def _():
        send_ref[0:half, :] = value[half : 2 * half].astype(BF16)


def fold_inputs_kernel(mine_ref, theirs_ref, result_ref):
    result_ref[...] = (mine_ref[...] + theirs_ref[...].astype(F32)).astype(BF16)


def add_tokens_kernel(mine_ref, theirs_ref, other_ref, result_ref):
    other = theirs_ref[...].astype(F32) + other_ref[...].astype(F32)
    result_ref[...] = (mine_ref[...] + other).astype(BF16)


def fold_home_kernel(flags_ref, kept_ref, got_ref, far_ref, result_ref):
    got = got_ref[...].astype(F32)
    first = jnp.where(flags_ref[0] == 1, far_ref[...].astype(F32), kept_ref[...])
    result_ref[...] = (first + got).astype(result_ref.dtype)


def unit_results_kernel(flags_ref, mine_ref, other_ref, up_ref, down_ref):
    def put(first_ref, second_ref):
        part = first_ref.shape[1]
        for k in range(4):
            down_ref[k * part : (k + 1) * part, :] = second_ref[k].astype(F32)
        up_ref[...] = first_ref[...].reshape(4 * part, first_ref.shape[2]).astype(F32).T

    @pl.when(flags_ref[0] == 1)
    def _():
        put(other_ref, mine_ref)

    @pl.when(flags_ref[0] == 0)
    def _():
        put(mine_ref, other_ref)


def head_results_kernel(flags_ref, mine_ref, other_ref, layer_ref, tokens_ref, *results):
    half = mine_ref.shape[1]
    results[4][...] = layer_ref[...]
    results[5][...] = tokens_ref[...]
    for k, ref in enumerate(results[:4]):
        mine, other = mine_ref[k].astype(F32), other_ref[k].astype(F32)
        ref[0:half, :] = jnp.where(flags_ref[0] == 1, other, mine)
        ref[half : 2 * half, :] = jnp.where(flags_ref[0] == 1, mine, other)


def normal_rows(value):
    center = value - jnp.mean(value, -1, keepdims=True)
    root = lax.rsqrt(jnp.mean(center * center, -1, keepdims=True) + EPS)
    return center * root, root


def normal_back(grad, normal, root):
    inner = jnp.mean(grad * normal, -1, keepdims=True)
    return root * (grad - jnp.mean(grad, -1, keepdims=True) - normal * inner)


STEP = 128


def first_norm_kernel(mine_ref, got_ref, token_ref, vector_ref, resid_ref, normed_ref, low_ref):
    def step(k, _):
        at = pl.ds(pl.multiple_of(k * STEP, STEP), STEP)
        attention = mine_ref[at, :] + got_ref[at, :].astype(F32)
        resid = token_ref[at, :].astype(F32) + attention + vector_ref[0:1, :]
        resid_ref[at, :] = resid
        normed = normal_rows(resid)[0] * vector_ref[1:2, :] + vector_ref[2:3, :]
        normed_ref[at, :] = normed
        low_ref[at, :] = normed.astype(BF16)
        return 0

    lax.fori_loop(0, mine_ref.shape[0] // STEP, step, 0)


def second_norm_kernel(
    flags_ref,
    mine_ref,
    got_ref,
    normed_ref,
    cotangent_ref,
    token_ref,
    vector_ref,
    layer_ref,
    dsummed_ref,
    low_ref,
    sums_ref,
):
    keep = flags_ref[1].astype(F32)
    sums_ref[...] = jnp.zeros(sums_ref.shape, F32)

    def step(k, _):
        at = pl.ds(pl.multiple_of(k * STEP, STEP), STEP)
        units = mine_ref[at, :] + got_ref[at, :].astype(F32)
        normal, root = normal_rows(normed_ref[at, :] + units + vector_ref[0:1, :])
        final = normal * vector_ref[1:2, :] + vector_ref[2:3, :]
        token = token_ref[at, :].astype(F32)
        layer_ref[at, :] = (keep * final + (1.0 - keep) * token).astype(BF16)
        cotangent = cotangent_ref[at, :].astype(F32)
        dfinal = keep * cotangent
        dsummed = normal_back(dfinal * vector_ref[1:2, :], normal, root)
        dsummed_ref[at, :] = dsummed
        low_ref[at, :] = dsummed.astype(BF16)
        sums_ref[0:1, :] += jnp.sum(dsummed, 0, keepdims=True)
        sums_ref[1:2, :] += jnp.sum(dfinal * normal, 0, keepdims=True)
        sums_ref[2:3, :] += jnp.sum(dfinal, 0, keepdims=True)
        return 0

    lax.fori_loop(0, mine_ref.shape[0] // STEP, step, 0)


def first_norm_back_kernel(
    flags_ref,
    mine_ref,
    got_ref,
    dsummed_ref,
    resid_ref,
    vector_ref,
    ffn_ref,
    bias_ref,
    dresid_ref,
    low_ref,
    small_ref,
):
    rows, model = mine_ref.shape
    part = model // 4
    small_ref[...] = jnp.zeros(small_ref.shape, F32)

    def step(k, _):
        at = pl.ds(pl.multiple_of(k * STEP, STEP), STEP)
        dnormed = dsummed_ref[at, :] + (mine_ref[at, :] + got_ref[at, :].astype(F32))
        normal, root = normal_rows(resid_ref[at, :])
        dresid = normal_back(dnormed * vector_ref[1:2, :], normal, root)
        dresid_ref[at, :] = dresid
        low_ref[at, :] = dresid.astype(BF16)
        small_ref[0:1, :] += jnp.sum(dresid, 0, keepdims=True)
        small_ref[1:2, :] += jnp.sum(dnormed * normal, 0, keepdims=True)
        small_ref[2:3, :] += jnp.sum(dnormed, 0, keepdims=True)
        return 0

    lax.fori_loop(0, rows // STEP, step, 0)
    small_ref[3:6, :] = ffn_ref[0:3, :]
    wide = 0.0
    for n in range(2):
        slots = [bias_ref[0:1, (2 * k + n) * part : (2 * k + n + 1) * part] for k in range(4)]
        value = jnp.concatenate(plane_slots(flags_ref, slots), 1)
        at = lax.broadcasted_iota(jnp.int32, (4, model), 0) == (flags_ref[4] ^ n)
        wide = wide + jnp.where(at, value, 0.0)
    small_ref[6:10, :] = wide
    low_ref[rows : rows + 16, :] = small_ref[...].astype(BF16)


def vectors(bias, gain, shift):
    return jnp.concatenate([jnp.stack([bias, gain, shift]), jnp.zeros((5,) + bias.shape)]).astype(F32)


def rowwise(kernel, name, kinds, flags, *operands):
    shape = operands[0].shape
    results = tuple(SHAPE(shape if kind else (8, shape[1]), kind or F32) for kind in kinds)
    return pl.pallas_call(
        kernel,
        out_shape=results,
        in_specs=[SMEM] * len(flags) + [VMEM] * len(operands),
        out_specs=(VMEM,) * len(results),
        cost_estimate=cost(2),
        compiler_params=room(16),
        name=name,
    )(*flags, *operands)


def project_kernel(own_ref, core_ref, z_ref, zc_ref, gathered_ref, qkv_ref, weights_ref):
    rows = own_ref.shape[0]
    fourth = weights_ref.shape[0] // 4
    width = weights_ref.shape[0] // 3
    for k in range(4):
        for n in range(3):
            piece = fourth // 3
            to = slice(n * width + k * piece, n * width + (k + 1) * piece)
            weights_ref[to, :] = gathered_ref[k, n * piece : (n + 1) * piece, :]
    weights = weights_ref[...]
    biases = gathered_ref[0, fourth : fourth + 16, 0 : 3 * width]
    first = lax.broadcasted_iota(jnp.int32, (16, rows), 0) == 0
    columns = matmul_left(biases, jnp.where(first, 1.0, 0.0).astype(BF16))
    for k, ref in enumerate((own_ref, core_ref, z_ref, zc_ref)):
        at = slice(k * rows, (k + 1) * rows)
        value = matmul_right(weights, ref[...]) + columns
        qkv_ref[0:width, at] = (value[:width] * 0.125).astype(BF16)
        qkv_ref[width:, at] = value[width:].astype(BF16)


def project(tokens, gathered):
    rows, model = tokens[0].shape
    units = 4 * (gathered.shape[1] - 16)
    return pl.pallas_call(
        project_kernel,
        out_shape=(SHAPE((units, 4 * rows), BF16), SHAPE((units, model), BF16)),
        in_specs=[VMEM] * 5,
        out_specs=(VMEM,) * 2,
        cost_estimate=cost(4),
        compiler_params=room(20),
        name="project",
    )(*tokens, gathered)


def weight_grads_kernel(
    own_ref,
    core_ref,
    z_ref,
    zc_ref,
    dq_own_ref,
    dq_core_ref,
    dq_z_ref,
    dq_zc_ref,
    sums_ref,
    context_ref,
    dresid_ref,
    dresid_core_ref,
    other_ref,
    small_ref,
    packed_ref,
):
    rows = own_ref.shape[0]
    width = dq_own_ref.shape[0]
    tokens = (own_ref, core_ref, z_ref, zc_ref)
    dquery = (dq_own_ref, dq_core_ref, dq_z_ref, dq_zc_ref)
    total, query, bias = 0.0, 0.0, 0.0
    count = jnp.ones((8, rows), BF16)
    for k in range(4):
        value = tokens[k][...]
        query = query + matmul(dquery[k][...], value)
        total = total + matmul(sums_ref[:, k * rows : (k + 1) * rows], value)
        bias = bias + matmul_right(count, dquery[k][...])
    packed_ref[0, 0:width, :] = (query * 0.125).astype(BF16)
    packed_ref[1, 0:width, :] = total[:width].astype(BF16)
    packed_ref[2, 0:width, :] = total[width:].astype(BF16)
    out = matmul(context_ref[:, 0:rows], dresid_ref[0:rows, :])
    out = out + matmul(context_ref[:, rows : 2 * rows], dresid_core_ref[0:rows, :])
    packed_ref[3, 0:width, :] = (out + other_ref[0:width, :].astype(F32)).astype(BF16)
    small = small_ref[...] + other_ref[width : width + 16, :].astype(F32)
    count = jnp.ones((8, 4 * rows), BF16)
    values = matmul_right(count, sums_ref[width : 2 * width, :])
    biases = jnp.concatenate([bias * 0.125, values, jnp.zeros_like(bias), jnp.zeros_like(bias)], 1)
    at_row = lax.broadcasted_iota(jnp.int32, (8, 4 * width), 0) == 4
    late = jnp.where(at_row, biases, small[8:16])
    tail = jnp.concatenate([small[0:8], late], 0).astype(BF16)
    for k in range(4):
        packed_ref[k, width : width + 16, :] = tail


def weight_grads(tokens, dquery, sums, context, dresid, dresid_core, other, small):
    width = dquery[0].shape[0]
    return pl.pallas_call(
        weight_grads_kernel,
        out_shape=SHAPE((4, width + 16, tokens[0].shape[1]), BF16),
        in_specs=[VMEM] * 14,
        out_specs=VMEM,
        cost_estimate=cost(8),
        compiler_params=room(18),
        name="weight_grads",
    )(*tokens, *dquery, sums, context, dresid, dresid_core, other, small)


def solution(mesh):
    ndp, nt = mesh.shape["dp"], mesh.shape["tensor"]
    fine = Mesh(
        mesh.devices.reshape(ndp // 8, 2, 2, 2, nt), ("outer", "y", "x", "core", "tensor")
    )
    DP, AXES = ("outer", "y", "x", "core"), ("outer", "y", "x", "core", "tensor")

    def moved_at(i, t):
        return (i & 1) != (t >> 1)

    def exchange(value, target, only=None):
        pairs = []
        for i in range(ndp):
            for t in range(nt):
                if only is None or only(i, t):
                    j, u = target(i, t)
                    pairs.append((i * nt + t, j * nt + u))
        return lax.ppermute(value, AXES, pairs)

    def swap(value):
        return exchange(value, lambda i, t: (i ^ 1, t ^ 2) if moved_at(i, t) else (i, t))

    def over_core(value):
        return exchange(value, lambda i, t: (i ^ 1, t))

    def over_z(value):
        return exchange(value, lambda i, t: (i, t ^ 1))

    def over_x(value):
        return exchange(value, lambda i, t: (i ^ 2, t))

    def over_y(value):
        return exchange(value, lambda i, t: (i ^ 4, t))

    def shards(
        tokens,
        cotangent,
        segment_ids,
        drop_flags,
        query_weight,
        query_bias,
        key_weight,
        value_weight,
        value_bias,
        out_weight,
        out_bias,
        attn_gain,
        attn_shift,
        up_weight,
        up_bias,
        down_weight,
        down_bias,
        ffn_gain,
        ffn_shift,
    ):
        i, t = lax.axis_index(DP), lax.axis_index("tensor")
        core, zbit, xbit, ybit = i & 1, t & 1, (i >> 1) & 1, (i >> 2) & 1
        moved = core != (t >> 1)
        length = segment_ids.shape[1]
        rows, model = tokens.shape
        width = query_weight.shape[1]
        part = up_weight.shape[1] // 4

        def turned(value, axis, bit):
            return jnp.where(bit == 1, jnp.flip(value, axis), value)

        def over_plane(value):
            copies = jnp.broadcast_to(value[None], (4,) + value.shape)
            return lax.all_to_all(copies, ("y", "x"), split_axis=0, concat_axis=0, tiled=True)

        def absolute(value):
            return turned(turned(value, 0, ybit), 1, xbit)

        token_own = swap(tokens)
        token_z = exchange(tokens, lambda i, t: (i, t ^ 1), lambda i, t: not moved_at(i, t))
        blank = jnp.zeros_like(query_bias)
        biases = jnp.concatenate([query_bias, blank, value_bias, blank])
        extra = jnp.concatenate(
            [jnp.broadcast_to(v[None], (16, model)) for v in (biases, up_bias)], 0
        )
        piece, quarter, local = take(
            jnp.stack([ybit * 2 + xbit, moved.astype(jnp.int32)]),
            (query_weight.T, key_weight.T, value_weight.T),
            extra,
            up_weight,
            down_weight,
            out_weight,
        )
        piece = swap(piece)
        notes = jnp.concatenate(
            [segment_ids, jnp.broadcast_to(drop_flags[:, None], (1, 128))], axis=1
        )
        notes_core = over_core(notes)
        token_own, token_z, piece, quarter, out_weight, notes, notes_core = stage(
            token_own, token_z, piece, quarter, out_weight, notes, notes_core
        )
        token_core = over_core(token_own)
        token_zm = exchange(token_own, lambda i, t: (i, t ^ 1), moved_at)
        gathered = over_plane(piece)
        quarter = swap(quarter)
        first_vectors = vectors(out_bias, attn_gain, attn_shift)
        second_vectors = vectors(down_bias, ffn_gain, ffn_shift)
        notes = jnp.where(moved, notes_core, notes)
        shard = 2 * core + zbit
        flags = jnp.stack([moved.astype(jnp.int32), 1 - notes[0, length], xbit, ybit, shard])
        segment = notes[0, :length].reshape(2, 2, length // 4)
        segment = turned(turned(segment, 0, core), 1, zbit)
        segment = jnp.swapaxes(segment, 0, 1).reshape(length)
        marks = (
            *bounds(segment, QUERIES),
            *bounds(segment, KEYS),
            jnp.broadcast_to(segment[None], (8, length)),
            jnp.broadcast_to(segment[:, None], (length, 128)),
        )
        token_zm, token_z, gathered, quarter, out_weight, *rest = stage(
            token_zm,
            token_z,
            gathered,
            quarter,
            out_weight,
            flags,
            first_vectors,
            second_vectors,
            *marks,
        )
        flags, first_vectors, second_vectors, *marks = rest
        token_z = jnp.where(moved, token_zm, token_z)
        token_zc = over_core(token_z)
        group = (token_own, token_core, token_z, token_zc)
        qkv, weights = project(group, gathered)

        qkv, quarter, out_weight = stage(qkv, quarter, out_weight)
        quarter_z = over_z(quarter)
        own_x = exchange(quarter[: 2 * part], lambda i, t: (i ^ 2, t), moved_at)
        own_y = exchange(quarter[: 2 * part], lambda i, t: (i ^ 4, t), moved_at)
        half = 2 * rows
        wide_z, context_z, totals_z = attend_forward(qkv, marks, half, half)

        qkv, context_z, quarter_z, own_x, own_y = stage(
            qkv, context_z, quarter_z, own_x, own_y
        )
        context_other = over_z(context_z)
        units_z = quarter_z[: 2 * part]
        quarter_zy, quarter_zx = over_y(units_z), over_x(units_z)
        own_xy = exchange(own_x, lambda i, t: (i ^ 4, t), moved_at)
        wide_own, context_own, totals_own = attend_forward(qkv, marks, 0, half)

        context_own, context_other, quarter_zy, quarter_zx, own_xy = stage(
            context_own, context_other, quarter_zy, quarter_zx, own_xy
        )
        up_zxy = over_y(quarter_zx[:part])
        down_zxy = over_x(quarter_zy[part : 2 * part])
        mine, theirs = out_project(context_own, context_other, quarter, quarter_z)
        theirs = over_core(theirs)
        mine, theirs, cotangent = stage(mine, theirs, cotangent)
        cotangent = swap(cotangent)
        resid, normed, normed_low = rowwise(
            first_norm_kernel,
            "first_norm",
            (F32, F32, BF16),
            (),
            mine,
            theirs,
            token_own,
            first_vectors,
        )
        normed_core = over_core(normed_low)

        normed_low, normed_core, up_zxy, down_zxy = stage(
            normed_low, normed_core, up_zxy, down_zxy
        )
        pieces = (quarter, own_x, own_y, own_xy, quarter_z, quarter_zx, quarter_zy)
        pieces = (*pieces, up_zxy, down_zxy)
        hidden, slope, mine, theirs, up_all, down_all = feed_forward(
            flags, normed_low, normed_core, (*pieces, local)
        )
        layer_out, dsummed, dffn, sums_ffn = rowwise(
            second_norm_kernel,
            "second_norm",
            (BF16, F32, BF16, None),
            (flags,),
            mine,
            over_core(theirs),
            normed,
            cotangent,
            token_own,
            second_vectors,
        )
        dffn_core = over_core(dffn)

        dffn, dffn_core, layer_out = stage(dffn, dffn_core, layer_out)
        dpre, mine, theirs, up_bias_grad = hidden_back(dffn, dffn_core, slope, up_all, down_all)
        dpre, theirs = stage(dpre, theirs)
        got = over_core(theirs)
        parts = unit_grads(dpre, normed_low, normed_core, hidden, dffn, dffn_core)
        got, *parts = stage(got, *parts)
        plane_got = over_x(parts[1]), over_y(parts[3])
        dresid, dresid_low, small = small_kernel(
            first_norm_back_kernel,
            "first_norm_back",
            (((rows, model), F32), ((rows + 16, model), BF16), ((16, model), F32)),
            (flags,),
            mine,
            got,
            dsummed,
            resid,
            first_vectors,
            sums_ffn,
            up_bias_grad,
        )
        dresid_core = over_core(dresid_low)
        dcontext_own, dcontext_z, out_grad_z, small = small_kernel(
            context_back_kernel,
            "context_back",
            (
                ((width, half), BF16),
                ((width, half), BF16),
                ((width + 16, model), BF16),
                ((16, model), F32),
            ),
            (),
            dresid_low,
            dresid_core,
            small,
            quarter,
            quarter_z,
            context_other,
        )
        dcontext_z, dcontext_own, out_grad_z, layer_out = stage(
            dcontext_z, dcontext_own, out_grad_z, layer_out
        )
        dcontext_other = over_z(dcontext_z)
        layer_out = swap(layer_out)
        around = (dcontext_own, wide_own, totals_own)
        dq_own, sums = attend_backward(qkv, around, marks, 0, 0, rows, None, F32)

        dq_core, sums = attend_backward(qkv, around, marks, rows, rows, rows, sums, F32)
        dq_core, sums, dcontext_other, out_grad_z = stage(
            dq_core, sums, dcontext_other, out_grad_z
        )
        out_grad_other = over_z(out_grad_z)
        around = (dcontext_other, wide_z, totals_z)
        dq_z, sums = attend_backward(qkv, around, marks, half, 0, rows, sums, F32)

        dq_z, sums, layer_out, *plane_got = stage(dq_z, sums, layer_out, *plane_got)
        kept_own, send_own, kept_other, send_other = small_kernel(
            fold_plane_kernel,
            "fold_plane",
            (((2 * part, model), F32), ((2 * part, model), BF16)) * 2,
            (),
            parts[0],
            plane_got[0],
            parts[2],
            plane_got[1],
        )
        send_own, send_other = over_y(send_own), over_x(send_other)
        dq_zc, sums = attend_backward(qkv, around, marks, 3 * rows, rows, rows, sums, BF16)

        def home(value):
            kept, send, far = value
            send = exchange(send, lambda i, t: (i, t ^ 2) if moved_at(i, t) else (i ^ 1, t))
            far = exchange(far, lambda i, t: (i ^ 1, t ^ 2), moved_at)
            return kept, send, far

        def outer(value):
            bit = 8
            while bit < ndp:
                value = value + exchange(
                    value.astype(BF16), lambda i, t, bit=bit: (i ^ bit, t)
                ).astype(F32)
                bit *= 2
            return value

        def fold_home(name, value, kind=BF16):
            result = small_kernel(
                fold_home_kernel,
                name,
                ((value[0].shape, kind if ndp == 8 else F32),),
                (flags,),
                *value,
            )[0]
            return outer(result).astype(kind)

        dq_zc, sums, out_grad_other = stage(dq_zc, sums, out_grad_other)
        input_z, input_zc = input_back(half, dq_z, dq_zc, sums, weights)
        input_z, input_zc, sums, send_own, send_other = stage(
            input_z, input_zc, sums, send_own, send_other
        )
        unit_sum, unit_z = small_kernel(
            fold_shards_kernel,
            "fold_shards",
            (((2 * part, model), F32), ((2 * part, model), BF16)),
            (),
            kept_own,
            send_own,
            kept_other,
            send_other,
        )
        unit_z, input_zc, sums = stage(unit_z, input_zc, sums)
        unit_z = over_z(unit_z)
        input_zc = over_core(input_zc)
        mine, theirs = small_kernel(
            input_own_kernel,
            "input_own",
            (((rows, model), F32), ((rows, model), BF16)),
            (flags,),
            dq_own,
            dq_core,
            sums,
            weights,
            dresid,
            cotangent,
        )
        packed = weight_grads(
            group,
            (dq_own, dq_core, dq_z, dq_zc),
            sums,
            context_own,
            dresid_low,
            dresid_core,
            out_grad_other,
            small,
        )
        packed, input_z, input_zc, mine, theirs = stage(packed, input_z, input_zc, mine, theirs)
        input_z = small_kernel(
            fold_inputs_kernel, "fold_inputs", (((rows, model), BF16),), (), input_z, input_zc
        )[0]
        input_z, packed, theirs, unit_z = stage(input_z, packed, theirs, unit_z)
        input_other = over_z(input_z)
        parted = lax.all_to_all(packed, ("y", "x"), split_axis=0, concat_axis=0, tiled=True)
        theirs = over_core(theirs)
        unit_home = small_kernel(
            fold_z_kernel,
            "fold_z",
            (((part, model), F32), ((part, model), BF16), ((part, model), BF16)),
            (flags,),
            unit_sum,
            unit_z,
        )
        mine, theirs, *unit_home = stage(mine, theirs, *unit_home)
        unit_home = home(unit_home)

        parted, input_other, mine, theirs, *unit_home = stage(
            parted, input_other, mine, theirs, *unit_home
        )
        head_home = small_kernel(
            fold_parts_kernel,
            "fold_parts",
            (
                ((width // 2 + 16, model), F32),
                ((width // 2 + 16, model), BF16),
                ((width // 2 + 16, model), BF16),
            ),
            (flags,),
            parted,
        )
        mine, theirs, kept, send, far, *head_home = stage(mine, theirs, *unit_home, *head_home)
        head_home = home(head_home)
        unit_all = over_plane(fold_home("fold_units", (kept, send, far)))
        mine, theirs, input_other = stage(mine, theirs, input_other)
        tokens_grad = small_kernel(
            add_tokens_kernel,
            "add_tokens",
            (((rows, model), BF16),),
            (),
            mine,
            theirs,
            input_other,
        )[0]
        tokens_grad, *head_home = stage(tokens_grad, *head_home)
        tokens_grad = swap(tokens_grad)
        heads = fold_home("fold_heads", head_home, F32)
        heads, unit_all = stage(heads, unit_all)
        head_all = over_plane(heads[: width // 2].astype(BF16))
        small = heads[width // 2 :]
        up_bias_sum = lax.dynamic_slice_in_dim(small[6:10], t, 1, 0)[0]
        unit_other = over_core(unit_all)
        up_sum, down_sum = small_kernel(
            unit_results_kernel,
            "unit_results",
            (((model, 4 * part), F32), ((4 * part, model), F32)),
            (flags,),
            unit_all,
            unit_other,
        )
        head_all, up_sum, down_sum, tokens_grad, small, up_bias_sum = stage(
            head_all, up_sum, down_sum, tokens_grad, small, up_bias_sum
        )
        head_other = over_core(head_all)
        sums = small_kernel(
            head_results_kernel,
            "head_results",
            (((width, model), F32),) * 4 + (((rows, model), BF16),) * 2,
            (flags,),
            head_all,
            head_other,
            layer_out,
            tokens_grad,
        )
        layer_out, tokens_grad = sums[4:]
        narrow = small[12, :width], small[12, width : 2 * width]

        return (
            layer_out,
            tokens_grad,
            sums[0].T,
            narrow[0],
            sums[1].T,
            sums[2].T,
            narrow[1],
            sums[3],
            small[0],
            small[1],
            small[2],
            up_sum,
            up_bias_sum,
            down_sum,
            small[3],
            small[4],
            small[5],
        )

    return jax.shard_map(
        shards,
        mesh=fine,
        in_specs=(
            P(AXES, None),
            P(AXES, None),
            P(DP, None),
            P(DP),
            P(None, "tensor"),
            P("tensor"),
            P(None, "tensor"),
            P(None, "tensor"),
            P("tensor"),
            P("tensor", None),
            P(),
            P(),
            P(),
            P(None, "tensor"),
            P("tensor"),
            P("tensor", None),
            P(),
            P(),
            P(),
        ),
        out_specs=(
            P(AXES, None),
            P(AXES, None),
            P(None, "tensor"),
            P("tensor"),
            P(None, "tensor"),
            P(None, "tensor"),
            P("tensor"),
            P("tensor", None),
            P(),
            P(),
            P(),
            P(None, "tensor"),
            P("tensor"),
            P("tensor", None),
            P(),
            P(),
            P(),
        ),
        check_vma=False,
    )
```
